128 devices in a mesh: gx: 8 (over y, core), gy: 16 (over z, x).
Axes of the slice: x: 4, y: 4, z: 4, core: 2. Of those that a mesh axis runs over, the one named last changes fastest.
Arguments:
- slope_depth: float32 [2048, 8192], P('gx', 'gy'), may hold values from 0.2 to 2
- slope_momentum: float32 [2, 2048, 8192], P(None, 'gx', 'gy'), may hold values from -1.2 to 1.2
- bed_slope: float32 [2, 2048, 8192], P(None, 'gx', 'gy'), may hold values from -3 to 3
- friction: float32 [2048, 8192], P('gx', 'gy'), may hold values from 0.2 to 2
- slope_active: int32 [2048, 8192], P('gx', 'gy'), may hold values 0 or 1
- owners: int32 [8, 16, 256, 1], P('gx', 'gy'), may hold values from 0 to 127; in each aligned block of 256 rows (0 to 255, 256 to 511, ..., all dimensions but the last counted through in order) at most 4 rows name the same one
- offsets: int32 [8, 16, 256], P('gx', 'gy'), may hold values from 0 to 511
- lake_height: float32 [4096, 8192], P('gx', 'gy'), may hold values from -6 to 6
- lake_momentum: float32 [2, 4096, 8192], P(None, 'gx', 'gy'), may hold values from -16 to 16
- lake_diagonal: float32 [4096, 8192], P('gx', 'gy'), may hold values from 0.2 to 2
Outputs:
- slope_fields: float32 [3, 2048, 8192], P(None, 'gx', 'gy')
- new_height: float32 [4096, 8192], P('gx', 'gy')
- new_momentum: float32 [2, 4096, 8192], P(None, 'gx', 'gy')
The draws below stay inside these ranges and needn't reach their ends.
Inputs may be any that keep to these rules, and one draw needn't show every extreme that they name: `owners`: among the 256 rows of one device, no owner is named by more than 4 rows, a bound that some block reaches.
All inputs are finite; a program needn't handle non-finite values. No bound on the sum of `slope_active` on one device may be relied on, other than what follows from the above.
Results may differ from the reference program's by a relative error of at most 0.0001.
Values sent between devices are 32-bit elements; how exact they have to be, the bound alone decides.
No kernel may reach another device: no remote copies, remote signals or barrier semaphores. Data moves between devices by JAX's collectives and lax.ppermute only.
A program may use at most 128 MiB of HBM per device.

```python
import math
import jax
import jax.numpy as jnp
import numpy as np

CX = 256
CY = 512
LX = 512
SECTIONS = 2
ITERS = 3
CAP = 4
SLOPE_ROWS = 2048
LAKE_ROWS = 4096
GRID_COLS = 8192
N_GX = 8
N_GY = 16
DEVICES = 128


def draw_lake_momentum(key, part):
    first_key = jax.random.fold_in(key, 0)
    row_frac = jnp.arange(LAKE_ROWS, dtype=jnp.float32) / LAKE_ROWS
    row_scale = 0.6 + 0.6 * row_frac
    normal_part = jnp.clip(jax.random.normal(first_key, (2, LAKE_ROWS, GRID_COLS), jnp.float32), -4.0, 4.0)
    return normal_part * row_scale[None, :, None]


def set_ends(result, key, smallest, top_value):
    dims = result.shape
    place = [jax.random.randint(jax.random.fold_in(key, axis), (), 0, dims[axis]) for axis in range(len(dims))]
    result = result.at[tuple(place)].set(smallest)
    longest = dims.index(max(dims))
    place[longest] = (place[longest] + 1) % dims[longest]
    return result.at[tuple(place)].set(top_value)


def shard_levels(key, shape, shards, low, high):
    loudness, own = 1.0, jax.random.fold_in(key, 6)
    for dim, parts in shards:
        heights = jnp.exp(jax.random.uniform(jax.random.fold_in(own, dim), (parts,), jnp.float32, low / len(shards), high / len(shards)))
        loudness = loudness * jnp.repeat(heights, shape[dim] // parts).reshape([-1 if axis == dim else 1 for axis in range(len(shape))])
    return loudness


def shared_out(own_key, own, number, rows, amount, top, most, lean):
    ranking = jax.random.permutation(own_key, amount)
    heavy_load, ordinary = portions_of(amount, rows * top, most, lean, True), portions_of(amount, rows * top, most, lean, False)
    places = jnp.arange(amount)

    def named(lengths, rotation):
        used = int((lengths > 0).sum())
        fixed = max(1, used // 4)
        shifted = fixed + (places - fixed + rotation * (used - fixed)) % max(1, amount - fixed)
        return jnp.zeros((amount,), jnp.int32).at[ranking[jnp.where(places < fixed, places, shifted)]].set(jnp.asarray(lengths, jnp.int32))

    lengths = jnp.where(number % 4 == 0, named(heavy_load, number // 4), named(ordinary, number - number // 4 - 1))
    mixed = jax.random.permutation(jax.random.fold_in(own, 3), amount)
    donor, taker = mixed[0:amount // 2 * 2:2], mixed[1:amount // 2 * 2:2]
    margin = jnp.minimum(lengths[donor] - 1, most - lengths[taker]) // 2
    margin = jnp.where((donor == ranking[0]) | (taker == ranking[0]) | (lengths[taker] == 0), 0, jnp.maximum(margin, 0))
    shifted = jax.random.randint(jax.random.fold_in(own, 4), (amount // 2,), 0, 1 << 20) % (margin + 1)
    lengths = lengths.at[donor].add(-shifted).at[taker].add(shifted)
    members = jnp.searchsorted(jnp.cumsum(lengths), jnp.arange(rows * top), side="right").astype(jnp.int32)
    listing = members.reshape(top, rows).T
    listing = listing[jax.random.permutation(jax.random.fold_in(own, 1), rows)]
    rotation = jax.random.randint(jax.random.fold_in(own, 2), (rows, 1), 0, top)
    return jnp.take_along_axis(listing, (jnp.arange(top)[None, :] + rotation) % top, axis=1)


def portions_of(count, total, bound, slope, full):
    portions = [(1 << 20) // math.isqrt(grade ** slope) + 1 for grade in range(1, count + 1)]
    largest = bound if full else min(bound, max(-(-total // count), total * portions[0] // sum(portions)))
    least = 1 if total - largest >= count - 1 else 0
    given, rest = [largest] + [least] * (count - 1), total - largest - least * (count - 1)
    while rest > 0:
        free = [i for i in range(1, count) if given[i] < largest] or [i for i in range(1, count) if given[i] < bound]
        pool, remaining = sum([portions[i] for i in free]), rest
        for i in free:
            more = min(bound - given[i], max(1, remaining * portions[i] // pool), rest)
            given[i] = given[i] + more
            rest = rest - more
    return np.array(given)


def gaussian(rng, extent, scale, bound, pieces=(), held_as=jnp.bfloat16):
    entries = jax.random.normal(rng, extent, jnp.float32) * scale
    if len(pieces) > 0:
        entries = shard_levels(rng, extent, pieces, -0.22, 0.18) * entries
    return jnp.clip(entries, min=-bound, max=bound).astype(held_as)


def setup_inputs(seed: int = 0) -> dict:
    arg_keys = jax.random.split(jax.random.key(seed), 11)
    slope_depth = jnp.clip(jnp.exp(math.log(2.0) - 2.3025851 * jax.random.uniform(arg_keys[0], (SLOPE_ROWS, GRID_COLS), jnp.float32) ** shard_levels(arg_keys[0], (SLOPE_ROWS, GRID_COLS), ((0, 8), (1, 16)), -0.2, 0.2)), 0.2, 2.0)
    slope_momentum = gaussian(arg_keys[1], (2, SLOPE_ROWS, GRID_COLS), 0.3, 1.2, ((1, 8), (2, 16)), jnp.float32)
    bed_slope = gaussian(arg_keys[2], (2, SLOPE_ROWS, GRID_COLS), 0.5, 3.0, ((1, 8), (2, 16)), jnp.float32)
    friction = jnp.clip(jnp.exp(math.log(2.0) - 2.3025851 * jax.random.uniform(arg_keys[3], (SLOPE_ROWS, GRID_COLS), jnp.float32) ** shard_levels(arg_keys[3], (SLOPE_ROWS, GRID_COLS), ((0, 8), (1, 16)), -0.2, 0.2)), 0.2, 2.0)
    slope_active = set_ends((jax.random.randint(arg_keys[4], (SLOPE_ROWS, GRID_COLS), 0, 4) < 3).astype(jnp.int32), jax.random.fold_in(arg_keys[4], 1), 0, 1)
    owners_keys = jax.random.split(jax.random.fold_in(arg_keys[5], 1), N_GX * N_GY * CX // CX)
    owners_turns = jax.random.permutation(jax.random.fold_in(arg_keys[5], 3), N_GX * N_GY * CX // CX)
    owners = jax.vmap(lambda own, number: shared_out(jax.random.fold_in(arg_keys[5], 2), own, number, CX, DEVICES, 1, CAP, 2))(owners_keys, owners_turns).reshape((N_GX, N_GY, CX, 1))
    offsets = set_ends(jax.random.randint(arg_keys[6], (N_GX, N_GY, CX), 0, LX), jax.random.fold_in(arg_keys[6], 1), 0, LX - 1).astype(jnp.int32)
    lake_height = gaussian(arg_keys[7], (LAKE_ROWS, GRID_COLS), 1.0, 6.0, ((0, 8), (1, 16)), jnp.float32)
    lake_momentum = draw_lake_momentum(jax.random.fold_in(arg_keys[10], 71), 0)
    lake_diagonal = jnp.clip(0.2 + 1.8 * jax.random.uniform(arg_keys[9], (LAKE_ROWS, GRID_COLS), jnp.float32) ** shard_levels(arg_keys[9], (LAKE_ROWS, GRID_COLS), ((0, 8), (1, 16)), -0.2, 0.2), 0.2, 2.0)
    return {"slope_depth": slope_depth, "slope_momentum": slope_momentum, "bed_slope": bed_slope, "friction": friction, "slope_active": slope_active, "owners": owners, "offsets": offsets, "lake_height": lake_height, "lake_momentum": lake_momentum, "lake_diagonal": lake_diagonal}


courant = 0.15
depth_floor = 0.25
dispersion = 0.5


def advance(fields, padded, bed_slope, friction, active):
    height = padded[0]
    floored = jnp.maximum(height, depth_floor)
    along_speed = padded[1] / floored
    across_speed = padded[2] / floored
    pressure = 0.5 * height * height
    flux_along = jnp.stack([padded[1], padded[1] * along_speed + pressure, padded[2] * along_speed])
    flux_across = jnp.stack([padded[2], padded[1] * across_speed, padded[2] * across_speed + pressure])
    average = 0.25 * (padded[:, 2:, 1:-1] + padded[:, :-2, 1:-1] + padded[:, 1:-1, 2:] + padded[:, 1:-1, :-2])
    update = average - 0.5 * courant * (flux_along[:, 2:, 1:-1] - flux_along[:, :-2, 1:-1])
    update = update - 0.5 * courant * (flux_across[:, 1:-1, 2:] - flux_across[:, 1:-1, :-2])
    forcing = jnp.stack([jnp.zeros_like(fields[0]), fields[0] * bed_slope[0] - friction * fields[1], fields[0] * bed_slope[1] - friction * fields[2]])
    return (update + courant * forcing) * active[None]


def operate(vectors, lake_diagonal):
    padded = jnp.pad(vectors, ((0, 0), (1, 1), (1, 1)))
    beside = padded[:, 2:, 1:-1] + padded[:, :-2, 1:-1] + padded[:, 1:-1, 2:] + padded[:, 1:-1, :-2]
    return (1.0 + 4.0 * dispersion + lake_diagonal)[None] * vectors - dispersion * beside


def reference(slope_depth, slope_momentum, bed_slope, friction, slope_active, owners, offsets, lake_height, lake_momentum, lake_diagonal):
    active = slope_active.astype(jnp.float32)
    fields = jnp.concatenate([slope_depth[None], slope_momentum], axis=0)
    for section_index in range(SECTIONS):
        padded = jnp.pad(fields, ((0, 0), (1, 1), (1, 1)))
        fields = advance(fields, padded, bed_slope, friction, active)
    blocks = fields.reshape(3, N_GX, CX, N_GY, CY).transpose(1, 3, 2, 0, 4).reshape(N_GX * N_GY * CX, 3, CY)
    owner_flat = owners.reshape(-1).astype(jnp.int32)
    offset_flat = offsets.reshape(-1).astype(jnp.int32)
    target = ((owner_flat // N_GY) * LX + offset_flat) * N_GY + owner_flat % N_GY
    inflow = jax.ops.segment_sum(blocks, target, num_segments=LAKE_ROWS * N_GY)
    inflow = inflow.reshape(LAKE_ROWS, N_GY, 3, CY).transpose(2, 0, 1, 3).reshape(3, LAKE_ROWS, GRID_COLS)
    new_height = lake_height + inflow[0]
    right_side = lake_momentum + inflow[1:]
    solution = jnp.zeros_like(right_side)
    residual = right_side
    direction = right_side
    norm_now = jnp.sum(residual * residual, axis=(1, 2))
    for iteration in range(ITERS):
        applied = operate(direction, lake_diagonal)
        step_length = norm_now / jnp.sum(direction * applied, axis=(1, 2))
        solution = solution + step_length[:, None, None] * direction
        residual = residual - step_length[:, None, None] * applied
        norm_next = jnp.sum(residual * residual, axis=(1, 2))
        direction = residual + (norm_next / norm_now)[:, None, None] * direction
        norm_now = norm_next
    return fields, new_height, solution
```

```python
import functools

import jax
import jax.numpy as jnp
from jax import lax
from jax.experimental import pallas as pl
from jax.experimental.pallas import tpu as pltpu
from jax.sharding import PartitionSpec as P

F32 = jnp.float32
BF16 = jnp.bfloat16
AXES = ("gx", "gy")
NX, NY = 8, 16
DEV = NX * NY
R, C, L = 256, 512, 512
CAP = 4
UNITS = 12 * CAP + 1
TAG = 12 * CAP
WIDE = C + 128
TOP = 16
SROWS = R + 3 * TOP
LROWS = L + 2 * TOP
MIB = 1 << 20


def params(limit):
    return pltpu.CompilerParams(vmem_limit_bytes=limit * MIB)


def lanes(shape):
    return lax.broadcasted_iota(jnp.int32, shape, len(shape) - 1)


def rows(shape):
    return lax.broadcasted_iota(jnp.int32, shape, len(shape) - 2)


def next_row(x, i, r, n, width):
    block = x[i, pl.ds(r, n + 8), 0:width]
    return pltpu.roll(block, n + 7, 0)[0:n, :]


def previous_row(x, i, r, n, width):
    block = x[i, pl.ds(pl.multiple_of(r - 8, 8), n + 8), 0:width]
    return pltpu.roll(block, 1, 0)[8 : n + 8, :]


def edge_rows_kernel(ht, hb, mt, mb, bt, bb, ft, fb, at, ab, dt, db, up, dn):
    for out, h, m, b, f, a, d, two, one in (
        (up, ht, mt, bt, ft, at, dt, slice(0, 2), slice(0, 1)),
        (dn, hb, mb, bb, fb, ab, db, slice(6, 8), slice(7, 8)),
    ):
        out[0:2, :] = h[two, :]
        out[2:4, :] = m[0, two, :]
        out[4:6, :] = m[1, two, :]
        out[6:7, :] = b[0, one, :]
        out[7:8, :] = b[1, one, :]
        out[8:9, :] = f[one, :]
        out[9:10, :] = a[one, :].astype(F32)
        out[10:12, :] = d[two, :]
        out[12:16, :] = jnp.zeros((4, C), F32)


def edge_rows(h, mom, bed, fric, act, d):
    last, lake_last = R // 8 - 1, L // 8 - 1
    two = lambda r: pl.BlockSpec((8, C), lambda i: (r, 0))
    three = lambda r: pl.BlockSpec((2, 8, C), lambda i: (0, r, 0))
    return pl.pallas_call(
        edge_rows_kernel,
        grid=(1,),
        in_specs=[two(0), two(last), three(0), three(last), three(0), three(last), two(0), two(last), two(0), two(last), two(0), two(lake_last)],
        out_specs=[pl.BlockSpec((16, C), lambda i: (0, 0))] * 2,
        out_shape=[jax.ShapeDtypeStruct((16, C), F32)] * 2,
        compiler_params=params(8),
        name="edge_rows",
    )(h, h, mom, mom, bed, bed, fric, fric, act, act, d, d)


def edge_columns_kernel(hl, hr, ml, mr, bl, br, fl, fr, al, ar, dl, dr, ll, lr, above, below, right, left, mat):
    slope = (
        (lambda s: hl[s, :], lambda s: hr[s, :]),
        (lambda s: ml[0, s, :], lambda s: mr[0, s, :]),
        (lambda s: ml[1, s, :], lambda s: mr[1, s, :]),
        (lambda s: bl[0, s, :], lambda s: br[0, s, :]),
        (lambda s: bl[1, s, :], lambda s: br[1, s, :]),
        (lambda s: fl[s, :], lambda s: fr[s, :]),
        (lambda s: al[s, :].astype(F32), lambda s: ar[s, :].astype(F32)),
    )
    lake = (
        (lambda s: dl[s, :], lambda s: dr[s, :]),
        (lambda s: ll[0, s, :], lambda s: lr[0, s, :]),
        (lambda s: ll[1, s, :], lambda s: lr[1, s, :]),
    )
    step = 64

    def put(acc, lane, first, last, i, wide):
        base, base_left = (2 * i, 64 + 2 * i) if wide == 2 else (16 + 3 * i, 80 + 3 * i)
        turned = pltpu.roll(last, (base + wide) % 128, 1)
        acc = jnp.where((lane >= base) & (lane < base + wide), turned, acc)
        turned = pltpu.roll(first, base_left, 1)
        return jnp.where((lane >= base_left) & (lane < base_left + wide), turned, acc)

    def both(t, _):
        s = pl.ds(pl.multiple_of(t * step, step), step)
        lane = lanes((step, 128))
        acc = jnp.zeros((step, 128), F32)
        for i, (first, last) in enumerate(slope):
            acc = put(acc, lane, first(s), last(s), i, 2)
        for i, (first, last) in enumerate(lake):
            acc = put(acc, lane, first(s), last(s), i, 3)
        mat[s, :] = acc
        return 0

    def lake_only(t, _):
        s = pl.ds(pl.multiple_of(t * step, step), step)
        lane = lanes((step, 128))
        acc = jnp.zeros((step, 128), F32)
        for i, (first, last) in enumerate(lake):
            acc = put(acc, lane, first(s), last(s), i, 3)
        mat[s, :] = acc
        return 0

    lax.fori_loop(0, R // step, both, 0)
    lax.fori_loop(R // step, L // step, lake_only, 0)
    lane, row = lanes((8, 128)), rows((8, 128))

    def corner(b_row, a_row, where):
        low = jnp.broadcast_to(below[b_row : b_row + 1, where], (8, 128))
        high = jnp.broadcast_to(above[a_row : a_row + 1, where], (8, 128))
        return jnp.where(row == 0, low, jnp.where(row == 7, high, 0.0))

    acc = mat[R : R + 8, :]
    for i in range(3):
        acc = put(acc, lane, corner(2 * i, 2 * i + 1, slice(0, 128)), corner(2 * i, 2 * i + 1, slice(C - 128, C)), i, 2)
    mat[R : R + 8, :] = acc
    acc = put(jnp.zeros((8, 128), F32), lane, corner(10, 11, slice(0, 128)), corner(10, 11, slice(C - 128, C)), 0, 3)
    mat[L : L + 8, :] = acc
    mat[L + 8 : L + 128, :] = jnp.zeros((120, 128), F32)
    for t in range(5):
        turned = mat[128 * t : 128 * t + 128, :].T
        right[:, 128 * t : 128 * t + 128] = turned[0:32, :]
        left[:, 128 * t : 128 * t + 128] = turned[64:96, :]


def edge_columns(h, mom, bed, fric, act, d, lm, above, below):
    last = C // 128 - 1
    two = lambda n, c: pl.BlockSpec((n, 128), lambda i: (0, c))
    three = lambda n, c: pl.BlockSpec((2, n, 128), lambda i: (0, 0, c))
    whole = pl.BlockSpec((16, C), lambda i: (0, 0))
    specs, args = [], []
    for spec, n, x in ((two, R, h), (three, R, mom), (three, R, bed), (two, R, fric), (two, R, act), (two, L, d), (three, L, lm)):
        specs += [spec(n, 0), spec(n, last)]
        args += [x, x]
    return pl.pallas_call(
        edge_columns_kernel,
        grid=(1,),
        in_specs=specs + [whole, whole],
        out_specs=[pl.BlockSpec((32, WIDE), lambda i: (0, 0))] * 2,
        out_shape=[jax.ShapeDtypeStruct((32, WIDE), F32)] * 2,
        scratch_shapes=[pltpu.VMEM((WIDE, 128), F32)],
        compiler_params=params(16),
        name="edge_columns",
    )(*args, above, below)


def split3(x):
    hi = x.astype(BF16)
    rest = x - hi.astype(F32)
    mid = rest.astype(BF16)
    return hi, mid, (rest - mid.astype(F32)).astype(BF16)


def slope_kernel(
    h_hbm, mom_hbm, bed_hbm, fric_hbm, act_hbm, above, below, from_left, from_right, own, off,
    out, payload,
    ext, act_ext, nxt, pa, qa, acc, turn, sems,
):
    srcs = (h_hbm, mom_hbm.at[0], mom_hbm.at[1], bed_hbm.at[0], bed_hbm.at[1], fric_hbm)
    tile = (pl.ds(TOP, R), pl.ds(0, C))
    copies = [pltpu.make_async_copy(s, ext.at[(i,) + tile], sems.at[i]) for i, s in enumerate(srcs)]
    copies.append(pltpu.make_async_copy(act_hbm, act_ext.at[tile], sems.at[6]))
    for c in copies:
        c.start()

    def arr(i):
        return ext.at[i] if i < 6 else act_ext

    for i in range(7):
        x = arr(i)
        x[0:TOP, :] = jnp.zeros((TOP, WIDE), x.dtype)
        x[TOP + R :, :] = jnp.zeros((2 * TOP, WIDE), x.dtype)
        if i < 3:
            x[TOP - 2 : TOP, 0:C] = above[2 * i : 2 * i + 2, :]
            x[TOP + R : TOP + R + 2, 0:C] = below[2 * i : 2 * i + 2, :]
        else:
            x[TOP - 1 : TOP, 0:C] = above[3 + i : 4 + i, :].astype(x.dtype)
            x[TOP + R : TOP + R + 1, 0:C] = below[3 + i : 4 + i, :].astype(x.dtype)
    for t in range(3):
        s = slice(128 * t, 128 * t + 128)
        both = jnp.concatenate(
            [from_left[:, s], jnp.zeros((32, 128), F32), from_right[:, s], jnp.zeros((32, 128), F32)], axis=0
        )
        turn[s, :] = both.T

    def halo(w, lane, i):
        left = pltpu.roll(w, 126 - 2 * i, 1)
        right = pltpu.roll(w, 64 - 2 * i, 1)
        return jnp.where(lane >= 126, left, jnp.where(lane < 2, right, 0.0))

    step = 64

    def columns(t, _):
        r = pl.multiple_of(t * step, step)
        w = turn[pl.ds(r, step), :]
        lane = lanes((step, 128))
        for i in range(7):
            x = arr(i)
            x[pl.ds(pl.multiple_of(TOP + r, 8), step), C:WIDE] = halo(w, lane, i).astype(x.dtype)
        return 0

    lax.fori_loop(0, R // step, columns, 0)
    w = turn[R : R + 8, :]
    row = rows((8, 128))
    for i in range(3):
        block = halo(w, lanes((8, 128)), i)
        ext[i, TOP - 8 : TOP, C:WIDE] = jnp.where(row == 7, block, 0.0)
        ext[i, TOP + R : TOP + R + 8, C:WIDE] = jnp.where(row == 0, block, 0.0)
    for c in copies:
        c.wait()

    k = 0.075
    chunk = 16

    def fluxes(src, begin, count):
        def body(t, _):
            s = pl.ds(pl.multiple_of(begin + t * chunk, 8), chunk)
            h, m, n = (src[i, s, :] for i in range(3))
            inv = 1.0 / jnp.maximum(h, 0.25)
            p = (0.5 * h) * h
            mi = m * inv
            cross = k * (mi * n)
            fm = k * (mi * m + p)
            gn = k * ((n * inv) * n + p)
            h4, m4, n4, mk, nk = 0.25 * h, 0.25 * m, 0.25 * n, k * m, k * n
            pa[0, s, :] = h4 - mk
            qa[0, s, :] = h4 + mk
            pa[1, s, :] = m4 - fm
            qa[1, s, :] = m4 + fm
            pa[2, s, :] = n4 - cross
            qa[2, s, :] = n4 + cross
            fr = ext[5, s, :]
            acc[0, s, :] = pltpu.roll(h4 - nk, WIDE - 1, 1) + pltpu.roll(h4 + nk, 1, 1)
            acc[1, s, :] = (
                pltpu.roll(m4 - cross, WIDE - 1, 1) + pltpu.roll(m4 + cross, 1, 1) + 0.15 * (h * ext[3, s, :] - fr * m)
            )
            acc[2, s, :] = (
                pltpu.roll(n4 - gn, WIDE - 1, 1) + pltpu.roll(n4 + gn, 1, 1) + 0.15 * (h * ext[4, s, :] - fr * n)
            )
            return 0

        lax.fori_loop(0, count, body, 0)

    def combine(begin, count, store, width):
        def body(t, _):
            r = pl.multiple_of(begin + t * chunk, 8)
            s = pl.ds(r, chunk)
            on = act_ext[s, 0:width].astype(F32)
            for i in range(3):
                store(
                    i,
                    t,
                    s,
                    on * (acc[i, s, 0:width] + next_row(pa, i, r, chunk, width) + previous_row(qa, i, r, chunk, width)),
                )
            return 0

        lax.fori_loop(0, count, body, 0)

    def to_next(i, t, s, value):
        nxt[i, s, :] = value

    def to_out(i, t, s, value):
        out[i, pl.ds(pl.multiple_of(t * chunk, 8), chunk), :] = value

    fluxes(ext, 0, SROWS // chunk)
    combine(8, (R + 16) // chunk, to_next, WIDE)
    fluxes(nxt, 8, (R + 16) // chunk)
    combine(TOP, R // chunk, to_out, C)

    owner = jnp.broadcast_to(own[...], (DEV, R))
    mine = rows((DEV, R)) == owner
    before = (rows((R, R)) < lanes((R, R))).astype(BF16)
    rank = jnp.dot(mine.astype(BF16), before, preferred_element_type=F32)
    picks = [mine & (rank == float(k_)) for k_ in range(CAP)]
    pickb = [p.astype(BF16) for p in picks]
    for i in range(3):
        parts = split3(out[i])
        for k_ in range(CAP):
            y = (
                jnp.dot(pickb[k_], parts[0], preferred_element_type=F32)
                + jnp.dot(pickb[k_], parts[1], preferred_element_type=F32)
                + jnp.dot(pickb[k_], parts[2], preferred_element_type=F32)
            )
            for j in range(4):
                payload[pl.ds(12 * k_ + 4 * i + j, DEV, stride=UNITS), :] = y[:, 128 * j : 128 * j + 128]

    lane, dest = lanes((DEV, 128)), rows((DEV, 128))
    tags = jnp.zeros((DEV, 128), F32)
    tag_value = jnp.broadcast_to((off[...] + 1).astype(F32), (DEV, R))
    edge_lane = lanes((R, 128))
    m_first, n_first = out[1, :, 0:128], out[2, :, 0:128]
    m_last, n_last = out[1, :, C - 128 : C], out[2, :, C - 128 : C]
    edges = jnp.where(edge_lane < 3, m_first, 0.0)
    edges = jnp.where((edge_lane >= 3) & (edge_lane < 6), pltpu.roll(n_first, 3, 1), edges)
    edges = jnp.where((edge_lane >= 8) & (edge_lane < 11), pltpu.roll(m_last, 11, 1), edges)
    edges = jnp.where((edge_lane >= 11) & (edge_lane < 14), pltpu.roll(n_last, 14, 1), edges)
    parts = split3(edges)
    to_right = jnp.zeros((DEV, 128), F32)
    to_left = jnp.zeros((DEV, 128), F32)
    for k_ in range(CAP):
        tag = jnp.sum(jnp.where(picks[k_], tag_value, 0.0), axis=1, keepdims=True)
        tags = jnp.where(lane == k_, tag, tags)
        g = (
            jnp.dot(pickb[k_], parts[0], preferred_element_type=F32)
            + jnp.dot(pickb[k_], parts[1], preferred_element_type=F32)
            + jnp.dot(pickb[k_], parts[2], preferred_element_type=F32)
        )
        at = 8 + 6 * k_
        to_right = jnp.where((lane >= at) & (lane < at + 6), pltpu.roll(g, at - 8, 1) if k_ else g, to_right)
        to_right = jnp.where(lane == 56 + k_, tag, to_right)
        at = 32 + 6 * k_
        to_left = jnp.where((lane >= at) & (lane < at + 6), pltpu.roll(g, at, 1), to_left)
        to_left = jnp.where(lane == 60 + k_, tag, to_left)
    column = lax.rem(dest, NY)
    to_right = jnp.where(column > 0, pltpu.roll(to_right, 1, 0), 0.0)
    to_left = jnp.where(column < NY - 1, pltpu.roll(to_left, DEV - 1, 0), 0.0)
    payload[pl.ds(TAG, DEV, stride=UNITS), :] = tags + to_right + to_left


def slope(h, mom, bed, fric, act, above, below, from_left, from_right, own, off):
    hbm = pl.BlockSpec(memory_space=pl.ANY)
    vmem = pl.BlockSpec(memory_space=pltpu.VMEM)
    return pl.pallas_call(
        slope_kernel,
        in_specs=[hbm] * 5 + [vmem] * 6,
        out_specs=[vmem, vmem],
        out_shape=[jax.ShapeDtypeStruct((3, R, C), F32), jax.ShapeDtypeStruct((DEV * UNITS, 128), F32)],
        scratch_shapes=[
            pltpu.VMEM((6, SROWS, WIDE), F32),
            pltpu.VMEM((SROWS, WIDE), jnp.int32),
            pltpu.VMEM((3, SROWS, WIDE), F32),
            pltpu.VMEM((3, SROWS, WIDE), F32),
            pltpu.VMEM((3, SROWS, WIDE), F32),
            pltpu.VMEM((3, SROWS, WIDE), F32),
            pltpu.VMEM((384, 128), F32),
            pltpu.SemaphoreType.DMA((7,)),
        ],
        compiler_params=params(40),
        name="slope",
    )(h, mom, bed, fric, act, above, below, from_left, from_right, own, off)


def prepare_kernel(d, lm, above, below, from_left, from_right, coef, momentum, turn):
    for t in range(5):
        s = slice(128 * t, 128 * t + 128)
        both = jnp.concatenate(
            [from_left[:, s], jnp.zeros((32, 128), F32), from_right[:, s], jnp.zeros((32, 128), F32)], axis=0
        )
        turn[s, :] = both.T
    third = 1.0 / 3.0

    def halo(w, lane, i):
        left = pltpu.roll(w, 109 - 3 * i, 1)
        right = pltpu.roll(w, 48 - 3 * i, 1)
        return jnp.where(lane >= 125, left, jnp.where(lane < 3, right, 0.0))

    step = 64

    def body(t, _):
        r = pl.multiple_of(t * step, step)
        s = pl.ds(r, step)
        w = turn[s, :]
        lane = lanes((step, 128))
        to = pl.ds(pl.multiple_of(TOP + r, 8), step)
        coef[to, 0:C] = (d[s, :] - 1.0) * third
        coef[to, C:WIDE] = (halo(w, lane, 0) - 1.0) * third
        for i in range(2):
            momentum[i, s, 0:C] = lm[i, s, :]
            momentum[i, s, C:WIDE] = halo(w, lane, i + 1)
        return 0

    lax.fori_loop(0, L // step, body, 0)
    coef[0:TOP, :] = jnp.zeros((TOP, WIDE), F32)
    coef[TOP + L :, :] = jnp.zeros((TOP, WIDE), F32)
    coef[TOP - 2 : TOP, 0:C] = (above[10:12, :] - 1.0) * third
    coef[TOP + L : TOP + L + 2, 0:C] = (below[10:12, :] - 1.0) * third
    block = (halo(turn[L : L + 8, :], lanes((8, 128)), 0) - 1.0) * third
    row = rows((8, 128))
    coef[TOP - 8 : TOP, C:WIDE] = jnp.where(row == 7, block, 0.0)
    coef[TOP + L : TOP + L + 8, C:WIDE] = jnp.where(row == 0, block, 0.0)


def prepare(d, lm, above, below, from_left, from_right):
    return pl.pallas_call(
        prepare_kernel,
        out_shape=[jax.ShapeDtypeStruct((LROWS, WIDE), F32), jax.ShapeDtypeStruct((2, L, WIDE), F32)],
        scratch_shapes=[pltpu.VMEM((WIDE, 128), F32)],
        compiler_params=params(24),
        cost_estimate=pl.CostEstimate(flops=4 * MIB, bytes_accessed=8 * MIB, transcendentals=0),
        name="prepare",
    )(d, lm, above, below, from_left, from_right)


def place_kernel(recv, momentum, height, b, first, last, new_height, hot, term):
    marks = recv[pl.ds(TAG, DEV, stride=UNITS), :]
    tags = marks.T
    here = (rows((L, DEV)) + 1).astype(F32)
    for group, at in enumerate((0, 56, 60)):
        for k in range(CAP):
            col = (group * CAP + k) * DEV
            hot[:, col : col + DEV] = (here == tags[at + k : at + k + 1, :]).astype(BF16)
    own = hot[:, 0 : CAP * DEV]
    for c in range(3):
        for k in range(CAP):
            for j in range(4):
                parts = split3(recv[pl.ds(12 * k + 4 * c + j, DEV, stride=UNITS), :])
                for t in range(3):
                    term[t, DEV * k : DEV * k + DEV, 128 * j : 128 * j + 128] = parts[t]
        flow = (
            jnp.dot(own, term[0], preferred_element_type=F32)
            + jnp.dot(own, term[1], preferred_element_type=F32)
            + jnp.dot(own, term[2], preferred_element_type=F32)
        )
        if c == 0:
            new_height[...] = height[...] + flow
        else:
            b[c - 1, :, 0:C] = momentum[c - 1, :, 0:C] + flow
    side = hot[:, CAP * DEV : 3 * CAP * DEV]
    lane = lanes((DEV, 128))
    for c in range(2):
        left, right = [], []
        for k in range(CAP):
            left.append(jnp.where(lane >= 125, pltpu.roll(marks, 117 - 6 * k - 3 * c, 1), 0.0))
            right.append(jnp.where(lane < 3, pltpu.roll(marks, 96 - 6 * k - 3 * c, 1), 0.0))
        parts = split3(jnp.concatenate(left + right, axis=0))
        b[c, :, C:WIDE] = (
            momentum[c, :, C:WIDE]
            + jnp.dot(side, parts[0], preferred_element_type=F32)
            + jnp.dot(side, parts[1], preferred_element_type=F32)
            + jnp.dot(side, parts[2], preferred_element_type=F32)
        )
    first[...] = b[:, 0:8, :]
    last[...] = b[:, L - 8 : L, :]


def place(recv, momentum, height):
    return pl.pallas_call(
        place_kernel,
        out_shape=[
            jax.ShapeDtypeStruct((2, L, WIDE), F32),
            jax.ShapeDtypeStruct((2, 8, WIDE), F32),
            jax.ShapeDtypeStruct((2, 8, WIDE), F32),
            jax.ShapeDtypeStruct((L, C), F32),
        ],
        scratch_shapes=[pltpu.VMEM((L, 3 * CAP * DEV), BF16), pltpu.VMEM((3, CAP * DEV, C), BF16)],
        compiler_params=params(40),
        name="place",
    )(recv, momentum, height)


def krylov_kernel(sides, b_in, above, below, coef, w1_out, w2_out, sums, b, w1, w2, sems):
    copies = [
        pltpu.make_async_copy(b_in.at[i], b.at[i, pl.ds(TOP, L), :], sems.at[i]) for i in range(2)
    ]
    for c in copies:
        c.start()
    for x in (b, w1, w2):
        for i in range(2):
            x[i, 0 : TOP - 8, :] = jnp.zeros((TOP - 8, WIDE), F32)
            x[i, TOP + L + 8 :, :] = jnp.zeros((TOP - 8, WIDE), F32)
    b[:, TOP - 8 : TOP, :] = above[...]
    b[:, TOP + L : TOP + L + 8, :] = below[...]
    up, down, left, right = (sides[i].astype(F32) for i in range(4))
    edge = jnp.where(lanes((1, 128)) < 64, right, left)
    for c in copies:
        c.wait()
    sixth = 1.0 / 6.0

    def image(x, i, r, n):
        s = pl.ds(r, n)
        v = x[i, s, :]
        around = (previous_row(x, i, r, n, WIDE) + next_row(x, i, r, n, WIDE)) + (
            pltpu.roll(v, 1, 1) + pltpu.roll(v, WIDE - 1, 1)
        )
        return v, coef[s, :] * v - sixth * around

    def store(x, i, s, w, scale=None):
        tail = w[:, C:WIDE] * edge
        if scale is not None:
            w, tail = w * scale, tail * scale
        x[i, s, 0:C] = w[:, 0:C]
        x[i, s, C:WIDE] = tail

    def dot(x, y):
        p = x[:, 0:C] * y[:, 0:C]
        p = (p[:, 0:128] + p[:, 128:256]) + (p[:, 256:384] + p[:, 384:512])
        return sum(p[8 * q : 8 * q + 8, :] for q in range(p.shape[0] // 8))

    chunk = 16
    zero = jnp.zeros((8, 128), F32)

    def sweep(src, dst, out, kinds):
        if dst is not None:
            for i in range(2):
                _, w = image(src, i, TOP - 8, 8)
                store(dst, i, slice(TOP - 8, TOP), w, up)
                _, w = image(src, i, TOP + L, 8)
                store(dst, i, slice(TOP + L, TOP + L + 8), w, down)

        def body(t, carry):
            r = pl.multiple_of(TOP + t * chunk, 8)
            carry = list(carry)
            for i in range(2):
                v, w = image(src, i, r, chunk)
                if dst is not None:
                    store(dst, i, pl.ds(r, chunk), w)
                    out[i, pl.ds(pl.multiple_of(t * chunk, 8), chunk), :] = w[:, 0:C]
                for q, kind in enumerate(kinds):
                    a, c = {"vv": (v, v), "vw": (v, w), "ww": (w, w)}[kind]
                    at = i * len(kinds) + q
                    carry[at] = carry[at] + dot(a, c)
            return tuple(carry)

        total = lax.fori_loop(0, L // chunk, body, (zero,) * (2 * len(kinds)))
        return total[: len(kinds)], total[len(kinds) :]

    s1 = sweep(b, w1, w1_out, ("vv", "vw", "ww"))
    s2 = sweep(w1, w2, w2_out, ("vw", "ww"))
    s3 = sweep(w2, None, None, ("vw",))
    flat = []
    for i in range(2):
        flat += list(s1[i]) + list(s2[i]) + list(s3[i]) + [zero, zero]
    stack = jnp.concatenate([jnp.sum(x, axis=0, keepdims=True) for x in flat], axis=0)
    total = jnp.sum(stack, axis=1, keepdims=True)
    line = jnp.sum(jnp.where(lanes((16, 128)) == rows((16, 128)), total, 0.0), axis=0, keepdims=True)
    sums[...] = jnp.broadcast_to(line, (DEV, 128))


def krylov(sides, b, above, below, coef):
    hbm = pl.BlockSpec(memory_space=pl.ANY)
    vmem = pl.BlockSpec(memory_space=pltpu.VMEM)
    return pl.pallas_call(
        krylov_kernel,
        in_specs=[pl.BlockSpec(memory_space=pltpu.SMEM), hbm, vmem, vmem, vmem],
        out_specs=[vmem] * 3,
        out_shape=[
            jax.ShapeDtypeStruct((2, L, C), F32),
            jax.ShapeDtypeStruct((2, L, C), F32),
            jax.ShapeDtypeStruct((DEV, 128), F32),
        ],
        scratch_shapes=[pltpu.VMEM((2, LROWS, WIDE), F32)] * 3 + [pltpu.SemaphoreType.DMA((2,))],
        compiler_params=params(40),
        name="krylov",
    )(sides, b, above, below, coef)


def steps(nu):
    def inner(u, v):
        return sum(u[i] * v[j] * nu[i + j] for i in range(len(u)) for j in range(len(v)))

    def times(u):
        lo = [4.0 * x for x in u] + [None]
        hi = [None] + [3.0 * x for x in u]
        return [a if b is None else b if a is None else a + b for a, b in zip(lo, hi)]

    def add(u, v, scale):
        u = list(u) + [None] * (len(v) - len(u))
        return [x + scale * y if x is not None and y is not None else scale * y if x is None else x
                for x, y in zip(u, list(v) + [None] * (len(u) - len(v)))]

    r = p = [jnp.ones_like(nu[0])]
    rr = nu[0]
    x = None
    for it in range(3):
        image = times(p)
        curve = inner(p, image)
        alpha = jnp.where(curve > 0.0, rr / curve, 0.25)
        alpha = jnp.minimum(jnp.maximum(alpha, 1.0 / 7.0), 1.0 / 1.2)
        x = [alpha * q for q in p] if x is None else add(x, p, alpha)
        if it == 2:
            return x
        r = add(r, image, -alpha)
        new = jnp.maximum(inner(r, r), 0.0)
        beta = jnp.minimum(jnp.where(rr > 0.0, new / rr, 0.0), 6.0)
        p = add(r, p, beta)
        rr = new


def finish_kernel(sums, b, w1, w2, x, coef):
    total = jnp.sum(sums[...], axis=0, keepdims=True)
    lane = lanes((1, 128))
    for c in range(2):
        nu = [
            jnp.sum(jnp.where(lane == 8 * c + k, total, 0.0), axis=1, keepdims=True) for k in range(6)
        ]
        e = steps(nu)
        for k in range(3):
            coef[3 * c + k : 3 * c + k + 1, :] = jnp.broadcast_to(e[k], (1, 128))
    step = 32

    for c in range(2):
        e = [jnp.broadcast_to(coef[3 * c + k : 3 * c + k + 1, 0:1], (step, C)) for k in range(3)]

        def body(t, _):
            s = pl.ds(pl.multiple_of(t * step, step), step)
            x[c, s, :] = e[0] * b[c, s, 0:C] + e[1] * w1[c, s, :] + e[2] * w2[c, s, :]
            return 0

        lax.fori_loop(0, L // step, body, 0)


def finish(sums, b, w1, w2):
    return pl.pallas_call(
        finish_kernel,
        out_shape=jax.ShapeDtypeStruct((2, L, C), F32),
        scratch_shapes=[pltpu.VMEM((8, 128), F32)],
        compiler_params=params(24),
        name="finish",
    )(sums, b, w1, w2)


def shift(x, axis, by):
    n = {"gx": NX, "gy": NY}[axis]
    return lax.ppermute(x, axis, [(i, i + by) for i in range(n) if 0 <= i + by < n])


def exchange(x):
    return lax.all_to_all(x, AXES, split_axis=0, concat_axis=0, tiled=True)


def per_device(h, mom, bed, fric, act, owners, offsets, height, lm, d):
    up, dn = edge_rows(h, mom, bed, fric, act, d)
    above, below = shift(dn, "gx", 1), shift(up, "gx", -1)
    to_right, to_left = edge_columns(h, mom, bed, fric, act, d, lm, above, below)
    from_left, from_right = shift(to_right, "gy", 1), shift(to_left, "gy", -1)
    own, off = owners.reshape(1, R), offsets.reshape(1, R)
    fields, payload = slope(h, mom, bed, fric, act, above, below, from_left, from_right, own, off)
    recv = exchange(payload.reshape(DEV, UNITS, 1, 128)).reshape(DEV * UNITS, 128)
    coef, momentum = prepare(d, lm, above, below, from_left, from_right)
    b, first, last, new_height = place(recv, momentum, height)
    b_above, b_below = shift(last, "gx", 1), shift(first, "gx", -1)
    i, j = lax.axis_index("gx"), lax.axis_index("gy")
    sides = jnp.stack([i > 0, i < NX - 1, j > 0, j < NY - 1]).astype(jnp.int32)
    w1, w2, sums = krylov(sides, b, b_above, b_below, coef)
    sums = exchange(sums.reshape(DEV, 1, 128)).reshape(DEV, 128)
    return fields, new_height, finish(sums, b, w1, w2)


def solution(mesh):
    return jax.shard_map(
        per_device,
        mesh=mesh,
        in_specs=(
            P("gx", "gy"),
            P(None, "gx", "gy"),
            P(None, "gx", "gy"),
            P("gx", "gy"),
            P("gx", "gy"),
            P("gx", "gy", None, None),
            P("gx", "gy", None),
            P("gx", "gy"),
            P(None, "gx", "gy"),
            P("gx", "gy"),
        ),
        out_specs=(P(None, "gx", "gy"), P("gx", "gy"), P(None, "gx", "gy")),
        check_vma=False,
    )
```

```python
import functools

import jax
import jax.numpy as jnp
from jax import lax
from jax.experimental import pallas as pl
from jax.experimental.pallas import tpu as pltpu
from jax.sharding import PartitionSpec as P

F32 = jnp.float32
BF16 = jnp.bfloat16
AXES = ("gx", "gy")
NX, NY = 8, 16
DEV = NX * NY
R, C, L = 256, 512, 512
CAP = 4
UNITS = 12 * CAP + 1
TAG = 12 * CAP
WIDE = C + 128
TOP = 16
SROWS = R + 2 * TOP
CHUNK = 32
LTOP = 16
LROWS = L + 2 * LTOP
LCHUNK = 64
LSUB = 16
MIB = 1 << 20


HBM = pl.BlockSpec(memory_space=pltpu.HBM)
VMEM = pl.BlockSpec(memory_space=pltpu.VMEM)


def params(limit=None):
    return pltpu.CompilerParams(vmem_limit_bytes=limit * MIB if limit else 60 * 1024 * 1024)


def lanes(shape):
    return lax.broadcasted_iota(jnp.int32, shape, len(shape) - 1)


def rows(shape):
    return lax.broadcasted_iota(jnp.int32, shape, len(shape) - 2)


def edge_rows_kernel(h, m, b, f, a, d, up, dn, hs, ms, bs, fs, as_, ds, sems):
    copies = []
    for q, (src, dst) in enumerate(((h, hs), (f, fs), (a, as_), (d, ds))):
        for side, r in enumerate((0, src.shape[0] - 8)):
            copies.append(pltpu.make_async_copy(src.at[pl.ds(r, 8), :], dst.at[side], sems.at[2 * q + side]))
    for q, (src, dst) in enumerate(((m, ms), (b, bs))):
        for side, r in enumerate((0, R - 8)):
            copies.append(pltpu.make_async_copy(src.at[:, pl.ds(r, 8), :], dst.at[side], sems.at[8 + 2 * q + side]))
    for c in copies:
        c.start()
    for c in copies:
        c.wait()
    for side, out, two, one in ((0, up, slice(0, 2), slice(0, 1)), (1, dn, slice(6, 8), slice(7, 8))):
        out[0:2, :] = hs[side, two, :]
        out[2:4, :] = ms[side, 0, two, :]
        out[4:6, :] = ms[side, 1, two, :]
        out[6:7, :] = bs[side, 0, one, :]
        out[7:8, :] = bs[side, 1, one, :]
        out[8:9, :] = fs[side, one, :]
        out[9:10, :] = as_[side, one, :].astype(F32)
        out[10:12, :] = ds[side, two, :]
        out[12:16, :] = jnp.zeros((4, C), F32)


def edge_rows(h, mom, bed, fric, act, d):
    return pl.pallas_call(
        edge_rows_kernel,
        in_specs=[HBM] * 6,
        out_specs=[VMEM] * 2,
        out_shape=[jax.ShapeDtypeStruct((16, C), F32)] * 2,
        scratch_shapes=[
            pltpu.VMEM((2, 8, C), F32),
            pltpu.VMEM((2, 2, 8, C), F32),
            pltpu.VMEM((2, 2, 8, C), F32),
            pltpu.VMEM((2, 8, C), F32),
            pltpu.VMEM((2, 8, C), jnp.int32),
            pltpu.VMEM((2, 8, C), F32),
            pltpu.SemaphoreType.DMA((12,)),
        ],
        compiler_params=params(),
        name="edge_rows",
    )(h, mom, bed, fric, act, d)


def edge_columns_kernel(h, m, b, f, a, d, l, above, below, right, left, mat):
    sides = (slice(0, 128), slice(C - 128, C))

    def pair(read):
        return tuple(functools.partial(read, lane) for lane in sides)

    slope = (
        pair(lambda lane, s: h[s, lane]),
        pair(lambda lane, s: m[0, s, lane]),
        pair(lambda lane, s: m[1, s, lane]),
        pair(lambda lane, s: b[0, s, lane]),
        pair(lambda lane, s: b[1, s, lane]),
        pair(lambda lane, s: f[s, lane]),
        pair(lambda lane, s: a[s, lane].astype(F32)),
    )
    lake = (
        pair(lambda lane, s: d[s, lane]),
        pair(lambda lane, s: l[0, s, lane]),
        pair(lambda lane, s: l[1, s, lane]),
    )
    step = 64

    def put(acc, lane, first, last, i, wide):
        base, base_left = (2 * i, 64 + 2 * i) if wide == 2 else (16 + 3 * i, 80 + 3 * i)
        turned = pltpu.roll(last, (base + wide) % 128, 1)
        acc = jnp.where((lane >= base) & (lane < base + wide), turned, acc)
        turned = pltpu.roll(first, base_left, 1)
        return jnp.where((lane >= base_left) & (lane < base_left + wide), turned, acc)

    def both(t, _):
        s = pl.ds(pl.multiple_of(t * step, step), step)
        lane = lanes((step, 128))
        acc = jnp.zeros((step, 128), F32)
        for i, (first, last) in enumerate(slope):
            acc = put(acc, lane, first(s), last(s), i, 2)
        for i, (first, last) in enumerate(lake):
            acc = put(acc, lane, first(s), last(s), i, 3)
        mat[s, :] = acc
        return 0

    def lake_only(t, _):
        s = pl.ds(pl.multiple_of(t * step, step), step)
        lane = lanes((step, 128))
        acc = jnp.zeros((step, 128), F32)
        for i, (first, last) in enumerate(lake):
            acc = put(acc, lane, first(s), last(s), i, 3)
        mat[s, :] = acc
        return 0

    lax.fori_loop(0, R // step, both, 0)
    lax.fori_loop(R // step, L // step, lake_only, 0)
    lane, row = lanes((8, 128)), rows((8, 128))

    def corner(b_row, a_row, where):
        low = jnp.broadcast_to(below[b_row : b_row + 1, where], (8, 128))
        high = jnp.broadcast_to(above[a_row : a_row + 1, where], (8, 128))
        return jnp.where(row == 0, low, jnp.where(row == 7, high, 0.0))

    acc = mat[R : R + 8, :]
    for i in range(3):
        acc = put(acc, lane, corner(2 * i, 2 * i + 1, slice(0, 128)), corner(2 * i, 2 * i + 1, slice(C - 128, C)), i, 2)
    mat[R : R + 8, :] = acc
    acc = put(jnp.zeros((8, 128), F32), lane, corner(10, 11, slice(0, 128)), corner(10, 11, slice(C - 128, C)), 0, 3)
    mat[L : L + 8, :] = acc
    mat[L + 8 : L + 128, :] = jnp.zeros((120, 128), F32)
    for t in range(5):
        turned = mat[128 * t : 128 * t + 128, :].T
        right[:, 128 * t : 128 * t + 128] = turned[0:32, :]
        left[:, 128 * t : 128 * t + 128] = turned[64:96, :]


def edge_columns(h, mom, bed, fric, act, d, lm, above, below):
    return pl.pallas_call(
        edge_columns_kernel,
        in_specs=[VMEM] * 9,
        out_specs=[VMEM] * 2,
        out_shape=[jax.ShapeDtypeStruct((32, WIDE), F32)] * 2,
        scratch_shapes=[pltpu.VMEM((WIDE, 128), F32)],
        compiler_params=params(16),
        name="edge_columns",
    )(h, mom, bed, fric, act, d, lm, above, below)


def split2(x):
    hi = x.astype(BF16)
    return hi, (x - hi.astype(F32)).astype(BF16)


def pick(hot, parts):
    return jnp.dot(hot, parts[0], preferred_element_type=F32) + jnp.dot(hot, parts[1], preferred_element_type=F32)


def beside(xs):
    lane = lanes(xs[0].shape)
    r = [pltpu.roll(x, 1, 1) for x in xs]
    left = [jnp.where(lane == 0, r[j - 1], r[j]) for j in range(5)]
    r = [pltpu.roll(x, 127, 1) for x in xs]
    right = [jnp.where(lane == 127, r[(j + 1) % 5], r[j]) for j in range(5)]
    return left, right


def slope_kernel(
    h_in, mom, bed, fric, act, above, below, from_left, from_right, own, off,
    out, payload,
    ends, side, pa, qa, acc, turn,
):
    tile = (
        lambda s, lane: h_in[s, lane],
        lambda s, lane: mom[0, s, lane],
        lambda s, lane: mom[1, s, lane],
        lambda s, lane: bed[0, s, lane],
        lambda s, lane: bed[1, s, lane],
        lambda s, lane: fric[s, lane],
        lambda s, lane: act[s, lane].astype(F32),
    )
    ends[...] = jnp.zeros(ends.shape, F32)
    for i in range(7):
        for j in range(4):
            s = slice(128 * j, 128 * j + 128)
            if i < 3:
                ends[0, i, j, 6:8, :] = above[2 * i : 2 * i + 2, s]
                ends[1, i, j, 0:2, :] = below[2 * i : 2 * i + 2, s]
            else:
                ends[0, i, j, 7:8, :] = above[3 + i : 4 + i, s]
                ends[1, i, j, 0:1, :] = below[3 + i : 4 + i, s]
    for t in range(3):
        s = slice(128 * t, 128 * t + 128)
        both = jnp.concatenate(
            [from_left[:, s], jnp.zeros((32, 128), F32), from_right[:, s], jnp.zeros((32, 128), F32)], axis=0
        )
        turn[s, :] = both.T

    def halo(w, lane, i):
        left = pltpu.roll(w, 126 - 2 * i, 1)
        right = pltpu.roll(w, 64 - 2 * i, 1)
        return jnp.where(lane >= 126, left, jnp.where(lane < 2, right, 0.0))

    step = 64

    def columns(t, _):
        r = pl.multiple_of(t * step, step)
        w = turn[pl.ds(r, step), :]
        lane = lanes((step, 128))
        for i in range(7):
            side[i, pl.ds(r, step), :] = halo(w, lane, i)
        return 0

    lax.fori_loop(0, R // step, columns, 0)
    w = turn[R : R + 8, :]
    row = rows((8, 128))
    for i in range(3):
        block = halo(w, lanes((8, 128)), i)
        ends[0, i, 4, :, :] = jnp.where(row == 7, block, 0.0)
        ends[1, i, 4, :, :] = jnp.where(row == 0, block, 0.0)

    k, q = 0.075, 0.25 / 0.075

    def fluxes(u, s, get, h, m, n):
        pairs = [[], [], []]
        for j in range(5):
            inv = 1.0 / jnp.maximum(h[j], 0.25)
            p = (0.5 * h[j]) * h[j]
            mi = m[j] * inv
            cross = mi * n[j]
            fm = mi * m[j] + p
            gn = (n[j] * inv) * n[j] + p
            h4, m4, n4 = q * h[j], q * m[j], q * n[j]
            pa[u, 0, j, s, :] = h4 - m[j]
            qa[u, 0, j, s, :] = h4 + m[j]
            pa[u, 1, j, s, :] = m4 - fm
            qa[u, 1, j, s, :] = m4 + fm
            pa[u, 2, j, s, :] = n4 - cross
            qa[u, 2, j, s, :] = n4 + cross
            fr = get(5, j)
            pairs[0].append((h4 - n[j], h4 + n[j], None))
            pairs[1].append((m4 - cross, m4 + cross, 2.0 * (h[j] * get(3, j) - fr * m[j])))
            pairs[2].append((n4 - gn, n4 + gn, 2.0 * (h[j] * get(4, j) - fr * n[j])))
        for i in range(3):
            _, right = beside([x[0] for x in pairs[i]])
            left, _ = beside([x[1] for x in pairs[i]])
            for j in range(5):
                x = left[j] + right[j]
                acc[u, i, j, s, :] = x if i == 0 else x + pairs[i][j][2]

    def combine(u, i, j, r, n, on):
        return (k * on) * (
            acc[u, i, j, pl.ds(r, n), :] + pa[u, i, j, pl.ds(r + 1, n), :] + qa[u, i, j, pl.ds(r - 1, n), :]
        )

    def reader(s):
        def get(i, j):
            return side[i, s, :] if j == 4 else tile[i](s, slice(128 * j, 128 * j + 128))

        return get

    def end_reader(e):
        return lambda i, j: ends[e, i, j, :, :]

    def section(u, to, n, get):
        if u == 0:
            new = [[get(i, j) for j in range(5)] for i in range(3)]
        else:
            new = [[combine(0, i, j, to, n, get(6, j)) for j in range(5)] for i in range(3)]
        fluxes(u, pl.ds(to, n), get, *new)

    def body(u):
        def run(t, _):
            r = pl.multiple_of(t * CHUNK, CHUNK)
            section(u, pl.multiple_of(TOP + r, 8), CHUNK, reader(pl.ds(r, CHUNK)))
            return 0

        return run

    def last(t, _):
        r = pl.multiple_of(t * CHUNK, CHUNK)
        to = pl.ds(r, CHUNK)
        for j in range(4):
            s = slice(128 * j, 128 * j + 128)
            on = tile[6](to, s)
            for i in range(3):
                out[i, to, s] = combine(1, i, j, pl.multiple_of(TOP + r, 8), CHUNK, on)
        return 0

    pa[0, :, :, TOP + R + 8 :, :] = jnp.zeros((3, 5, 8, 128), F32)
    qa[0, :, :, 0:8, :] = jnp.zeros((3, 5, 8, 128), F32)
    for u in range(2):
        section(u, TOP - 8, 8, end_reader(0))
        section(u, TOP + R, 8, end_reader(1))
        lax.fori_loop(0, R // CHUNK, body(u), 0)
    lax.fori_loop(0, R // CHUNK, last, 0)

    owner = jnp.broadcast_to(own[...], (DEV, R))
    mine = rows((DEV, R)) == owner
    before = (rows((R, R)) < lanes((R, R))).astype(BF16)
    rank = jnp.dot(mine.astype(BF16), before, preferred_element_type=F32)
    picks = [mine & (rank == float(k_)) for k_ in range(CAP)]
    pickb = [p.astype(BF16) for p in picks]
    for i in range(3):
        parts = split2(out[i])
        for k_ in range(CAP):
            y = pick(pickb[k_], parts)
            for j in range(4):
                payload[pl.ds(12 * k_ + 4 * i + j, DEV, stride=UNITS), :] = y[:, 128 * j : 128 * j + 128]

    lane, dest = lanes((DEV, 128)), rows((DEV, 128))
    tags = jnp.zeros((DEV, 128), F32)
    tag_value = jnp.broadcast_to((off[...] + 1).astype(F32), (DEV, R))
    edge_lane = lanes((R, 128))
    m_first, n_first = out[1, :, 0:128], out[2, :, 0:128]
    m_last, n_last = out[1, :, C - 128 : C], out[2, :, C - 128 : C]
    edges = jnp.where(edge_lane < 3, m_first, 0.0)
    edges = jnp.where((edge_lane >= 3) & (edge_lane < 6), pltpu.roll(n_first, 3, 1), edges)
    edges = jnp.where((edge_lane >= 8) & (edge_lane < 11), pltpu.roll(m_last, 11, 1), edges)
    edges = jnp.where((edge_lane >= 11) & (edge_lane < 14), pltpu.roll(n_last, 14, 1), edges)
    parts = split2(edges)
    to_right = jnp.zeros((DEV, 128), F32)
    to_left = jnp.zeros((DEV, 128), F32)
    for k_ in range(CAP):
        tag = jnp.sum(jnp.where(picks[k_], tag_value, 0.0), axis=1, keepdims=True)
        tags = jnp.where(lane == k_, tag, tags)
        g = pick(pickb[k_], parts)
        at = 8 + 6 * k_
        to_right = jnp.where((lane >= at) & (lane < at + 6), pltpu.roll(g, at - 8, 1) if k_ else g, to_right)
        to_right = jnp.where(lane == 56 + k_, tag, to_right)
        at = 32 + 6 * k_
        to_left = jnp.where((lane >= at) & (lane < at + 6), pltpu.roll(g, at, 1), to_left)
        to_left = jnp.where(lane == 60 + k_, tag, to_left)
    column = lax.rem(dest, NY)
    to_right = jnp.where(column > 0, pltpu.roll(to_right, 1, 0), 0.0)
    to_left = jnp.where(column < NY - 1, pltpu.roll(to_left, DEV - 1, 0), 0.0)
    payload[pl.ds(TAG, DEV, stride=UNITS), :] = tags + to_right + to_left


def slope(h, mom, bed, fric, act, above, below, from_left, from_right, own, off):
    return pl.pallas_call(
        slope_kernel,
        in_specs=[VMEM] * 11,
        out_specs=[VMEM] * 2,
        out_shape=[jax.ShapeDtypeStruct((3, R, C), F32), jax.ShapeDtypeStruct((DEV * UNITS, 128), F32)],
        scratch_shapes=[
            pltpu.VMEM((2, 7, 5, 8, 128), F32),
            pltpu.VMEM((7, R, 128), F32),
            pltpu.VMEM((2, 3, 5, SROWS, 128), F32),
            pltpu.VMEM((2, 3, 5, SROWS, 128), F32),
            pltpu.VMEM((2, 3, 5, SROWS, 128), F32),
            pltpu.VMEM((384, 128), F32),
        ],
        compiler_params=params(34),
        name="slope",
    )(h, mom, bed, fric, act, above, below, from_left, from_right, own, off)


def prepare_kernel(d, lm, above, below, from_left, from_right, coef, momentum, first, last, turn):
    for t in range(5):
        s = slice(128 * t, 128 * t + 128)
        both = jnp.concatenate(
            [from_left[:, s], jnp.zeros((32, 128), F32), from_right[:, s], jnp.zeros((32, 128), F32)], axis=0
        )
        turn[s, :] = both.T

    def halo(w, lane, i):
        left = pltpu.roll(w, 109 - 3 * i, 1)
        right = pltpu.roll(w, 48 - 3 * i, 1)
        return jnp.where(lane >= 125, left, jnp.where(lane < 3, right, 0.0))

    step = 64

    def body(t, _):
        r = pl.multiple_of(t * step, step)
        s = pl.ds(r, step)
        w = turn[s, :]
        lane = lanes((step, 128))
        to = pl.ds(pl.multiple_of(LTOP + r, 8), step)
        for j in range(4):
            coef[j, to, :] = 2.0 * d[s, 128 * j : 128 * j + 128] - 2.0
        coef[4, to, :] = 2.0 * halo(w, lane, 0) - 2.0
        for i in range(2):
            for j in range(4):
                momentum[i, j, s, :] = lm[i, s, 128 * j : 128 * j + 128]
            momentum[i, 4, s, :] = halo(w, lane, i + 1)
        return 0

    lax.fori_loop(0, L // step, body, 0)
    for j in range(5):
        coef[j, 0:LTOP, :] = jnp.zeros((LTOP, 128), F32)
        coef[j, LTOP + L :, :] = jnp.zeros((LTOP, 128), F32)
        if j < 4:
            s = slice(128 * j, 128 * j + 128)
            coef[j, LTOP - 2 : LTOP, :] = 2.0 * above[10:12, s] - 2.0
            coef[j, LTOP + L : LTOP + L + 2, :] = 2.0 * below[10:12, s] - 2.0
    block = 2.0 * halo(turn[L : L + 8, :], lanes((8, 128)), 0) - 2.0
    row = rows((8, 128))
    coef[4, LTOP - 8 : LTOP, :] = jnp.where(row == 7, block, 0.0)
    coef[4, LTOP + L : LTOP + L + 8, :] = jnp.where(row == 0, block, 0.0)
    first[...] = momentum[:, :, 0:8, :]
    last[...] = momentum[:, :, L - 8 : L, :]


def prepare(d, lm, above, below, from_left, from_right):
    return pl.pallas_call(
        prepare_kernel,
        out_shape=[jax.ShapeDtypeStruct(x, F32) for x in ((5, LROWS, 128), (2, 5, L, 128), (2, 5, 8, 128), (2, 5, 8, 128))],
        scratch_shapes=[pltpu.VMEM((WIDE, 128), F32)],
        compiler_params=params(16),
        cost_estimate=pl.CostEstimate(flops=4 * MIB, bytes_accessed=8 * MIB, transcendentals=0),
        name="prepare",
    )(d, lm, above, below, from_left, from_right)


def one_hot(hot, tags, first):
    here = (rows((L, DEV)) + 1).astype(F32)
    for group, at in enumerate(first):
        for k in range(CAP):
            col = (group * CAP + k) * DEV
            hot[:, col : col + DEV] = (here == tags[at + k : at + k + 1, :]).astype(BF16)


def gather(recv, term, c):
    for k in range(CAP):
        for j in range(4):
            parts = split2(recv[pl.ds(12 * k + 4 * c + j, DEV, stride=UNITS), :])
            for t in range(2):
                term[t, DEV * k : DEV * k + DEV, 128 * j : 128 * j + 128] = parts[t]


def place_kernel(recv, first_momentum, last_momentum, flow, first, last, hot, term):
    marks = recv[pl.ds(TAG, DEV, stride=UNITS), :]
    one_hot(hot, marks.T, (0, 56, 60))
    own = hot[:, 0 : CAP * DEV]
    side = hot[:, CAP * DEV : 3 * CAP * DEV]
    lane = lanes((DEV, 128))
    for c in range(2):
        gather(recv, term, c + 1)
        sums = pick(own, (term[0], term[1]))
        for j in range(4):
            flow[c, j, :, :] = sums[:, 128 * j : 128 * j + 128]
        left, right = [], []
        for k in range(CAP):
            left.append(jnp.where(lane >= 125, pltpu.roll(marks, 117 - 6 * k - 3 * c, 1), 0.0))
            right.append(jnp.where(lane < 3, pltpu.roll(marks, 96 - 6 * k - 3 * c, 1), 0.0))
        flow[c, 4, :, :] = pick(side, split2(jnp.concatenate(left + right, axis=0)))
    first[...] = first_momentum[...] + flow[:, :, 0:8, :]
    last[...] = last_momentum[...] + flow[:, :, L - 8 : L, :]


def place(recv, first_momentum, last_momentum):
    return pl.pallas_call(
        place_kernel,
        out_shape=[jax.ShapeDtypeStruct((2, 5, n, 128), F32) for n in (L, 8, 8)],
        scratch_shapes=[pltpu.VMEM((L, 3 * CAP * DEV), BF16), pltpu.VMEM((2, CAP * DEV, C), BF16)],
        compiler_params=params(20),
        name="place",
    )(recv, first_momentum, last_momentum)


def raise_kernel(recv, height, new_height, hot, term):
    one_hot(hot, recv[pl.ds(TAG, DEV, stride=UNITS), :].T, (0,))
    gather(recv, term, 0)
    new_height[...] = height[...] + pick(hot[...], (term[0], term[1]))


def raise_lake(recv, height):
    return pl.pallas_call(
        raise_kernel,
        in_specs=[VMEM] * 2,
        out_specs=VMEM,
        out_shape=jax.ShapeDtypeStruct((L, C), F32),
        scratch_shapes=[pltpu.VMEM((L, CAP * DEV), BF16), pltpu.VMEM((2, CAP * DEV, C), BF16)],
        compiler_params=params(8),
        cost_estimate=pl.CostEstimate(flops=600 * MIB, bytes_accessed=6 * MIB, transcendentals=0),
        name="raise_lake",
    )(recv, height)


def krylov_kernel(sides, flow, momentum, above, below, coef, b, w1, w2, sums):
    for x in (b, w1, w2):
        x[:, :, 0 : LTOP - 8, :] = jnp.zeros((2, 5, LTOP - 8, 128), F32)
        x[:, :, LTOP + L + 8 :, :] = jnp.zeros((2, 5, LTOP - 8, 128), F32)
    b[:, :, LTOP - 8 : LTOP, :] = above[...]
    b[:, :, LTOP + L : LTOP + L + 8, :] = below[...]
    up, down, left, right = (sides[i].astype(F32) for i in range(4))
    edge = jnp.where(lanes((1, 128)) < 64, right, left)

    def total_side(t, _):
        r = pl.multiple_of(t * 64, 64)
        for i in range(2):
            for j in range(5):
                b[i, j, pl.ds(pl.multiple_of(LTOP + r, 8), 64), :] = (
                    flow[i, j, pl.ds(r, 64), :] + momentum[i, j, pl.ds(r, 64), :]
                )
        return 0

    lax.fori_loop(0, L // 64, total_side, 0)

    def image(x, i, r, n):
        v = [x[i, j, pl.ds(r, n), :] for j in range(5)]
        west, east = beside(v)
        w = []
        for j in range(5):
            around = (x[i, j, pl.ds(r - 1, n), :] + x[i, j, pl.ds(r + 1, n), :]) + (west[j] + east[j])
            w.append(coef[j, pl.ds(r, n), :] * v[j] - around)
        w[4] = w[4] * edge
        return v, w

    def dot(x, y):
        p = (x[0] * y[0] + x[1] * y[1]) + (x[2] * y[2] + x[3] * y[3])
        p = [p[8 * q : 8 * q + 8, :] for q in range(p.shape[0] // 8)]
        while len(p) > 1:
            p = [a + c for a, c in zip(p[::2], p[1::2])]
        return p[0]

    zero = jnp.zeros((8, 128), F32)

    def sweep(src, dst, kinds):
        for i in range(2):
            for r, scale in ((LTOP - 8, up), (LTOP + L, down)):
                _, w = image(src, i, r, 8)
                for j in range(5):
                    dst[i, j, r : r + 8, :] = w[j] * scale

        def body(t, carry):
            r = pl.multiple_of(LTOP + t * LCHUNK, 8)
            carry = list(carry)
            for q0 in range(0, LCHUNK, LSUB):
                rq = pl.multiple_of(r + q0, 8)
                for i in range(2):
                    v, w = image(src, i, rq, LSUB)
                    for j in range(5):
                        dst[i, j, pl.ds(rq, LSUB), :] = w[j]
                    for q, kind in enumerate(kinds):
                        x, y = {"vv": (v, v), "vw": (v, w), "ww": (w, w)}[kind]
                        at = i * len(kinds) + q
                        carry[at] = carry[at] + dot(x, y)
            return tuple(carry)

        total = lax.fori_loop(0, L // LCHUNK, body, (zero,) * (2 * len(kinds)))
        return total[: len(kinds)], total[len(kinds) :]

    def last_sum(x):
        lane = lanes((LSUB, 128))

        def body(t, carry):
            r = pl.multiple_of(LTOP + t * LCHUNK, 8)
            carry = list(carry)
            for q0 in range(0, LCHUNK, LSUB):
                rq = pl.multiple_of(r + q0, 8)
                for i in range(2):
                    v = [x[i, j, pl.ds(rq, LSUB), :] for j in range(5)]
                    turned = [pltpu.roll(y, 127, 1) for y in v]
                    w = []
                    for j in range(4):
                        pair = jnp.where(lane == 127, turned[j + 1], turned[j]) + x[i, j, pl.ds(rq + 1, LSUB), :]
                        w.append(coef[j, pl.ds(rq, LSUB), :] * v[j] - 2.0 * pair)
                    carry[i] = carry[i] + dot(v, w)
            return tuple(carry)

        total = lax.fori_loop(0, L // LCHUNK, body, (zero,) * 2)
        return total[:1], total[1:]

    s1 = sweep(b, w1, ("vv", "vw", "ww"))
    s2 = sweep(w1, w2, ("vw", "ww"))
    s3 = last_sum(w2)
    flat = []
    for i in range(2):
        flat += list(s1[i]) + list(s2[i]) + list(s3[i]) + [zero, zero]
    stack = jnp.concatenate([jnp.sum(x, axis=0, keepdims=True) for x in flat], axis=0)
    total = jnp.sum(stack, axis=1, keepdims=True)
    line = jnp.sum(jnp.where(lanes((16, 128)) == rows((16, 128)), total, 0.0), axis=0, keepdims=True)
    sums[...] = jnp.broadcast_to(line, (DEV, 128))


def krylov(sides, flow, momentum, above, below, coef):
    return pl.pallas_call(
        krylov_kernel,
        in_specs=[pl.BlockSpec(memory_space=pltpu.SMEM)] + [VMEM] * 5,
        out_specs=[VMEM] * 4,
        out_shape=[jax.ShapeDtypeStruct((2, 5, LROWS, 128), F32)] * 3 + [jax.ShapeDtypeStruct((DEV, 128), F32)],
        compiler_params=params(24),
        name="krylov",
    )(sides, flow, momentum, above, below, coef)


def steps(nu):
    def inner(u, v):
        return sum(u[i] * v[j] * nu[i + j] for i in range(len(u)) for j in range(len(v)))

    def times(u):
        lo = [4.0 * x for x in u] + [None]
        hi = [None] + [0.5 * x for x in u]
        return [a if b is None else b if a is None else a + b for a, b in zip(lo, hi)]

    def add(u, v, scale):
        u = list(u) + [None] * (len(v) - len(u))
        return [x + scale * y if x is not None and y is not None else scale * y if x is None else x
                for x, y in zip(u, list(v) + [None] * (len(u) - len(v)))]

    r = p = [jnp.ones_like(nu[0])]
    rr = nu[0]
    x = None
    for it in range(3):
        image = times(p)
        curve = inner(p, image)
        alpha = jnp.where(curve > 0.0, rr / curve, 0.25)
        alpha = jnp.minimum(jnp.maximum(alpha, 1.0 / 7.0), 1.0 / 1.2)
        x = [alpha * q for q in p] if x is None else add(x, p, alpha)
        if it == 2:
            return x
        r = add(r, image, -alpha)
        new = jnp.maximum(inner(r, r), 0.0)
        beta = jnp.minimum(jnp.where(rr > 0.0, new / rr, 0.0), 6.0)
        p = add(r, p, beta)
        rr = new


def finish_kernel(sums, b, w1, w2, x_hbm, coef, x, sems):
    total = jnp.sum(sums[...], axis=0, keepdims=True)
    lane = lanes((1, 128))
    for c in range(2):
        nu = [
            jnp.sum(jnp.where(lane == 8 * c + k, total, 0.0), axis=1, keepdims=True) for k in range(6)
        ]
        e = steps(nu)
        for k in range(3):
            coef[3 * c + k : 3 * c + k + 1, :] = jnp.broadcast_to(e[k], (1, 128))
    step = 64
    copies = []
    for c in range(2):
        e = [jnp.broadcast_to(coef[3 * c + k : 3 * c + k + 1, :], (step, 128)) for k in range(3)]

        def body(t, _):
            s = pl.ds(pl.multiple_of(t * step, step), step)
            at = pl.ds(pl.multiple_of(LTOP + t * step, 8), step)
            for j in range(4):
                x[c, s, 128 * j : 128 * j + 128] = e[0] * b[c, j, at, :] + e[1] * w1[c, j, at, :] + e[2] * w2[c, j, at, :]
            return 0

        for half in range(2):
            lax.fori_loop(half * L // step // 2, (half + 1) * L // step // 2, body, 0)
            s = pl.ds(half * L // 2, L // 2)
            copies.append(pltpu.make_async_copy(x.at[c, s, :], x_hbm.at[c, s, :], sems.at[2 * c + half]))
            copies[-1].start()
    for copy in copies:
        copy.wait()


def finish(sums, b, w1, w2):
    return pl.pallas_call(
        finish_kernel,
        in_specs=[VMEM] * 4,
        out_specs=HBM,
        out_shape=jax.ShapeDtypeStruct((2, L, C), F32),
        scratch_shapes=[pltpu.VMEM((8, 128), F32), pltpu.VMEM((2, L, C), F32), pltpu.SemaphoreType.DMA((4,))],
        compiler_params=params(16),
        name="finish",
    )(sums, b, w1, w2)


def shift(x, axis, by):
    n = {"gx": NX, "gy": NY}[axis]
    return lax.ppermute(x, axis, [(i, i + by) for i in range(n) if 0 <= i + by < n])


def exchange(x):
    return lax.all_to_all(x, AXES, split_axis=0, concat_axis=0, tiled=True)


def per_device(h, mom, bed, fric, act, owners, offsets, height, lm, d):
    up, dn = edge_rows(h, mom, bed, fric, act, d)
    above, below = shift(dn, "gx", 1), shift(up, "gx", -1)
    to_right, to_left = edge_columns(h, mom, bed, fric, act, d, lm, above, below)
    from_left, from_right = shift(to_right, "gy", 1), shift(to_left, "gy", -1)
    own, off = owners.reshape(1, R), offsets.reshape(1, R)
    fields, payload = slope(h, mom, bed, fric, act, above, below, from_left, from_right, own, off)
    recv = exchange(payload.reshape(DEV, UNITS, 1, 128)).reshape(DEV * UNITS, 128)
    coef, momentum, first, last = prepare(d, lm, above, below, from_left, from_right)
    flow, first, last = place(recv, first, last)
    new_height = raise_lake(recv, height)
    b_above, b_below = shift(last, "gx", 1), shift(first, "gx", -1)
    i, j = lax.axis_index("gx"), lax.axis_index("gy")
    sides = jnp.stack([i > 0, i < NX - 1, j > 0, j < NY - 1]).astype(jnp.int32)
    flow, new_height = lax.optimization_barrier((flow, new_height))
    b, w1, w2, sums = krylov(sides, flow, momentum, b_above, b_below, coef)
    sums = exchange(sums.reshape(DEV, 1, 128)).reshape(DEV, 128)
    return fields, new_height, finish(sums, b, w1, w2)


def solution(mesh):
    return jax.shard_map(
        per_device,
        mesh=mesh,
        in_specs=(
            P("gx", "gy"),
            P(None, "gx", "gy"),
            P(None, "gx", "gy"),
            P("gx", "gy"),
            P("gx", "gy"),
            P("gx", "gy", None, None),
            P("gx", "gy", None),
            P("gx", "gy"),
            P(None, "gx", "gy"),
            P("gx", "gy"),
        ),
        out_specs=(P(None, "gx", "gy"), P("gx", "gy"), P(None, "gx", "gy")),
        check_vma=False,
    )
```

```python
import functools

import jax
import jax.numpy as jnp
from jax import lax
from jax.experimental import pallas as pl
from jax.experimental.pallas import tpu as pltpu
from jax.sharding import PartitionSpec as P

F32 = jnp.float32
BF16 = jnp.bfloat16
AXES = ("gx", "gy")
NX, NY = 8, 16
DEV = NX * NY
R, C, L = 256, 512, 512
CAP = 4
UNITS = 12 * CAP + 1
TAG = 12 * CAP
WIDE = C + 128
TOP = 16
SROWS = R + 2 * TOP
CHUNK = 32
LTOP = 16
LROWS = L + 2 * LTOP
LCHUNK = 64
LSUB = 16
MIB = 1 << 20


HBM = pl.BlockSpec(memory_space=pltpu.HBM)
VMEM = pl.BlockSpec(memory_space=pltpu.VMEM)


def params(limit=None):
    return pltpu.CompilerParams(vmem_limit_bytes=limit * MIB if limit else 60 * 1024 * 1024)


def lanes(shape):
    return lax.broadcasted_iota(jnp.int32, shape, len(shape) - 1)


def rows(shape):
    return lax.broadcasted_iota(jnp.int32, shape, len(shape) - 2)


def edge_rows_kernel(h, m, b, f, a, d, up, dn, hs, ms, bs, fs, as_, ds, sems):
    copies = []
    for q, (src, dst) in enumerate(((h, hs), (f, fs), (a, as_), (d, ds))):
        for side, r in enumerate((0, src.shape[0] - 8)):
            copies.append(pltpu.make_async_copy(src.at[pl.ds(r, 8), :], dst.at[side], sems.at[2 * q + side]))
    for q, (src, dst) in enumerate(((m, ms), (b, bs))):
        for side, r in enumerate((0, R - 8)):
            copies.append(pltpu.make_async_copy(src.at[:, pl.ds(r, 8), :], dst.at[side], sems.at[8 + 2 * q + side]))
    for c in copies:
        c.start()
    for c in copies:
        c.wait()
    for side, out, two, one in ((0, up, slice(0, 2), slice(0, 1)), (1, dn, slice(6, 8), slice(7, 8))):
        out[0:2, :] = hs[side, two, :]
        out[2:4, :] = ms[side, 0, two, :]
        out[4:6, :] = ms[side, 1, two, :]
        out[6:7, :] = bs[side, 0, one, :]
        out[7:8, :] = bs[side, 1, one, :]
        out[8:9, :] = fs[side, one, :]
        out[9:10, :] = as_[side, one, :].astype(F32)
        out[10:12, :] = ds[side, two, :]
        out[12:16, :] = jnp.zeros((4, C), F32)


def edge_rows(h, mom, bed, fric, act, d):
    return pl.pallas_call(
        edge_rows_kernel,
        in_specs=[HBM] * 6,
        out_specs=[VMEM] * 2,
        out_shape=[jax.ShapeDtypeStruct((16, C), F32)] * 2,
        scratch_shapes=[
            pltpu.VMEM((2, 8, C), F32),
            pltpu.VMEM((2, 2, 8, C), F32),
            pltpu.VMEM((2, 2, 8, C), F32),
            pltpu.VMEM((2, 8, C), F32),
            pltpu.VMEM((2, 8, C), jnp.int32),
            pltpu.VMEM((2, 8, C), F32),
            pltpu.SemaphoreType.DMA((12,)),
        ],
        compiler_params=params(),
        name="edge_rows",
    )(h, mom, bed, fric, act, d)


GROUP = R + 128
LAKE = 4 * GROUP
WIDTH = LAKE + L + 128


def put(acc, lane, first, last, base, wide):
    turned = pltpu.roll(last, (base + wide) % 128, 1)
    acc = jnp.where((lane >= base) & (lane < base + wide), turned, acc)
    turned = pltpu.roll(first, 64 + base, 1)
    return jnp.where((lane >= 64 + base) & (lane < 64 + base + wide), turned, acc)


def edge_columns_kernel(h, m, b, f, a, d, l, right, left, hs, ms, bs, fs, as_, ds, ls, mat, sems):
    copies = []
    pairs = ((h, hs), (m, ms), (b, bs), (f, fs), (a, as_), (d, ds), (l, ls))
    for q, (src, dst) in enumerate(pairs):
        for side, lane in enumerate((0, C - 128)):
            at = (slice(None),) * (len(src.shape) - 1) + (pl.ds(lane, 128),)
            copies.append(pltpu.make_async_copy(src.at[at], dst.at[side], sems.at[2 * q + side]))
    for c in copies:
        c.start()
    slope = (
        lambda e, s: hs[e, s, :],
        lambda e, s: ms[e, 0, s, :],
        lambda e, s: ms[e, 1, s, :],
        lambda e, s: bs[e, 0, s, :],
        lambda e, s: bs[e, 1, s, :],
        lambda e, s: fs[e, s, :],
        lambda e, s: as_[e, s, :].astype(F32),
    )
    lake = (
        (lambda e, s: ds[e, s, :], 32, 2),
        (lambda e, s: ls[e, 0, s, :], 34, 3),
        (lambda e, s: ls[e, 1, s, :], 37, 3),
    )
    step = 64
    mat[L:, :] = jnp.zeros((128, 128), F32)
    for c in copies:
        c.wait()

    def body(both):
        def run(t, _):
            s = pl.ds(pl.multiple_of(t * step, step), step)
            lane = lanes((step, 128))
            acc = jnp.zeros((step, 128), F32)
            if both:
                for i, read in enumerate(slope):
                    acc = put(acc, lane, read(0, s), read(1, s), 4 * i, 4)
            for read, base, wide in lake:
                acc = put(acc, lane, read(0, s), read(1, s), base, wide)
            mat[s, :] = acc
            return 0

        return run

    lax.fori_loop(0, R // step, body(True), 0)
    lax.fori_loop(R // step, L // step, body(False), 0)
    for t in range(5):
        turned = mat[128 * t : 128 * t + 128, :].T
        for out, row in ((right, 0), (left, 64)):
            if t < 3:
                for g in range(4):
                    at = GROUP * g + 128 * t
                    out[:, at : at + 128] = turned[row + 8 * g : row + 8 * g + 8, :]
            out[:, LAKE + 128 * t : LAKE + 128 * t + 128] = turned[row + 32 : row + 40, :]


def edge_columns(h, mom, bed, fric, act, d, lm):
    return pl.pallas_call(
        edge_columns_kernel,
        in_specs=[HBM] * 7,
        out_specs=[VMEM] * 2,
        out_shape=[jax.ShapeDtypeStruct((8, WIDTH), F32)] * 2,
        scratch_shapes=[
            pltpu.VMEM((2, R, 128), F32),
            pltpu.VMEM((2, 2, R, 128), F32),
            pltpu.VMEM((2, 2, R, 128), F32),
            pltpu.VMEM((2, R, 128), F32),
            pltpu.VMEM((2, R, 128), jnp.int32),
            pltpu.VMEM((2, L, 128), F32),
            pltpu.VMEM((2, 2, L, 128), F32),
            pltpu.VMEM((WIDE, 128), F32),
            pltpu.SemaphoreType.DMA((14,)),
        ],
        compiler_params=params(),
        cost_estimate=pl.CostEstimate(flops=8 * MIB, bytes_accessed=6 * MIB, transcendentals=0),
        name="edge_columns",
    )(h, mom, bed, fric, act, d, lm)


def corners_kernel(right_in, left_in, above, below, right, left):
    lane, row = lanes((8, 128)), rows((8, 128))

    def line(x, r, where):
        return jnp.broadcast_to(x[r : r + 1, where], (8, 128))

    def end(x, first_row, second_row, a, b):
        def block(where):
            y = jnp.where(row == first_row, line(x, a, where), 0.0)
            return y if b is None else jnp.where(row == second_row, line(x, b, where), y)

        return block(slice(0, 128)), block(slice(C - 128, C))

    low, high = jnp.zeros((8, 128), F32), jnp.zeros((8, 128), F32)
    for i in range(8):
        if i == 7:
            a, b, base, wide = 10, 11, 32, 2
        elif i < 3:
            a, b, base, wide = 2 * i, 2 * i + 1, 4 * i, 4
        else:
            a, b, base, wide = 3 + i, None, 4 * i, 4
        low = put(low, lane, *end(below, 0, 1, a, b), base, wide)
        if b is None:
            high = put(high, lane, *end(above, 7, None, a, None), base, wide)
        else:
            high = put(high, lane, *end(above, 6, 7, a, b), base, wide)
    turned = jnp.concatenate([low, jnp.zeros((112, 128), F32), high], axis=0).T
    for out, src, at in ((right, right_in, 0), (left, left_in, 64)):
        out[...] = src[...]
        for g in range(4):
            s = slice(GROUP * g + R, GROUP * g + R + 128)
            out[:, s] = turned[at + 8 * g : at + 8 * g + 8, :]
        out[:, LAKE + L :] = turned[at + 32 : at + 40, :]


def corners(right, left, above, below):
    return pl.pallas_call(
        corners_kernel,
        out_shape=[jax.ShapeDtypeStruct((8, WIDTH), F32)] * 2,
        compiler_params=params(4),
        name="corners",
    )(right, left, above, below)


def split2(x):
    hi = x.astype(BF16)
    return hi, (x - hi.astype(F32)).astype(BF16)


def pick(hot, parts):
    return jnp.dot(hot, parts[0], preferred_element_type=F32) + jnp.dot(hot, parts[1], preferred_element_type=F32)


def beside(xs):
    lane, n = lanes(xs[0].shape), len(xs)
    r = [pltpu.roll(x, 1, 1) for x in xs]
    left = [jnp.where(lane == 0, r[j - 1], r[j]) for j in range(n)]
    r = [pltpu.roll(x, 127, 1) for x in xs]
    right = [jnp.where(lane == 127, r[(j + 1) % n], r[j]) for j in range(n)]
    return left, right


def local_fluxes(h, m, n):
    q = 0.25 / 0.075
    inv = 1.0 / jnp.maximum(h, 0.25)
    p = (0.5 * h) * h
    mi = m * inv
    cross = mi * n
    fm = mi * m + p
    gn = (n * inv) * n + p
    h4, m4, n4 = q * h, q * m, q * n
    along = ((h4 - m, h4 + m), (m4 - fm, m4 + fm), (n4 - cross, n4 + cross))
    across = ((h4 - n, h4 + n), (m4 - cross, m4 + cross), (n4 - gn, n4 + gn))
    return along, across


def forcing(h, m, n, b0, b1, fr):
    return None, 2.0 * (h * b0 - fr * m), 2.0 * (h * b1 - fr * n)


def slope_kernel(h_in, mom, bed, fric, act, above, below, out, ends, pa, qa, acc):
    tile = (
        lambda s, lane: h_in[s, lane],
        lambda s, lane: mom[0, s, lane],
        lambda s, lane: mom[1, s, lane],
        lambda s, lane: bed[0, s, lane],
        lambda s, lane: bed[1, s, lane],
        lambda s, lane: fric[s, lane],
        lambda s, lane: act[s, lane].astype(F32),
    )
    ends[...] = jnp.zeros(ends.shape, F32)
    for i in range(7):
        for j in range(4):
            s = slice(128 * j, 128 * j + 128)
            if i < 3:
                ends[0, i, j, 6:8, :] = above[2 * i : 2 * i + 2, s]
                ends[1, i, j, 0:2, :] = below[2 * i : 2 * i + 2, s]
            else:
                ends[0, i, j, 7:8, :] = above[3 + i : 4 + i, s]
                ends[1, i, j, 0:1, :] = below[3 + i : 4 + i, s]
    k = 0.075

    def fluxes(u, s, get, h, m, n):
        pairs = [[], [], []]
        for j in range(4):
            along, across = local_fluxes(h[j], m[j], n[j])
            force = forcing(h[j], m[j], n[j], get(3, j), get(4, j), get(5, j))
            for i in range(3):
                pa[u, i, j, s, :], qa[u, i, j, s, :] = along[i]
                pairs[i].append(across[i] + (force[i],))
        for i in range(3):
            _, right = beside([x[0] for x in pairs[i]])
            left, _ = beside([x[1] for x in pairs[i]])
            for j in range(4):
                x = left[j] + right[j]
                acc[u, i, j, s, :] = x if i == 0 else x + pairs[i][j][2]

    def combine(u, i, j, r, n, on):
        return (k * on) * (
            acc[u, i, j, pl.ds(r, n), :] + pa[u, i, j, pl.ds(r + 1, n), :] + qa[u, i, j, pl.ds(r - 1, n), :]
        )

    def reader(s):
        def get(i, j):
            return tile[i](s, slice(128 * j, 128 * j + 128))

        return get

    def end_reader(e):
        return lambda i, j: ends[e, i, j, :, :]

    def section(u, to, n, get):
        if u == 0:
            new = [[get(i, j) for j in range(4)] for i in range(3)]
        else:
            new = [[combine(0, i, j, to, n, get(6, j)) for j in range(4)] for i in range(3)]
        fluxes(u, pl.ds(to, n), get, *new)

    def body(u):
        def run(t, _):
            r = pl.multiple_of(t * CHUNK, CHUNK)
            section(u, pl.multiple_of(TOP + r, 8), CHUNK, reader(pl.ds(r, CHUNK)))
            return 0

        return run

    def last(t, _):
        r = pl.multiple_of(t * CHUNK, CHUNK)
        to = pl.ds(r, CHUNK)
        for j in range(4):
            s = slice(128 * j, 128 * j + 128)
            on = tile[6](to, s)
            for i in range(3):
                out[i, to, s] = combine(1, i, j, pl.multiple_of(TOP + r, 8), CHUNK, on)
        return 0

    pa[0, :, :, TOP + R + 8 :, :] = jnp.zeros((3, 4, 8, 128), F32)
    qa[0, :, :, 0:8, :] = jnp.zeros((3, 4, 8, 128), F32)
    for u in range(2):
        section(u, TOP - 8, 8, end_reader(0))
        section(u, TOP + R, 8, end_reader(1))
        lax.fori_loop(0, R // CHUNK, body(u), 0)
    lax.fori_loop(0, R // CHUNK, last, 0)


def slope(h, mom, bed, fric, act, above, below):
    return pl.pallas_call(
        slope_kernel,
        out_shape=jax.ShapeDtypeStruct((3, R, C), F32),
        scratch_shapes=[pltpu.VMEM((2, 7, 4, 8, 128), F32)] + [pltpu.VMEM((2, 3, 4, SROWS, 128), F32)] * 3,
        compiler_params=params(24),
        cost_estimate=pl.CostEstimate(flops=32 * MIB, bytes_accessed=6 * MIB, transcendentals=0),
        name="slope",
    )(h, mom, bed, fric, act, above, below)


def pack_kernel(fields, to_right, to_left, from_left, from_right, own, off, out, payload, strip):
    shape = (8, GROUP)

    def section(x):
        h, m, n = x[:3]
        along, across = local_fluxes(h, m, n)
        force = forcing(h, m, n, *x[3:6])
        new = []
        for i in range(3):
            y = pltpu.roll(along[i][0], GROUP - 1, 1) + pltpu.roll(along[i][1], 1, 1)
            y = y + pltpu.roll(across[i][0], 7, 0) + pltpu.roll(across[i][1], 1, 0)
            y = y if i == 0 else y + force[i]
            new.append((0.075 * x[6]) * y)
        return new

    ends = []
    for e, (before, after) in enumerate(((from_left, to_left), (to_right, from_right))):
        for i in range(7):
            r, s = 4 * (i % 2), slice(GROUP * (i // 2), GROUP * (i // 2) + GROUP)
            strip[e, i, 0:4, :] = before[r : r + 4, s]
            strip[e, i, 4:8, :] = after[r : r + 4, s]
        x = [strip[e, i, :, :] for i in range(7)]
        x = section(x) + x[3:]
        ends.append([pltpu.roll(y, 4, 0) for y in section(x)])
    row, lane = rows(shape), lanes((128, 128))
    for i in range(3):
        first = jnp.where(row < 2, ends[0][i], 0.0)
        last = jnp.where(row >= 6, ends[1][i], 0.0)
        for t in range(R // 128):
            s = slice(128 * t, 128 * t + 128)
            turned = jnp.concatenate([first[:, s], jnp.zeros((112, 128), F32), last[:, s]], axis=0).T
            out[i, s, 0:128] = jnp.where(lane < 2, turned, fields[i, s, 0:128])
            out[i, s, C - 128 : C] = jnp.where(lane >= 126, turned, fields[i, s, C - 128 : C])
        out[i, :, 128 : C - 128] = fields[i, :, 128 : C - 128]

    owner = jnp.broadcast_to(own[...], (DEV, R))
    mine = rows((DEV, R)) == owner
    before = (rows((R, R)) < lanes((R, R))).astype(BF16)
    rank = jnp.dot(mine.astype(BF16), before, preferred_element_type=F32)
    picks = [mine & (rank == float(k_)) for k_ in range(CAP)]
    pickb = [p.astype(BF16) for p in picks]
    for i in range(3):
        parts = split2(out[i])
        for k_ in range(CAP):
            y = pick(pickb[k_], parts)
            for j in range(4):
                payload[pl.ds(12 * k_ + 4 * i + j, DEV, stride=UNITS), :] = y[:, 128 * j : 128 * j + 128]

    lane, dest = lanes((DEV, 128)), rows((DEV, 128))
    tags = jnp.zeros((DEV, 128), F32)
    tag_value = jnp.broadcast_to((off[...] + 1).astype(F32), (DEV, R))
    edge_lane = lanes((R, 128))
    m_first, n_first = out[1, :, 0:128], out[2, :, 0:128]
    m_last, n_last = out[1, :, C - 128 : C], out[2, :, C - 128 : C]
    edges = jnp.where(edge_lane < 3, m_first, 0.0)
    edges = jnp.where((edge_lane >= 3) & (edge_lane < 6), pltpu.roll(n_first, 3, 1), edges)
    edges = jnp.where((edge_lane >= 8) & (edge_lane < 11), pltpu.roll(m_last, 11, 1), edges)
    edges = jnp.where((edge_lane >= 11) & (edge_lane < 14), pltpu.roll(n_last, 14, 1), edges)
    parts = split2(edges)
    to_right = jnp.zeros((DEV, 128), F32)
    to_left = jnp.zeros((DEV, 128), F32)
    for k_ in range(CAP):
        tag = jnp.sum(jnp.where(picks[k_], tag_value, 0.0), axis=1, keepdims=True)
        tags = jnp.where(lane == k_, tag, tags)
        g = pick(pickb[k_], parts)
        at = 8 + 6 * k_
        to_right = jnp.where((lane >= at) & (lane < at + 6), pltpu.roll(g, at - 8, 1) if k_ else g, to_right)
        to_right = jnp.where(lane == 56 + k_, tag, to_right)
        at = 32 + 6 * k_
        to_left = jnp.where((lane >= at) & (lane < at + 6), pltpu.roll(g, at, 1), to_left)
        to_left = jnp.where(lane == 60 + k_, tag, to_left)
    column = lax.rem(dest, NY)
    to_right = jnp.where(column > 0, pltpu.roll(to_right, 1, 0), 0.0)
    to_left = jnp.where(column < NY - 1, pltpu.roll(to_left, DEV - 1, 0), 0.0)
    payload[pl.ds(TAG, DEV, stride=UNITS), :] = tags + to_right + to_left


def pack(fields, to_right, to_left, from_left, from_right, own, off):
    return pl.pallas_call(
        pack_kernel,
        out_shape=[jax.ShapeDtypeStruct((3, R, C), F32), jax.ShapeDtypeStruct((DEV * UNITS, 128), F32)],
        scratch_shapes=[pltpu.VMEM((2, 7, 8, GROUP), F32)],
        compiler_params=params(20),
        name="pack",
    )(fields, to_right, to_left, from_left, from_right, own, off)


def prepare_kernel(d, lm, above, below, from_left, from_right, coef, momentum, first, last, turn):
    gap = jnp.zeros((56, 128), F32)
    for t in range(5):
        s = slice(LAKE + 128 * t, LAKE + 128 * t + 128)
        both = jnp.concatenate([from_left[:, s], gap, from_right[:, s], gap], axis=0)
        turn[128 * t : 128 * t + 128, :] = both.T

    def halo(w, lane, i):
        wide, at = (2, 0) if i == 0 else (3, 3 * i - 1)
        left = pltpu.roll(w, 128 - wide - at, 1)
        right = pltpu.roll(w, 64 - at, 1)
        return jnp.where(lane >= 128 - wide, left, jnp.where(lane < wide, right, 0.0))

    step = 64

    def body(t, _):
        r = pl.multiple_of(t * step, step)
        s = pl.ds(r, step)
        w = turn[s, :]
        lane = lanes((step, 128))
        to = pl.ds(pl.multiple_of(LTOP + r, 8), step)
        for j in range(4):
            coef[j, to, :] = 2.0 * d[s, 128 * j : 128 * j + 128] - 2.0
        coef[4, to, :] = 2.0 * halo(w, lane, 0) - 2.0
        for i in range(2):
            for j in range(4):
                momentum[i, j, s, :] = lm[i, s, 128 * j : 128 * j + 128]
            momentum[i, 4, s, :] = halo(w, lane, i + 1)
        return 0

    lax.fori_loop(0, L // step, body, 0)
    for j in range(5):
        coef[j, 0:LTOP, :] = jnp.zeros((LTOP, 128), F32)
        coef[j, LTOP + L :, :] = jnp.zeros((LTOP, 128), F32)
        if j < 4:
            s = slice(128 * j, 128 * j + 128)
            coef[j, LTOP - 2 : LTOP, :] = 2.0 * above[10:12, s] - 2.0
            coef[j, LTOP + L : LTOP + L + 2, :] = 2.0 * below[10:12, s] - 2.0
    coef[4, LTOP - 8 : LTOP, :] = 2.0 * halo(turn[L + 120 :, :], lanes((8, 128)), 0) - 2.0
    coef[4, LTOP + L : LTOP + L + 8, :] = 2.0 * halo(turn[L : L + 8, :], lanes((8, 128)), 0) - 2.0
    first[...] = momentum[:, :, 0:8, :]
    last[...] = momentum[:, :, L - 8 : L, :]


def prepare(d, lm, above, below, from_left, from_right):
    return pl.pallas_call(
        prepare_kernel,
        out_shape=[jax.ShapeDtypeStruct(x, F32) for x in ((5, LROWS, 128), (2, 5, L, 128), (2, 5, 8, 128), (2, 5, 8, 128))],
        scratch_shapes=[pltpu.VMEM((WIDE, 128), F32)],
        compiler_params=params(16),
        cost_estimate=pl.CostEstimate(flops=4 * MIB, bytes_accessed=8 * MIB, transcendentals=0),
        name="prepare",
    )(d, lm, above, below, from_left, from_right)


def one_hot(hot, tags, first):
    here = (rows((L, DEV)) + 1).astype(F32)
    for group, at in enumerate(first):
        for k in range(CAP):
            col = (group * CAP + k) * DEV
            hot[:, col : col + DEV] = (here == tags[at + k : at + k + 1, :]).astype(BF16)


def gather(recv, term, c):
    for k in range(CAP):
        for j in range(4):
            parts = split2(recv[pl.ds(12 * k + 4 * c + j, DEV, stride=UNITS), :])
            for t in range(2):
                term[t, DEV * k : DEV * k + DEV, 128 * j : 128 * j + 128] = parts[t]


def place_kernel(recv, first_momentum, last_momentum, flow, first, last, hot, term):
    marks = recv[pl.ds(TAG, DEV, stride=UNITS), :]
    one_hot(hot, marks.T, (0, 56, 60))
    own = hot[:, 0 : CAP * DEV]
    side = hot[:, CAP * DEV : 3 * CAP * DEV]
    lane = lanes((DEV, 128))
    for c in range(2):
        gather(recv, term, c + 1)
        sums = pick(own, (term[0], term[1]))
        for j in range(4):
            flow[c, j, :, :] = sums[:, 128 * j : 128 * j + 128]
        left, right = [], []
        for k in range(CAP):
            left.append(jnp.where(lane >= 125, pltpu.roll(marks, 117 - 6 * k - 3 * c, 1), 0.0))
            right.append(jnp.where(lane < 3, pltpu.roll(marks, 96 - 6 * k - 3 * c, 1), 0.0))
        flow[c, 4, :, :] = pick(side, split2(jnp.concatenate(left + right, axis=0)))
    first[...] = first_momentum[...] + flow[:, :, 0:8, :]
    last[...] = last_momentum[...] + flow[:, :, L - 8 : L, :]


def place(recv, first_momentum, last_momentum):
    return pl.pallas_call(
        place_kernel,
        out_shape=[jax.ShapeDtypeStruct((2, 5, n, 128), F32) for n in (L, 8, 8)],
        scratch_shapes=[pltpu.VMEM((L, 3 * CAP * DEV), BF16), pltpu.VMEM((2, CAP * DEV, C), BF16)],
        compiler_params=params(20),
        name="place",
    )(recv, first_momentum, last_momentum)


def raise_kernel(recv, height, new_height, hot, term):
    one_hot(hot, recv[pl.ds(TAG, DEV, stride=UNITS), :].T, (0,))
    gather(recv, term, 0)
    new_height[...] = height[...] + pick(hot[...], (term[0], term[1]))


def raise_lake(recv, height):
    return pl.pallas_call(
        raise_kernel,
        in_specs=[VMEM] * 2,
        out_specs=VMEM,
        out_shape=jax.ShapeDtypeStruct((L, C), F32),
        scratch_shapes=[pltpu.VMEM((L, CAP * DEV), BF16), pltpu.VMEM((2, CAP * DEV, C), BF16)],
        compiler_params=params(8),
        cost_estimate=pl.CostEstimate(flops=600 * MIB, bytes_accessed=6 * MIB, transcendentals=0),
        name="raise_lake",
    )(recv, height)


def krylov_kernel(sides, flow, momentum, above, below, coef, b, w1, w2, sums):
    for x in (b, w1, w2):
        x[:, :, 0 : LTOP - 8, :] = jnp.zeros((2, 5, LTOP - 8, 128), F32)
        x[:, :, LTOP + L + 8 :, :] = jnp.zeros((2, 5, LTOP - 8, 128), F32)
    b[:, :, LTOP - 8 : LTOP, :] = above[...]
    b[:, :, LTOP + L : LTOP + L + 8, :] = below[...]
    up, down, left, right = (sides[i].astype(F32) for i in range(4))
    edge = jnp.where(lanes((1, 128)) < 64, right, left)

    def total_side(t, _):
        r = pl.multiple_of(t * 64, 64)
        for i in range(2):
            for j in range(5):
                b[i, j, pl.ds(pl.multiple_of(LTOP + r, 8), 64), :] = (
                    flow[i, j, pl.ds(r, 64), :] + momentum[i, j, pl.ds(r, 64), :]
                )
        return 0

    lax.fori_loop(0, L // 64, total_side, 0)

    def image(x, i, r, n):
        v = [x[i, j, pl.ds(r, n), :] for j in range(5)]
        west, east = beside(v)
        w = []
        for j in range(5):
            around = (x[i, j, pl.ds(r - 1, n), :] + x[i, j, pl.ds(r + 1, n), :]) + (west[j] + east[j])
            w.append(coef[j, pl.ds(r, n), :] * v[j] - around)
        w[4] = w[4] * edge
        return v, w

    def dot(x, y):
        p = (x[0] * y[0] + x[1] * y[1]) + (x[2] * y[2] + x[3] * y[3])
        p = [p[8 * q : 8 * q + 8, :] for q in range(p.shape[0] // 8)]
        while len(p) > 1:
            p = [a + c for a, c in zip(p[::2], p[1::2])]
        return p[0]

    zero = jnp.zeros((8, 128), F32)

    def sweep(src, dst, kinds):
        for i in range(2):
            for r, scale in ((LTOP - 8, up), (LTOP + L, down)):
                _, w = image(src, i, r, 8)
                for j in range(5):
                    dst[i, j, r : r + 8, :] = w[j] * scale

        def body(t, carry):
            r = pl.multiple_of(LTOP + t * LCHUNK, 8)
            carry = list(carry)
            for q0 in range(0, LCHUNK, LSUB):
                rq = pl.multiple_of(r + q0, 8)
                for i in range(2):
                    v, w = image(src, i, rq, LSUB)
                    for j in range(5):
                        dst[i, j, pl.ds(rq, LSUB), :] = w[j]
                    for q, kind in enumerate(kinds):
                        x, y = {"vv": (v, v), "vw": (v, w), "ww": (w, w)}[kind]
                        at = i * len(kinds) + q
                        carry[at] = carry[at] + dot(x, y)
            return tuple(carry)

        total = lax.fori_loop(0, L // LCHUNK, body, (zero,) * (2 * len(kinds)))
        return total[: len(kinds)], total[len(kinds) :]

    def last_sum(x):
        lane = lanes((LSUB, 128))

        def body(t, carry):
            r = pl.multiple_of(LTOP + t * LCHUNK, 8)
            carry = list(carry)
            for q0 in range(0, LCHUNK, LSUB):
                rq = pl.multiple_of(r + q0, 8)
                for i in range(2):
                    v = [x[i, j, pl.ds(rq, LSUB), :] for j in range(5)]
                    turned = [pltpu.roll(y, 127, 1) for y in v]
                    w = []
                    for j in range(4):
                        pair = jnp.where(lane == 127, turned[j + 1], turned[j]) + x[i, j, pl.ds(rq + 1, LSUB), :]
                        w.append(coef[j, pl.ds(rq, LSUB), :] * v[j] - 2.0 * pair)
                    carry[i] = carry[i] + dot(v, w)
            return tuple(carry)

        total = lax.fori_loop(0, L // LCHUNK, body, (zero,) * 2)
        return total[:1], total[1:]

    s1 = sweep(b, w1, ("vv", "vw", "ww"))
    s2 = sweep(w1, w2, ("vw", "ww"))
    s3 = last_sum(w2)
    flat = []
    for i in range(2):
        flat += list(s1[i]) + list(s2[i]) + list(s3[i]) + [zero, zero]
    stack = jnp.concatenate([jnp.sum(x, axis=0, keepdims=True) for x in flat], axis=0)
    total = jnp.sum(stack, axis=1, keepdims=True)
    line = jnp.sum(jnp.where(lanes((16, 128)) == rows((16, 128)), total, 0.0), axis=0, keepdims=True)
    sums[...] = jnp.broadcast_to(line, (DEV, 128))


def krylov(sides, flow, momentum, above, below, coef):
    return pl.pallas_call(
        krylov_kernel,
        in_specs=[pl.BlockSpec(memory_space=pltpu.SMEM)] + [VMEM] * 5,
        out_specs=[VMEM] * 4,
        out_shape=[jax.ShapeDtypeStruct((2, 5, LROWS, 128), F32)] * 3 + [jax.ShapeDtypeStruct((DEV, 128), F32)],
        compiler_params=params(24),
        name="krylov",
    )(sides, flow, momentum, above, below, coef)


def steps(nu):
    def inner(u, v):
        return sum(u[i] * v[j] * nu[i + j] for i in range(len(u)) for j in range(len(v)))

    def times(u):
        lo = [4.0 * x for x in u] + [None]
        hi = [None] + [0.5 * x for x in u]
        return [a if b is None else b if a is None else a + b for a, b in zip(lo, hi)]

    def add(u, v, scale):
        u = list(u) + [None] * (len(v) - len(u))
        return [x + scale * y if x is not None and y is not None else scale * y if x is None else x
                for x, y in zip(u, list(v) + [None] * (len(u) - len(v)))]

    r = p = [jnp.ones_like(nu[0])]
    rr = nu[0]
    x = None
    for it in range(3):
        image = times(p)
        curve = inner(p, image)
        alpha = jnp.where(curve > 0.0, rr / curve, 0.25)
        alpha = jnp.minimum(jnp.maximum(alpha, 1.0 / 7.0), 1.0 / 1.2)
        x = [alpha * q for q in p] if x is None else add(x, p, alpha)
        if it == 2:
            return x
        r = add(r, image, -alpha)
        new = jnp.maximum(inner(r, r), 0.0)
        beta = jnp.minimum(jnp.where(rr > 0.0, new / rr, 0.0), 6.0)
        p = add(r, p, beta)
        rr = new


def finish_kernel(sums, b, w1, w2, x_hbm, coef, x, sems):
    total = jnp.sum(sums[...], axis=0, keepdims=True)
    lane = lanes((1, 128))
    for c in range(2):
        nu = [
            jnp.sum(jnp.where(lane == 8 * c + k, total, 0.0), axis=1, keepdims=True) for k in range(6)
        ]
        e = steps(nu)
        for k in range(3):
            coef[3 * c + k : 3 * c + k + 1, :] = jnp.broadcast_to(e[k], (1, 128))
    step = 64
    copies = []
    for c in range(2):
        e = [jnp.broadcast_to(coef[3 * c + k : 3 * c + k + 1, :], (step, 128)) for k in range(3)]

        def body(t, _):
            s = pl.ds(pl.multiple_of(t * step, step), step)
            at = pl.ds(pl.multiple_of(LTOP + t * step, 8), step)
            for j in range(4):
                x[c, s, 128 * j : 128 * j + 128] = e[0] * b[c, j, at, :] + e[1] * w1[c, j, at, :] + e[2] * w2[c, j, at, :]
            return 0

        for half in range(2):
            lax.fori_loop(half * L // step // 2, (half + 1) * L // step // 2, body, 0)
            s = pl.ds(half * L // 2, L // 2)
            copies.append(pltpu.make_async_copy(x.at[c, s, :], x_hbm.at[c, s, :], sems.at[2 * c + half]))
            copies[-1].start()
    for copy in copies:
        copy.wait()


def finish(sums, b, w1, w2):
    return pl.pallas_call(
        finish_kernel,
        in_specs=[VMEM] * 4,
        out_specs=HBM,
        out_shape=jax.ShapeDtypeStruct((2, L, C), F32),
        scratch_shapes=[pltpu.VMEM((8, 128), F32), pltpu.VMEM((2, L, C), F32), pltpu.SemaphoreType.DMA((4,))],
        compiler_params=params(16),
        name="finish",
    )(sums, b, w1, w2)


def shift(x, axis, by):
    n = {"gx": NX, "gy": NY}[axis]
    return lax.ppermute(x, axis, [(i, i + by) for i in range(n) if 0 <= i + by < n])


def exchange(x):
    return lax.all_to_all(x, AXES, split_axis=0, concat_axis=0, tiled=True)


def per_device(h, mom, bed, fric, act, owners, offsets, height, lm, d):
    up, dn = edge_rows(h, mom, bed, fric, act, d)
    above, below = shift(dn, "gx", 1), shift(up, "gx", -1)
    to_right, to_left = edge_columns(h, mom, bed, fric, act, d, lm)
    to_right, to_left = corners(to_right, to_left, above, below)
    from_left, from_right = shift(to_right, "gy", 1), shift(to_left, "gy", -1)
    fields = slope(h, mom, bed, fric, act, above, below)
    own, off = owners.reshape(1, R), offsets.reshape(1, R)
    fields, payload = pack(fields, to_right, to_left, from_left, from_right, own, off)
    recv = exchange(payload.reshape(DEV, UNITS, 1, 128)).reshape(DEV * UNITS, 128)
    coef, momentum, first, last = prepare(d, lm, above, below, from_left, from_right)
    flow, first, last = place(recv, first, last)
    new_height = raise_lake(recv, height)
    b_above, b_below = shift(last, "gx", 1), shift(first, "gx", -1)
    i, j = lax.axis_index("gx"), lax.axis_index("gy")
    sides = jnp.stack([i > 0, i < NX - 1, j > 0, j < NY - 1]).astype(jnp.int32)
    flow, new_height = lax.optimization_barrier((flow, new_height))
    b, w1, w2, sums = krylov(sides, flow, momentum, b_above, b_below, coef)
    sums = exchange(sums.reshape(DEV, 1, 128)).reshape(DEV, 128)
    return fields, new_height, finish(sums, b, w1, w2)


def solution(mesh):
    return jax.shard_map(
        per_device,
        mesh=mesh,
        in_specs=(
            P("gx", "gy"),
            P(None, "gx", "gy"),
            P(None, "gx", "gy"),
            P("gx", "gy"),
            P("gx", "gy"),
            P("gx", "gy", None, None),
            P("gx", "gy", None),
            P("gx", "gy"),
            P(None, "gx", "gy"),
            P("gx", "gy"),
        ),
        out_specs=(P(None, "gx", "gy"), P("gx", "gy"), P(None, "gx", "gy")),
        check_vma=False,
    )
```

```python
import functools

import jax
import jax.numpy as jnp
from jax import lax
from jax.experimental import pallas as pl
from jax.experimental.pallas import tpu as pltpu
from jax.sharding import PartitionSpec as P

F32 = jnp.float32
BF16 = jnp.bfloat16
AXES = ("gx", "gy")
NX, NY = 8, 16
DEV = NX * NY
R, C, L = 256, 512, 512
CAP = 4
UNITS = 12 * CAP + 1
TAG = 12 * CAP
WIDE = C + 128
TOP = 16
SROWS = R + 2 * TOP
CHUNK = 32
LTOP = 16
LROWS = L + 2 * LTOP
LCHUNK = 64
LSUB = 16
MIB = 1 << 20


HBM = pl.BlockSpec(memory_space=pltpu.HBM)
SMEM = pl.BlockSpec(memory_space=pltpu.SMEM)
VMEM = pl.BlockSpec(memory_space=pltpu.VMEM)


def params(limit=None, room=0):
    return pltpu.CompilerParams(vmem_limit_bytes=limit * MIB if limit else 60 * 1024 * 1024 - room)


def present(sides):
    return tuple(sides[i].astype(F32) for i in range(4))


def lanes(shape):
    return lax.broadcasted_iota(jnp.int32, shape, len(shape) - 1)


def rows(shape):
    return lax.broadcasted_iota(jnp.int32, shape, len(shape) - 2)


def edge_rows_kernel(h, m, b, f, a, d, up, dn, hs, ms, bs, fs, as_, ds, sems):
    copies = []
    for q, (src, dst) in enumerate(((h, hs), (f, fs), (a, as_), (d, ds))):
        for side, r in enumerate((0, src.shape[0] - 8)):
            copies.append(pltpu.make_async_copy(src.at[pl.ds(r, 8), :], dst.at[side], sems.at[2 * q + side]))
    for q, (src, dst) in enumerate(((m, ms), (b, bs))):
        for side, r in enumerate((0, R - 8)):
            copies.append(pltpu.make_async_copy(src.at[:, pl.ds(r, 8), :], dst.at[side], sems.at[8 + 2 * q + side]))
    for c in copies:
        c.start()
    for c in copies:
        c.wait()
    for side, out, two, one in ((0, up, slice(0, 2), slice(0, 1)), (1, dn, slice(6, 8), slice(7, 8))):
        out[0:2, :] = hs[side, two, :]
        out[2:4, :] = ms[side, 0, two, :]
        out[4:6, :] = ms[side, 1, two, :]
        out[6:7, :] = bs[side, 0, one, :]
        out[7:8, :] = bs[side, 1, one, :]
        out[8:9, :] = fs[side, one, :]
        out[9:10, :] = as_[side, one, :].astype(F32)
        out[10:12, :] = ds[side, two, :]
        out[12:16, :] = jnp.zeros((4, C), F32)


def edge_rows(h, mom, bed, fric, act, d):
    return pl.pallas_call(
        edge_rows_kernel,
        in_specs=[HBM] * 6,
        out_specs=[VMEM] * 2,
        out_shape=[jax.ShapeDtypeStruct((16, C), F32)] * 2,
        scratch_shapes=[
            pltpu.VMEM((2, 8, C), F32),
            pltpu.VMEM((2, 2, 8, C), F32),
            pltpu.VMEM((2, 2, 8, C), F32),
            pltpu.VMEM((2, 8, C), F32),
            pltpu.VMEM((2, 8, C), jnp.int32),
            pltpu.VMEM((2, 8, C), F32),
            pltpu.SemaphoreType.DMA((12,)),
        ],
        compiler_params=params(room=7_000_000),
        name="edge_rows",
    )(h, mom, bed, fric, act, d)


GROUP = R + 128
LAKE = 4 * GROUP
WIDTH = LAKE + L + 128


def put(acc, lane, first, last, base, wide):
    turned = pltpu.roll(last, (base + wide) % 128, 1)
    acc = jnp.where((lane >= base) & (lane < base + wide), turned, acc)
    turned = pltpu.roll(first, 64 + base, 1)
    return jnp.where((lane >= 64 + base) & (lane < 64 + base + wide), turned, acc)


def edge_columns_kernel(h, m, b, f, a, d, l, both, hs, ms, bs, fs, as_, ds, ls, mat, sems):
    copies = []
    pairs = ((h, hs), (m, ms), (b, bs), (f, fs), (a, as_), (d, ds), (l, ls))
    for q, (src, dst) in enumerate(pairs):
        for side, lane in enumerate((0, C - 128)):
            at = (slice(None),) * (len(src.shape) - 1) + (pl.ds(lane, 128),)
            copies.append(pltpu.make_async_copy(src.at[at], dst.at[side], sems.at[2 * q + side]))
    for c in copies:
        c.start()
    slope = (
        lambda e, s: hs[e, s, :],
        lambda e, s: ms[e, 0, s, :],
        lambda e, s: ms[e, 1, s, :],
        lambda e, s: bs[e, 0, s, :],
        lambda e, s: bs[e, 1, s, :],
        lambda e, s: fs[e, s, :],
        lambda e, s: as_[e, s, :].astype(F32),
    )
    lake = (
        (lambda e, s: ds[e, s, :], 32, 2),
        (lambda e, s: ls[e, 0, s, :], 34, 3),
        (lambda e, s: ls[e, 1, s, :], 37, 3),
    )
    step = 64
    mat[L:, :] = jnp.zeros((128, 128), F32)
    for c in copies:
        c.wait()

    def body(slope_too):
        def run(t, _):
            s = pl.ds(pl.multiple_of(t * step, step), step)
            lane = lanes((step, 128))
            acc = jnp.zeros((step, 128), F32)
            if slope_too:
                for i, read in enumerate(slope):
                    acc = put(acc, lane, read(0, s), read(1, s), 4 * i, 4)
            for read, base, wide in lake:
                acc = put(acc, lane, read(0, s), read(1, s), base, wide)
            mat[s, :] = acc
            return 0

        return run

    lax.fori_loop(0, R // step, body(True), 0)
    lax.fori_loop(R // step, L // step, body(False), 0)
    for t in range(5):
        turned = mat[128 * t : 128 * t + 128, :].T
        for e, row in ((0, 0), (1, 64)):
            if t < 3:
                for g in range(4):
                    at = GROUP * g + 128 * t
                    both[e, :, at : at + 128] = turned[row + 8 * g : row + 8 * g + 8, :]
            both[e, :, LAKE + 128 * t : LAKE + 128 * t + 128] = turned[row + 32 : row + 40, :]


def edge_columns(h, mom, bed, fric, act, d, lm):
    return pl.pallas_call(
        edge_columns_kernel,
        in_specs=[HBM] * 7,
        out_specs=VMEM,
        out_shape=jax.ShapeDtypeStruct((2, 8, WIDTH), F32),
        scratch_shapes=[
            pltpu.VMEM((2, R, 128), F32),
            pltpu.VMEM((2, 2, R, 128), F32),
            pltpu.VMEM((2, 2, R, 128), F32),
            pltpu.VMEM((2, R, 128), F32),
            pltpu.VMEM((2, R, 128), jnp.int32),
            pltpu.VMEM((2, L, 128), F32),
            pltpu.VMEM((2, 2, L, 128), F32),
            pltpu.VMEM((WIDE, 128), F32),
            pltpu.SemaphoreType.DMA((14,)),
        ],
        compiler_params=params(room=7_300_000),
        cost_estimate=pl.CostEstimate(flops=8 * MIB, bytes_accessed=6 * MIB, transcendentals=0),
        name="edge_columns",
    )(h, mom, bed, fric, act, d, lm)


def corners_kernel(sides, both, above, below, right, left):
    lane, row = lanes((8, 128)), rows((8, 128))

    def line(x, r, where):
        return jnp.broadcast_to(x[r : r + 1, where], (8, 128))

    def end(x, first_row, second_row, a, b):
        def block(where):
            y = jnp.where(row == first_row, line(x, a, where), 0.0)
            return y if b is None else jnp.where(row == second_row, line(x, b, where), y)

        return block(slice(0, 128)), block(slice(C - 128, C))

    low, high = jnp.zeros((8, 128), F32), jnp.zeros((8, 128), F32)
    for i in range(8):
        if i == 7:
            a, b, base, wide = 10, 11, 32, 2
        elif i < 3:
            a, b, base, wide = 2 * i, 2 * i + 1, 4 * i, 4
        else:
            a, b, base, wide = 3 + i, None, 4 * i, 4
        low = put(low, lane, *end(below, 0, 1, a, b), base, wide)
        if b is None:
            high = put(high, lane, *end(above, 7, None, a, None), base, wide)
        else:
            high = put(high, lane, *end(above, 6, 7, a, b), base, wide)
    up, down, _, _ = present(sides)
    turned = jnp.concatenate([down * low, jnp.zeros((112, 128), F32), up * high], axis=0).T
    for e, out, at in ((0, right, 0), (1, left, 64)):
        out[...] = both[e]
        for g in range(4):
            s = slice(GROUP * g + R, GROUP * g + R + 128)
            out[:, s] = turned[at + 8 * g : at + 8 * g + 8, :]
        out[:, LAKE + L :] = turned[at + 32 : at + 40, :]


def corners(sides, both, above, below):
    return pl.pallas_call(
        corners_kernel,
        in_specs=[SMEM] + [VMEM] * 3,
        out_shape=[jax.ShapeDtypeStruct((8, WIDTH), F32)] * 2,
        compiler_params=params(4),
        name="corners",
    )(sides, both, above, below)


def split2(x):
    hi = x.astype(BF16)
    return hi, (x - hi.astype(F32)).astype(BF16)


def pick(hot, parts):
    return jnp.dot(hot, parts[0], preferred_element_type=F32) + jnp.dot(hot, parts[1], preferred_element_type=F32)


def beside(xs):
    lane, n = lanes(xs[0].shape), len(xs)
    r = [pltpu.roll(x, 1, 1) for x in xs]
    left = [jnp.where(lane == 0, r[j - 1], r[j]) for j in range(n)]
    r = [pltpu.roll(x, 127, 1) for x in xs]
    right = [jnp.where(lane == 127, r[(j + 1) % n], r[j]) for j in range(n)]
    return left, right


def local_fluxes(h, m, n):
    q = 0.25 / 0.075
    inv = 1.0 / jnp.maximum(h, 0.25)
    p = (0.5 * h) * h
    mi = m * inv
    cross = mi * n
    fm = mi * m + p
    gn = (n * inv) * n + p
    h4, m4, n4 = q * h, q * m, q * n
    along = ((h4 - m, h4 + m), (m4 - fm, m4 + fm), (n4 - cross, n4 + cross))
    across = ((h4 - n, h4 + n), (m4 - cross, m4 + cross), (n4 - gn, n4 + gn))
    return along, across


def forcing(h, m, n, b0, b1, fr):
    return None, 2.0 * (h * b0 - fr * m), 2.0 * (h * b1 - fr * n)


def slope_kernel(sides, h_in, mom, bed, fric, act, above, below, out, ends, pa, qa, acc):
    tile = (
        lambda s, lane: h_in[s, lane],
        lambda s, lane: mom[0, s, lane],
        lambda s, lane: mom[1, s, lane],
        lambda s, lane: bed[0, s, lane],
        lambda s, lane: bed[1, s, lane],
        lambda s, lane: fric[s, lane],
        lambda s, lane: act[s, lane].astype(F32),
    )
    up, down, _, _ = present(sides)
    ends[...] = jnp.zeros(ends.shape, F32)
    for i in range(7):
        for j in range(4):
            s = slice(128 * j, 128 * j + 128)
            if i < 3:
                ends[0, i, j, 6:8, :] = up * above[2 * i : 2 * i + 2, s]
                ends[1, i, j, 0:2, :] = down * below[2 * i : 2 * i + 2, s]
            else:
                ends[0, i, j, 7:8, :] = up * above[3 + i : 4 + i, s]
                ends[1, i, j, 0:1, :] = down * below[3 + i : 4 + i, s]
    k = 0.075

    def fluxes(u, s, get, h, m, n):
        pairs = [[], [], []]
        for j in range(4):
            along, across = local_fluxes(h[j], m[j], n[j])
            force = forcing(h[j], m[j], n[j], get(3, j), get(4, j), get(5, j))
            for i in range(3):
                pa[u, i, j, s, :], qa[u, i, j, s, :] = along[i]
                pairs[i].append(across[i] + (force[i],))
        for i in range(3):
            _, right = beside([x[0] for x in pairs[i]])
            left, _ = beside([x[1] for x in pairs[i]])
            for j in range(4):
                x = left[j] + right[j]
                acc[u, i, j, s, :] = x if i == 0 else x + pairs[i][j][2]

    def combine(u, i, j, r, n, on):
        return (k * on) * (
            acc[u, i, j, pl.ds(r, n), :] + pa[u, i, j, pl.ds(r + 1, n), :] + qa[u, i, j, pl.ds(r - 1, n), :]
        )

    def reader(s):
        def get(i, j):
            return tile[i](s, slice(128 * j, 128 * j + 128))

        return get

    def end_reader(e):
        return lambda i, j: ends[e, i, j, :, :]

    def section(u, to, n, get):
        if u == 0:
            new = [[get(i, j) for j in range(4)] for i in range(3)]
        else:
            new = [[combine(0, i, j, to, n, get(6, j)) for j in range(4)] for i in range(3)]
        fluxes(u, pl.ds(to, n), get, *new)

    def body(u):
        def run(t, _):
            r = pl.multiple_of(t * CHUNK, CHUNK)
            section(u, pl.multiple_of(TOP + r, 8), CHUNK, reader(pl.ds(r, CHUNK)))
            return 0

        return run

    def last(t, _):
        r = pl.multiple_of(t * CHUNK, CHUNK)
        to = pl.ds(r, CHUNK)
        for j in range(4):
            s = slice(128 * j, 128 * j + 128)
            on = tile[6](to, s)
            for i in range(3):
                out[i, to, s] = combine(1, i, j, pl.multiple_of(TOP + r, 8), CHUNK, on)
        return 0

    pa[0, :, :, TOP + R + 8 :, :] = jnp.zeros((3, 4, 8, 128), F32)
    qa[0, :, :, 0:8, :] = jnp.zeros((3, 4, 8, 128), F32)
    for u in range(2):
        section(u, TOP - 8, 8, end_reader(0))
        section(u, TOP + R, 8, end_reader(1))
        lax.fori_loop(0, R // CHUNK, body(u), 0)
    lax.fori_loop(0, R // CHUNK, last, 0)


def slope(sides, h, mom, bed, fric, act, above, below):
    return pl.pallas_call(
        slope_kernel,
        in_specs=[SMEM] + [VMEM] * 7,
        out_shape=jax.ShapeDtypeStruct((3, R, C), F32),
        scratch_shapes=[pltpu.VMEM((2, 7, 4, 8, 128), F32)] + [pltpu.VMEM((2, 3, 4, SROWS, 128), F32)] * 3,
        compiler_params=params(24),
        cost_estimate=pl.CostEstimate(flops=32 * MIB, bytes_accessed=6 * MIB, transcendentals=0),
        name="slope",
    )(sides, h, mom, bed, fric, act, above, below)


def pack_kernel(sides, fields, to_right, to_left, from_left, from_right, own, off, fields_out, sent, strip, out, payload, sems):
    shape = (8, GROUP)

    def section(x):
        h, m, n = x[:3]
        along, across = local_fluxes(h, m, n)
        force = forcing(h, m, n, *x[3:6])
        new = []
        for i in range(3):
            y = pltpu.roll(along[i][0], GROUP - 1, 1) + pltpu.roll(along[i][1], 1, 1)
            y = y + pltpu.roll(across[i][0], 7, 0) + pltpu.roll(across[i][1], 1, 0)
            y = y if i == 0 else y + force[i]
            new.append((0.075 * x[6]) * y)
        return new

    ends = []
    _, _, on_left, on_right = present(sides)
    for e, (before, after, a, b) in enumerate(((from_left, to_left, on_left, 1.0), (to_right, from_right, 1.0, on_right))):
        for i in range(7):
            r, s = 4 * (i % 2), slice(GROUP * (i // 2), GROUP * (i // 2) + GROUP)
            strip[e, i, 0:4, :] = a * before[r : r + 4, s]
            strip[e, i, 4:8, :] = b * after[r : r + 4, s]
        x = [strip[e, i, :, :] for i in range(7)]
        x = section(x) + x[3:]
        ends.append([pltpu.roll(y, 4, 0) for y in section(x)])
    row, lane = rows(shape), lanes((128, 128))
    copies = []
    for i in range(3):
        first = jnp.where(row < 2, ends[0][i], 0.0)
        last = jnp.where(row >= 6, ends[1][i], 0.0)
        for t in range(R // 128):
            s = slice(128 * t, 128 * t + 128)
            turned = jnp.concatenate([first[:, s], jnp.zeros((112, 128), F32), last[:, s]], axis=0).T
            out[i, s, 0:128] = jnp.where(lane < 2, turned, fields[i, s, 0:128])
            out[i, s, C - 128 : C] = jnp.where(lane >= 126, turned, fields[i, s, C - 128 : C])
        out[i, :, 128 : C - 128] = fields[i, :, 128 : C - 128]
        for t in range(2):
            s = pl.ds(R // 2 * t, R // 2)
            copies.append(pltpu.make_async_copy(out.at[i, s, :], fields_out.at[i, s, :], sems.at[2 * i + t]))
            copies[-1].start()

    owner = jnp.broadcast_to(own[...], (DEV, R))
    mine = rows((DEV, R)) == owner
    before = (rows((R, R)) < lanes((R, R))).astype(BF16)
    rank = jnp.dot(mine.astype(BF16), before, preferred_element_type=F32)
    picks = [mine & (rank == float(k_)) for k_ in range(CAP)]
    pickb = [p.astype(BF16) for p in picks]
    lane, dest = lanes((DEV, 128)), rows((DEV, 128))
    tags = jnp.zeros((DEV, 128), F32)
    tag_value = jnp.broadcast_to((off[...] + 1).astype(F32), (DEV, R))
    edge_lane = lanes((R, 128))
    m_first, n_first = out[1, :, 0:128], out[2, :, 0:128]
    m_last, n_last = out[1, :, C - 128 : C], out[2, :, C - 128 : C]
    edges = jnp.where(edge_lane < 3, m_first, 0.0)
    edges = jnp.where((edge_lane >= 3) & (edge_lane < 6), pltpu.roll(n_first, 3, 1), edges)
    edges = jnp.where((edge_lane >= 8) & (edge_lane < 11), pltpu.roll(m_last, 11, 1), edges)
    edges = jnp.where((edge_lane >= 11) & (edge_lane < 14), pltpu.roll(n_last, 14, 1), edges)
    parts = split2(edges)
    to_right = jnp.zeros((DEV, 128), F32)
    to_left = jnp.zeros((DEV, 128), F32)
    for k_ in range(CAP):
        tag = jnp.sum(jnp.where(picks[k_], tag_value, 0.0), axis=1, keepdims=True)
        tags = jnp.where(lane == k_, tag, tags)
        g = pick(pickb[k_], parts)
        at = 8 + 6 * k_
        to_right = jnp.where((lane >= at) & (lane < at + 6), pltpu.roll(g, at - 8, 1) if k_ else g, to_right)
        to_right = jnp.where(lane == 56 + k_, tag, to_right)
        at = 32 + 6 * k_
        to_left = jnp.where((lane >= at) & (lane < at + 6), pltpu.roll(g, at, 1), to_left)
        to_left = jnp.where(lane == 60 + k_, tag, to_left)
    column = lax.rem(dest, NY)
    to_right = jnp.where(column > 0, pltpu.roll(to_right, 1, 0), 0.0)
    to_left = jnp.where(column < NY - 1, pltpu.roll(to_left, DEV - 1, 0), 0.0)
    payload[pl.ds(TAG, DEV, stride=UNITS), :] = tags + to_right + to_left

    parts = [split2(out[i]) for i in range(3)]
    groups, piece = 4, 32
    part = DEV // groups
    for e in range(groups):
        some = jnp.concatenate([x[part * e : part * e + part, :] for x in pickb], axis=0)
        for i in range(3):
            y = pick(some, parts[i])
            for k_ in range(CAP):
                for j in range(4):
                    at = part * UNITS * e + 12 * k_ + 4 * i + j
                    payload[pl.ds(at, part, stride=UNITS), :] = y[part * k_ : part * k_ + part, 128 * j : 128 * j + 128]
        for t in range(part * e, part * e + part, piece):
            s = pl.ds(UNITS * t, UNITS * piece)
            copies.append(pltpu.make_async_copy(payload.at[s, :], sent.at[s, :], sems.at[6 + t // piece]))
            copies[-1].start()
    for copy in copies:
        copy.wait()


def pack(sides, fields, to_right, to_left, from_left, from_right, own, off):
    return pl.pallas_call(
        pack_kernel,
        in_specs=[SMEM] + [VMEM] * 7,
        out_specs=[HBM, HBM],
        out_shape=[jax.ShapeDtypeStruct((3, R, C), F32), jax.ShapeDtypeStruct((DEV * UNITS, 128), F32)],
        scratch_shapes=[
            pltpu.VMEM((2, 7, 8, GROUP), F32),
            pltpu.VMEM((3, R, C), F32),
            pltpu.VMEM((DEV * UNITS, 128), F32),
            pltpu.SemaphoreType.DMA((22,)),
        ],
        compiler_params=params(room=12_000_000),
        name="pack",
    )(sides, fields, to_right, to_left, from_left, from_right, own, off)


def prepare_kernel(sides, d, lm, above, below, from_left, from_right, coef, momentum, first, last, turn):
    _, _, on_left, on_right = present(sides)
    gap = jnp.zeros((56, 128), F32)
    for t in range(5):
        s = slice(LAKE + 128 * t, LAKE + 128 * t + 128)
        both = jnp.concatenate([from_left[:, s], gap, from_right[:, s], gap], axis=0)
        turn[128 * t : 128 * t + 128, :] = both.T

    def halo(w, lane, i):
        wide, at = (2, 0) if i == 0 else (3, 3 * i - 1)
        left = pltpu.roll(w, 128 - wide - at, 1)
        right = pltpu.roll(w, 64 - at, 1)
        return jnp.where(lane >= 128 - wide, on_left * left, jnp.where(lane < wide, on_right * right, 0.0))

    step = 64

    def body(t, _):
        r = pl.multiple_of(t * step, step)
        s = pl.ds(r, step)
        w = turn[s, :]
        lane = lanes((step, 128))
        to = pl.ds(pl.multiple_of(LTOP + r, 8), step)
        for j in range(4):
            coef[j, to, :] = 2.0 * d[s, 128 * j : 128 * j + 128] - 2.0
        coef[4, to, :] = 2.0 * halo(w, lane, 0) - 2.0
        for i in range(2):
            for j in range(4):
                momentum[i, j, s, :] = lm[i, s, 128 * j : 128 * j + 128]
            momentum[i, 4, s, :] = halo(w, lane, i + 1)
        return 0

    lax.fori_loop(0, L // step, body, 0)
    for j in range(5):
        coef[j, 0:LTOP, :] = jnp.zeros((LTOP, 128), F32)
        coef[j, LTOP + L :, :] = jnp.zeros((LTOP, 128), F32)
        if j < 4:
            s = slice(128 * j, 128 * j + 128)
            coef[j, LTOP - 2 : LTOP, :] = 2.0 * above[10:12, s] - 2.0
            coef[j, LTOP + L : LTOP + L + 2, :] = 2.0 * below[10:12, s] - 2.0
    coef[4, LTOP - 8 : LTOP, :] = 2.0 * halo(turn[L + 120 :, :], lanes((8, 128)), 0) - 2.0
    coef[4, LTOP + L : LTOP + L + 8, :] = 2.0 * halo(turn[L : L + 8, :], lanes((8, 128)), 0) - 2.0
    first[...] = momentum[:, :, 0:8, :]
    last[...] = momentum[:, :, L - 8 : L, :]


def prepare(sides, d, lm, above, below, from_left, from_right):
    return pl.pallas_call(
        prepare_kernel,
        in_specs=[SMEM] + [VMEM] * 6,
        out_shape=[jax.ShapeDtypeStruct(x, F32) for x in ((5, LROWS, 128), (2, 5, L, 128), (2, 5, 8, 128), (2, 5, 8, 128))],
        scratch_shapes=[pltpu.VMEM((WIDE, 128), F32)],
        compiler_params=params(16),
        cost_estimate=pl.CostEstimate(flops=4 * MIB, bytes_accessed=8 * MIB, transcendentals=0),
        name="prepare",
    )(sides, d, lm, above, below, from_left, from_right)


def one_hot(hot, tags, first):
    here = (rows((L, DEV)) + 1).astype(F32)
    for group, at in enumerate(first):
        for k in range(CAP):
            col = (group * CAP + k) * DEV
            hot[:, col : col + DEV] = (here == tags[at + k : at + k + 1, :]).astype(BF16)


def gather(recv, term, c):
    for k in range(CAP):
        for j in range(4):
            parts = split2(recv[pl.ds(12 * k + 4 * c + j, DEV, stride=UNITS), :])
            for t in range(2):
                term[t, DEV * k : DEV * k + DEV, 128 * j : 128 * j + 128] = parts[t]


def place_kernel(recv, first_momentum, last_momentum, flow, first, last, hot, term):
    marks = recv[pl.ds(TAG, DEV, stride=UNITS), :]
    one_hot(hot, marks.T, (0, 56, 60))
    own = hot[:, 0 : CAP * DEV]
    side = hot[:, CAP * DEV : 3 * CAP * DEV]
    lane = lanes((DEV, 128))
    for c in range(2):
        gather(recv, term, c + 1)
        sums = pick(own, (term[0], term[1]))
        for j in range(4):
            flow[c, j, :, :] = sums[:, 128 * j : 128 * j + 128]
        left, right = [], []
        for k in range(CAP):
            left.append(jnp.where(lane >= 125, pltpu.roll(marks, 117 - 6 * k - 3 * c, 1), 0.0))
            right.append(jnp.where(lane < 3, pltpu.roll(marks, 96 - 6 * k - 3 * c, 1), 0.0))
        flow[c, 4, :, :] = pick(side, split2(jnp.concatenate(left + right, axis=0)))
    first[...] = first_momentum[...] + flow[:, :, 0:8, :]
    last[...] = last_momentum[...] + flow[:, :, L - 8 : L, :]


def place(recv, first_momentum, last_momentum):
    return pl.pallas_call(
        place_kernel,
        out_shape=[jax.ShapeDtypeStruct((2, 5, n, 128), F32) for n in (L, 8, 8)],
        scratch_shapes=[pltpu.VMEM((L, 3 * CAP * DEV), BF16), pltpu.VMEM((2, CAP * DEV, C), BF16)],
        compiler_params=params(20),
        name="place",
    )(recv, first_momentum, last_momentum)


def raise_kernel(recv, height, new_height, hot, term):
    one_hot(hot, recv[pl.ds(TAG, DEV, stride=UNITS), :].T, (0,))
    gather(recv, term, 0)
    new_height[...] = height[...] + pick(hot[...], (term[0], term[1]))


def raise_lake(recv, height):
    return pl.pallas_call(
        raise_kernel,
        in_specs=[VMEM] * 2,
        out_specs=VMEM,
        out_shape=jax.ShapeDtypeStruct((L, C), F32),
        scratch_shapes=[pltpu.VMEM((L, CAP * DEV), BF16), pltpu.VMEM((2, CAP * DEV, C), BF16)],
        compiler_params=params(8),
        cost_estimate=pl.CostEstimate(flops=600 * MIB, bytes_accessed=6 * MIB, transcendentals=0),
        name="raise_lake",
    )(recv, height)


def krylov_kernel(sides, flow, momentum, above, below, coef, b, w1, w2, sums):
    for x in (b, w1, w2):
        x[:, :, 0 : LTOP - 8, :] = jnp.zeros((2, 5, LTOP - 8, 128), F32)
        x[:, :, LTOP + L + 8 :, :] = jnp.zeros((2, 5, LTOP - 8, 128), F32)
    up, down, left, right = present(sides)
    b[:, :, LTOP - 8 : LTOP, :] = up * above[...]
    b[:, :, LTOP + L : LTOP + L + 8, :] = down * below[...]
    edge = jnp.where(lanes((1, 128)) < 64, right, left)

    def total_side(t, _):
        r = pl.multiple_of(t * 64, 64)
        for i in range(2):
            for j in range(5):
                b[i, j, pl.ds(pl.multiple_of(LTOP + r, 8), 64), :] = (
                    flow[i, j, pl.ds(r, 64), :] + momentum[i, j, pl.ds(r, 64), :]
                )
        return 0

    lax.fori_loop(0, L // 64, total_side, 0)

    def image(x, i, r, n):
        v = [x[i, j, pl.ds(r, n), :] for j in range(5)]
        west, east = beside(v)
        w = []
        for j in range(5):
            around = (x[i, j, pl.ds(r - 1, n), :] + x[i, j, pl.ds(r + 1, n), :]) + (west[j] + east[j])
            w.append(coef[j, pl.ds(r, n), :] * v[j] - around)
        w[4] = w[4] * edge
        return v, w

    def dot(x, y):
        p = (x[0] * y[0] + x[1] * y[1]) + (x[2] * y[2] + x[3] * y[3])
        p = [p[8 * q : 8 * q + 8, :] for q in range(p.shape[0] // 8)]
        while len(p) > 1:
            p = [a + c for a, c in zip(p[::2], p[1::2])]
        return p[0]

    zero = jnp.zeros((8, 128), F32)

    def sweep(src, dst, kinds):
        for i in range(2):
            for r, scale in ((LTOP - 8, up), (LTOP + L, down)):
                _, w = image(src, i, r, 8)
                for j in range(5):
                    dst[i, j, r : r + 8, :] = w[j] * scale

        def body(t, carry):
            r = pl.multiple_of(LTOP + t * LCHUNK, 8)
            carry = list(carry)
            for q0 in range(0, LCHUNK, LSUB):
                rq = pl.multiple_of(r + q0, 8)
                for i in range(2):
                    v, w = image(src, i, rq, LSUB)
                    for j in range(5):
                        dst[i, j, pl.ds(rq, LSUB), :] = w[j]
                    for q, kind in enumerate(kinds):
                        x, y = {"vv": (v, v), "vw": (v, w), "ww": (w, w)}[kind]
                        at = i * len(kinds) + q
                        carry[at] = carry[at] + dot(x, y)
            return tuple(carry)

        total = lax.fori_loop(0, L // LCHUNK, body, (zero,) * (2 * len(kinds)))
        return total[: len(kinds)], total[len(kinds) :]

    def last_sum(x):
        lane = lanes((LSUB, 128))

        def body(t, carry):
            r = pl.multiple_of(LTOP + t * LCHUNK, 8)
            carry = list(carry)
            for q0 in range(0, LCHUNK, LSUB):
                rq = pl.multiple_of(r + q0, 8)
                for i in range(2):
                    v = [x[i, j, pl.ds(rq, LSUB), :] for j in range(5)]
                    turned = [pltpu.roll(y, 127, 1) for y in v]
                    w = []
                    for j in range(4):
                        pair = jnp.where(lane == 127, turned[j + 1], turned[j]) + x[i, j, pl.ds(rq + 1, LSUB), :]
                        w.append(coef[j, pl.ds(rq, LSUB), :] * v[j] - 2.0 * pair)
                    carry[i] = carry[i] + dot(v, w)
            return tuple(carry)

        total = lax.fori_loop(0, L // LCHUNK, body, (zero,) * 2)
        return total[:1], total[1:]

    s1 = sweep(b, w1, ("vv", "vw", "ww"))
    s2 = sweep(w1, w2, ("vw", "ww"))
    s3 = last_sum(w2)
    flat = []
    for i in range(2):
        flat += list(s1[i]) + list(s2[i]) + list(s3[i]) + [zero, zero]
    stack = jnp.concatenate([jnp.sum(x, axis=0, keepdims=True) for x in flat], axis=0)
    total = jnp.sum(stack, axis=1, keepdims=True)
    line = jnp.sum(jnp.where(lanes((16, 128)) == rows((16, 128)), total, 0.0), axis=0, keepdims=True)
    sums[...] = jnp.broadcast_to(line, (DEV, 128))


def krylov(sides, flow, momentum, above, below, coef):
    return pl.pallas_call(
        krylov_kernel,
        in_specs=[pl.BlockSpec(memory_space=pltpu.SMEM)] + [VMEM] * 5,
        out_specs=[VMEM] * 4,
        out_shape=[jax.ShapeDtypeStruct((2, 5, LROWS, 128), F32)] * 3 + [jax.ShapeDtypeStruct((DEV, 128), F32)],
        compiler_params=params(24),
        name="krylov",
    )(sides, flow, momentum, above, below, coef)


def steps(nu):
    def inner(u, v):
        return sum(u[i] * v[j] * nu[i + j] for i in range(len(u)) for j in range(len(v)))

    def times(u):
        lo = [4.0 * x for x in u] + [None]
        hi = [None] + [0.5 * x for x in u]
        return [a if b is None else b if a is None else a + b for a, b in zip(lo, hi)]

    def add(u, v, scale):
        u = list(u) + [None] * (len(v) - len(u))
        return [x + scale * y if x is not None and y is not None else scale * y if x is None else x
                for x, y in zip(u, list(v) + [None] * (len(u) - len(v)))]

    r = p = [jnp.ones_like(nu[0])]
    rr = nu[0]
    x = None
    for it in range(3):
        image = times(p)
        curve = inner(p, image)
        alpha = jnp.where(curve > 0.0, rr / curve, 0.25)
        alpha = jnp.minimum(jnp.maximum(alpha, 1.0 / 7.0), 1.0 / 1.2)
        x = [alpha * q for q in p] if x is None else add(x, p, alpha)
        if it == 2:
            return x
        r = add(r, image, -alpha)
        new = jnp.maximum(inner(r, r), 0.0)
        beta = jnp.minimum(jnp.where(rr > 0.0, new / rr, 0.0), 6.0)
        p = add(r, p, beta)
        rr = new


def finish_kernel(sums, b, w1, w2, x_hbm, coef, x, sems):
    total = jnp.sum(sums[...], axis=0, keepdims=True)
    lane = lanes((1, 128))
    for c in range(2):
        nu = [
            jnp.sum(jnp.where(lane == 8 * c + k, total, 0.0), axis=1, keepdims=True) for k in range(6)
        ]
        e = steps(nu)
        for k in range(3):
            coef[3 * c + k : 3 * c + k + 1, :] = jnp.broadcast_to(e[k], (1, 128))
    step = 64
    copies = []
    for c in range(2):
        e = [jnp.broadcast_to(coef[3 * c + k : 3 * c + k + 1, :], (step, 128)) for k in range(3)]

        def body(t, _):
            s = pl.ds(pl.multiple_of(t * step, step), step)
            at = pl.ds(pl.multiple_of(LTOP + t * step, 8), step)
            for j in range(4):
                x[c, s, 128 * j : 128 * j + 128] = e[0] * b[c, j, at, :] + e[1] * w1[c, j, at, :] + e[2] * w2[c, j, at, :]
            return 0

        for half in range(2):
            lax.fori_loop(half * L // step // 2, (half + 1) * L // step // 2, body, 0)
            s = pl.ds(half * L // 2, L // 2)
            copies.append(pltpu.make_async_copy(x.at[c, s, :], x_hbm.at[c, s, :], sems.at[2 * c + half]))
            copies[-1].start()
    for copy in copies:
        copy.wait()


def finish(sums, b, w1, w2):
    return pl.pallas_call(
        finish_kernel,
        in_specs=[VMEM] * 4,
        out_specs=HBM,
        out_shape=jax.ShapeDtypeStruct((2, L, C), F32),
        scratch_shapes=[pltpu.VMEM((8, 128), F32), pltpu.VMEM((2, L, C), F32), pltpu.SemaphoreType.DMA((4,))],
        compiler_params=params(16),
        name="finish",
    )(sums, b, w1, w2)


def shift(x, axis, by):
    n = {"gx": NX, "gy": NY}[axis]
    return lax.ppermute(x, axis, [(i, (i + by) % n) for i in range(n)])


def exchange(x):
    return lax.all_to_all(x, AXES, split_axis=0, concat_axis=0, tiled=True)


def per_device(h, mom, bed, fric, act, owners, offsets, height, lm, d):
    i, j = lax.axis_index("gx"), lax.axis_index("gy")
    sides = jnp.stack([i > 0, i < NX - 1, j > 0, j < NY - 1]).astype(jnp.int32)
    up, dn = edge_rows(h, mom, bed, fric, act, d)
    above, below = shift(dn, "gx", 1), shift(up, "gx", -1)
    columns = edge_columns(h, mom, bed, fric, act, d, lm)
    to_right, to_left = corners(sides, columns, above, below)
    from_left, from_right = shift(to_right, "gy", 1), shift(to_left, "gy", -1)
    fields = slope(sides, h, mom, bed, fric, act, above, below)
    own, off = owners.reshape(1, R), offsets.reshape(1, R)
    fields, payload = pack(sides, fields, to_right, to_left, from_left, from_right, own, off)
    recv = exchange(payload.reshape(DEV, UNITS, 1, 128)).reshape(DEV * UNITS, 128)
    coef, momentum, first, last = prepare(sides, d, lm, above, below, from_left, from_right)
    flow, first, last = place(recv, first, last)
    new_height = raise_lake(recv, height)
    b_above, b_below = shift(last, "gx", 1), shift(first, "gx", -1)
    flow, new_height = lax.optimization_barrier((flow, new_height))
    b, w1, w2, sums = krylov(sides, flow, momentum, b_above, b_below, coef)
    sums = exchange(sums.reshape(DEV, 1, 128)).reshape(DEV, 128)
    return fields, new_height, finish(sums, b, w1, w2)


def solution(mesh):
    return jax.shard_map(
        per_device,
        mesh=mesh,
        in_specs=(
            P("gx", "gy"),
            P(None, "gx", "gy"),
            P(None, "gx", "gy"),
            P("gx", "gy"),
            P("gx", "gy"),
            P("gx", "gy", None, None),
            P("gx", "gy", None),
            P("gx", "gy"),
            P(None, "gx", "gy"),
            P("gx", "gy"),
        ),
        out_specs=(P(None, "gx", "gy"), P("gx", "gy"), P(None, "gx", "gy")),
        check_vma=False,
    )
```

```python
import functools

import jax
import jax.numpy as jnp
from jax import lax
from jax.experimental import pallas as pl
from jax.experimental.pallas import tpu as pltpu
from jax.sharding import PartitionSpec as P

F32 = jnp.float32
BF16 = jnp.bfloat16
AXES = ("gx", "gy")
NX, NY = 8, 16
DEV = NX * NY
R, C, L = 256, 512, 512
CAP = 4
UNITS = 12 * CAP + 1
TAG = 12 * CAP
WIDE = C + 128
TOP = 16
SROWS = R + 2 * TOP
CHUNK = 64
LTOP = 16
LROWS = L + 2 * LTOP
LCHUNK = 256
LSUB = 16
MIB = 1 << 20


HBM = pl.BlockSpec(memory_space=pltpu.HBM)
VMEM = pl.BlockSpec(memory_space=pltpu.VMEM)


def params(limit=None, room=0):
    return pltpu.CompilerParams(vmem_limit_bytes=limit * MIB if limit else 60 * 1024 * 1024 - room)


def present(sides):
    return tuple(sides[i : i + 1, :] for i in range(4))


def lanes(shape):
    return lax.broadcasted_iota(jnp.int32, shape, len(shape) - 1)


def rows(shape):
    return lax.broadcasted_iota(jnp.int32, shape, len(shape) - 2)


def edge_rows_kernel(h, m, b, f, a, d, up, dn, hs, ms, bs, fs, as_, ds, sems):
    copies = []
    for q, (src, dst) in enumerate(((h, hs), (f, fs), (a, as_), (d, ds))):
        for side, r in enumerate((0, src.shape[0] - 8)):
            copies.append(pltpu.make_async_copy(src.at[pl.ds(r, 8), :], dst.at[side], sems.at[2 * q + side]))
    for q, (src, dst) in enumerate(((m, ms), (b, bs))):
        for side, r in enumerate((0, R - 8)):
            copies.append(pltpu.make_async_copy(src.at[:, pl.ds(r, 8), :], dst.at[side], sems.at[8 + 2 * q + side]))
    for c in copies:
        c.start()
    for c in copies:
        c.wait()
    for side, out, two, one in ((0, up, slice(0, 2), slice(0, 1)), (1, dn, slice(6, 8), slice(7, 8))):
        out[0:2, :] = hs[side, two, :]
        out[2:4, :] = ms[side, 0, two, :]
        out[4:6, :] = ms[side, 1, two, :]
        out[6:7, :] = bs[side, 0, one, :]
        out[7:8, :] = bs[side, 1, one, :]
        out[8:9, :] = fs[side, one, :]
        out[9:10, :] = as_[side, one, :].astype(F32)
        out[10:12, :] = ds[side, two, :]
        out[12:16, :] = jnp.zeros((4, C), F32)


def edge_rows(h, mom, bed, fric, act, d):
    return pl.pallas_call(
        edge_rows_kernel,
        in_specs=[HBM] * 6,
        out_specs=[VMEM] * 2,
        out_shape=[jax.ShapeDtypeStruct((16, C), F32)] * 2,
        scratch_shapes=[
            pltpu.VMEM((2, 8, C), F32),
            pltpu.VMEM((2, 2, 8, C), F32),
            pltpu.VMEM((2, 2, 8, C), F32),
            pltpu.VMEM((2, 8, C), F32),
            pltpu.VMEM((2, 8, C), jnp.int32),
            pltpu.VMEM((2, 8, C), F32),
            pltpu.SemaphoreType.DMA((12,)),
        ],
        compiler_params=params(room=7_000_000),
        name="edge_rows",
    )(h, mom, bed, fric, act, d)


GROUP = R + 128
WIDTH = 4 * GROUP
LAKE_WIDTH = L + 128
LAKE_CHANNELS = ((0, 2), (2, 3), (5, 3))


def put(acc, lane, first, last, base, wide):
    turned = pltpu.roll(last, (base + wide) % 128, 1)
    acc = jnp.where((lane >= base) & (lane < base + wide), turned, acc)
    turned = pltpu.roll(first, 64 + base, 1)
    return jnp.where((lane >= 64 + base) & (lane < 64 + base + wide), turned, acc)


def edge_columns_kernel(h, m, b, f, a, both, hs, ms, bs, fs, as_, mat, sems):
    copies = []
    pairs = ((h, hs), (m, ms), (b, bs), (f, fs), (a, as_))
    for q, (src, dst) in enumerate(pairs):
        for side, lane in enumerate((0, C - 128)):
            at = (slice(None),) * (len(src.shape) - 1) + (pl.ds(lane, 128),)
            copies.append(pltpu.make_async_copy(src.at[at], dst.at[side], sems.at[2 * q + side]))
    for c in copies:
        c.start()
    slope = (
        lambda e, s: hs[e, s, :],
        lambda e, s: ms[e, 0, s, :],
        lambda e, s: ms[e, 1, s, :],
        lambda e, s: bs[e, 0, s, :],
        lambda e, s: bs[e, 1, s, :],
        lambda e, s: fs[e, s, :],
        lambda e, s: as_[e, s, :].astype(F32),
    )
    step = 64
    mat[R:, :] = jnp.zeros((128, 128), F32)
    for c in copies:
        c.wait()

    def body(t, _):
        s = pl.ds(pl.multiple_of(t * step, step), step)
        lane = lanes((step, 128))
        acc = jnp.zeros((step, 128), F32)
        for i, read in enumerate(slope):
            acc = put(acc, lane, read(0, s), read(1, s), 4 * i, 4)
        mat[s, :] = acc
        return 0

    lax.fori_loop(0, R // step, body, 0)
    for t in range(3):
        turned = mat[128 * t : 128 * t + 128, :].T
        for e, row in ((0, 0), (1, 64)):
            for g in range(4):
                at = GROUP * g + 128 * t
                both[e, :, at : at + 128] = turned[row + 8 * g : row + 8 * g + 8, :]


def edge_columns(h, mom, bed, fric, act):
    return pl.pallas_call(
        edge_columns_kernel,
        in_specs=[HBM] * 5,
        out_specs=VMEM,
        out_shape=jax.ShapeDtypeStruct((2, 8, WIDTH), F32),
        scratch_shapes=[
            pltpu.VMEM((2, R, 128), F32),
            pltpu.VMEM((2, 2, R, 128), F32),
            pltpu.VMEM((2, 2, R, 128), F32),
            pltpu.VMEM((2, R, 128), F32),
            pltpu.VMEM((2, R, 128), jnp.int32),
            pltpu.VMEM((GROUP, 128), F32),
            pltpu.SemaphoreType.DMA((10,)),
        ],
        compiler_params=params(room=7_300_000),
        cost_estimate=pl.CostEstimate(flops=8 * MIB, bytes_accessed=6 * MIB, transcendentals=0),
        name="edge_columns",
    )(h, mom, bed, fric, act)


def corner_block(x, first_row, second_row, a, b):
    row = rows((8, 128))

    def block(where):
        y = jnp.where(row == first_row, jnp.broadcast_to(x[a : a + 1, where], (8, 128)), 0.0)
        return y if b is None else jnp.where(row == second_row, jnp.broadcast_to(x[b : b + 1, where], (8, 128)), y)

    return block(slice(0, 128)), block(slice(C - 128, C))


def corners_kernel(sides, both, above, below, right, left):
    lane = lanes((8, 128))
    low, high = jnp.zeros((8, 128), F32), jnp.zeros((8, 128), F32)
    for i in range(7):
        if i < 3:
            a, b, base, wide = 2 * i, 2 * i + 1, 4 * i, 4
        else:
            a, b, base, wide = 3 + i, None, 4 * i, 4
        low = put(low, lane, *corner_block(below, 0, 1, a, b), base, wide)
        if b is None:
            high = put(high, lane, *corner_block(above, 7, None, a, None), base, wide)
        else:
            high = put(high, lane, *corner_block(above, 6, 7, a, b), base, wide)
    up, down, _, _ = present(sides)
    turned = jnp.concatenate([down * low, jnp.zeros((112, 128), F32), up * high], axis=0).T
    for e, out, at in ((0, right, 0), (1, left, 64)):
        out[...] = both[e]
        for g in range(4):
            s = slice(GROUP * g + R, GROUP * g + R + 128)
            out[:, s] = turned[at + 8 * g : at + 8 * g + 8, :]


def corners(sides, both, above, below):
    return pl.pallas_call(
        corners_kernel,
        in_specs=[VMEM] * 4,
        out_shape=[jax.ShapeDtypeStruct((8, WIDTH), F32)] * 2,
        compiler_params=params(4),
        name="corners",
    )(sides, both, above, below)


def lake_columns_kernel(sides, d, l, above, below, right, left, mat):
    reads = (lambda s, at: d[s, at], lambda s, at: l[0, s, at], lambda s, at: l[1, s, at])
    ends = (slice(0, 128), slice(C - 128, C))
    step = 128

    def body(t, _):
        s = pl.ds(pl.multiple_of(t * step, step), step)
        lane = lanes((step, 128))
        acc = jnp.zeros((step, 128), F32)
        for read, (base, wide) in zip(reads, LAKE_CHANNELS):
            acc = put(acc, lane, read(s, ends[0]), read(s, ends[1]), base, wide)
        mat[s, :] = acc
        return 0

    lax.fori_loop(0, L // step, body, 0)
    up, down, _, _ = present(sides)
    lane, zero = lanes((8, 128)), jnp.zeros((8, 128), F32)
    mat[L:, :] = jnp.zeros((128, 128), F32)
    mat[L : L + 8, :] = down * put(zero, lane, *corner_block(below, 0, 1, 10, 11), *LAKE_CHANNELS[0])
    mat[L + 120 :, :] = up * put(zero, lane, *corner_block(above, 6, 7, 10, 11), *LAKE_CHANNELS[0])
    for t in range(5):
        turned = mat[128 * t : 128 * t + 128, :].T
        right[:, 128 * t : 128 * t + 128] = turned[0:8, :]
        left[:, 128 * t : 128 * t + 128] = turned[64:72, :]


def lake_columns(sides, d, lm, above, below):
    return pl.pallas_call(
        lake_columns_kernel,
        out_shape=[jax.ShapeDtypeStruct((8, LAKE_WIDTH), F32)] * 2,
        scratch_shapes=[pltpu.VMEM((LAKE_WIDTH, 128), F32)],
        compiler_params=params(16),
        cost_estimate=pl.CostEstimate(flops=4 * MIB, bytes_accessed=4 * MIB, transcendentals=0),
        name="lake_columns",
    )(sides, d, lm, above, below)


def split2(x):
    hi = x.astype(BF16)
    return hi, (x - hi.astype(F32)).astype(BF16)


def pick(hot, parts):
    return jnp.dot(hot, parts[0], preferred_element_type=F32) + jnp.dot(hot, parts[1], preferred_element_type=F32)


def beside(xs):
    lane, n = lanes(xs[0].shape), len(xs)
    r = [pltpu.roll(x, 1, 1) for x in xs]
    left = [jnp.where(lane == 0, r[j - 1], r[j]) for j in range(n)]
    r = [pltpu.roll(x, 127, 1) for x in xs]
    right = [jnp.where(lane == 127, r[(j + 1) % n], r[j]) for j in range(n)]
    return left, right


def local_fluxes(h, m, n):
    q = 0.25 / 0.075
    inv = 1.0 / jnp.maximum(h, 0.25)
    p = (0.5 * h) * h
    mi = m * inv
    cross = mi * n
    fm = mi * m + p
    gn = (n * inv) * n + p
    h4, m4, n4 = q * h, q * m, q * n
    along = ((h4 - m, h4 + m), (m4 - fm, m4 + fm), (n4 - cross, n4 + cross))
    across = ((h4 - n, h4 + n), (m4 - cross, m4 + cross), (n4 - gn, n4 + gn))
    return along, across


def forcing(h, m, n, b0, b1, fr):
    return None, 2.0 * (h * b0 - fr * m), 2.0 * (h * b1 - fr * n)


def slope_kernel(sides, h_in, mom, bed, fric, act, above, below, out, ends, pa, qa, acc):
    tile = (
        lambda s, lane: h_in[s, lane],
        lambda s, lane: mom[0, s, lane],
        lambda s, lane: mom[1, s, lane],
        lambda s, lane: bed[0, s, lane],
        lambda s, lane: bed[1, s, lane],
        lambda s, lane: fric[s, lane],
        lambda s, lane: act[s, lane].astype(F32),
    )
    up, down, _, _ = present(sides)
    ends[...] = jnp.zeros(ends.shape, F32)
    for i in range(7):
        for j in range(4):
            s = slice(128 * j, 128 * j + 128)
            if i < 3:
                ends[0, i, j, 6:8, :] = up * above[2 * i : 2 * i + 2, s]
                ends[1, i, j, 0:2, :] = down * below[2 * i : 2 * i + 2, s]
            else:
                ends[0, i, j, 7:8, :] = up * above[3 + i : 4 + i, s]
                ends[1, i, j, 0:1, :] = down * below[3 + i : 4 + i, s]
    k = 0.075

    def fluxes(u, s, get, h, m, n):
        pairs = [[], [], []]
        for j in range(4):
            along, across = local_fluxes(h[j], m[j], n[j])
            force = forcing(h[j], m[j], n[j], get(3, j), get(4, j), get(5, j))
            for i in range(3):
                pa[u, i, j, s, :], qa[u, i, j, s, :] = along[i]
                pairs[i].append(across[i] + (force[i],))
        for i in range(3):
            _, right = beside([x[0] for x in pairs[i]])
            left, _ = beside([x[1] for x in pairs[i]])
            for j in range(4):
                x = left[j] + right[j]
                acc[u, i, j, s, :] = x if i == 0 else x + pairs[i][j][2]

    def combine(u, i, j, r, n, on):
        return (k * on) * (
            acc[u, i, j, pl.ds(r, n), :] + pa[u, i, j, pl.ds(r + 1, n), :] + qa[u, i, j, pl.ds(r - 1, n), :]
        )

    def reader(s):
        def get(i, j):
            return tile[i](s, slice(128 * j, 128 * j + 128))

        return get

    def end_reader(e):
        return lambda i, j: ends[e, i, j, :, :]

    def section(u, to, n, get):
        if u == 0:
            new = [[get(i, j) for j in range(4)] for i in range(3)]
        else:
            new = [[combine(0, i, j, to, n, get(6, j)) for j in range(4)] for i in range(3)]
        fluxes(u, pl.ds(to, n), get, *new)

    def body(u):
        def run(t, _):
            r = pl.multiple_of(t * CHUNK, CHUNK)
            section(u, pl.multiple_of(TOP + r, 8), CHUNK, reader(pl.ds(r, CHUNK)))
            return 0

        return run

    def last(t, _):
        r = pl.multiple_of(t * CHUNK, CHUNK)
        to = pl.ds(r, CHUNK)
        for j in range(4):
            s = slice(128 * j, 128 * j + 128)
            on = tile[6](to, s)
            for i in range(3):
                out[i, to, s] = combine(1, i, j, pl.multiple_of(TOP + r, 8), CHUNK, on)
        return 0

    pa[0, :, :, TOP + R + 8 :, :] = jnp.zeros((3, 4, 8, 128), F32)
    qa[0, :, :, 0:8, :] = jnp.zeros((3, 4, 8, 128), F32)
    for u in range(2):
        section(u, TOP - 8, 8, end_reader(0))
        section(u, TOP + R, 8, end_reader(1))
        lax.fori_loop(0, R // CHUNK, body(u), 0)
    lax.fori_loop(0, R // CHUNK, last, 0)


def slope(sides, h, mom, bed, fric, act, above, below):
    return pl.pallas_call(
        slope_kernel,
        in_specs=[VMEM] * 8,
        out_shape=jax.ShapeDtypeStruct((3, R, C), F32),
        scratch_shapes=[pltpu.VMEM((2, 7, 4, 8, 128), F32)] + [pltpu.VMEM((2, 3, 4, SROWS, 128), F32)] * 3,
        compiler_params=params(24),
        cost_estimate=pl.CostEstimate(flops=32 * MIB, bytes_accessed=6 * MIB, transcendentals=0),
        name="slope",
    )(sides, h, mom, bed, fric, act, above, below)


def pack_kernel(sides, fields, to_right, to_left, from_left, from_right, own, off, fields_out, sent, strip, out, payload, sems):
    shape = (8, GROUP)

    def section(x):
        h, m, n = x[:3]
        along, across = local_fluxes(h, m, n)
        force = forcing(h, m, n, *x[3:6])
        new = []
        for i in range(3):
            y = pltpu.roll(along[i][0], GROUP - 1, 1) + pltpu.roll(along[i][1], 1, 1)
            y = y + pltpu.roll(across[i][0], 7, 0) + pltpu.roll(across[i][1], 1, 0)
            y = y if i == 0 else y + force[i]
            new.append((0.075 * x[6]) * y)
        return new

    ends = []
    _, _, on_left, on_right = present(sides)
    for e, (before, after, a, b) in enumerate(((from_left, to_left, on_left, None), (to_right, from_right, None, on_right))):
        a, b = (1.0 if x is None else jnp.concatenate([x] * (GROUP // 128), axis=1) for x in (a, b))
        for i in range(7):
            r, s = 4 * (i % 2), slice(GROUP * (i // 2), GROUP * (i // 2) + GROUP)
            strip[e, i, 0:4, :] = a * before[r : r + 4, s]
            strip[e, i, 4:8, :] = b * after[r : r + 4, s]
        x = [strip[e, i, :, :] for i in range(7)]
        x = section(x) + x[3:]
        ends.append([pltpu.roll(y, 4, 0) for y in section(x)])
    row, lane = rows(shape), lanes((128, 128))
    copies = []
    for i in range(3):
        first = jnp.where(row < 2, ends[0][i], 0.0)
        last = jnp.where(row >= 6, ends[1][i], 0.0)
        for t in range(R // 128):
            s = slice(128 * t, 128 * t + 128)
            turned = jnp.concatenate([first[:, s], jnp.zeros((112, 128), F32), last[:, s]], axis=0).T
            out[i, s, 0:128] = jnp.where(lane < 2, turned, fields[i, s, 0:128])
            out[i, s, C - 128 : C] = jnp.where(lane >= 126, turned, fields[i, s, C - 128 : C])
        out[i, :, 128 : C - 128] = fields[i, :, 128 : C - 128]
        for t in range(2):
            s = pl.ds(R // 2 * t, R // 2)
            copies.append(pltpu.make_async_copy(out.at[i, s, :], fields_out.at[i, s, :], sems.at[2 * i + t]))
            copies[-1].start()

    owner = jnp.broadcast_to(own[...], (DEV, R))
    mine = rows((DEV, R)) == owner
    before = (rows((R, R)) < lanes((R, R))).astype(BF16)
    rank = jnp.dot(mine.astype(BF16), before, preferred_element_type=F32)
    picks = [mine & (rank == float(k_)) for k_ in range(CAP)]
    pickb = [p.astype(BF16) for p in picks]
    lane, dest = lanes((DEV, 128)), rows((DEV, 128))
    tags = jnp.zeros((DEV, 128), F32)
    tag_value = jnp.broadcast_to((off[...] + 1).astype(F32), (DEV, R))
    edge_lane = lanes((R, 128))
    m_first, n_first = out[1, :, 0:128], out[2, :, 0:128]
    m_last, n_last = out[1, :, C - 128 : C], out[2, :, C - 128 : C]
    edges = jnp.where(edge_lane < 3, m_first, 0.0)
    edges = jnp.where((edge_lane >= 3) & (edge_lane < 6), pltpu.roll(n_first, 3, 1), edges)
    edges = jnp.where((edge_lane >= 8) & (edge_lane < 11), pltpu.roll(m_last, 11, 1), edges)
    edges = jnp.where((edge_lane >= 11) & (edge_lane < 14), pltpu.roll(n_last, 14, 1), edges)
    parts = split2(edges)
    to_right = jnp.zeros((DEV, 128), F32)
    to_left = jnp.zeros((DEV, 128), F32)
    for k_ in range(CAP):
        tag = jnp.sum(jnp.where(picks[k_], tag_value, 0.0), axis=1, keepdims=True)
        tags = jnp.where(lane == k_, tag, tags)
        g = pick(pickb[k_], parts)
        at = 8 + 6 * k_
        to_right = jnp.where((lane >= at) & (lane < at + 6), pltpu.roll(g, at - 8, 1) if k_ else g, to_right)
        to_right = jnp.where(lane == 56 + k_, tag, to_right)
        at = 32 + 6 * k_
        to_left = jnp.where((lane >= at) & (lane < at + 6), pltpu.roll(g, at, 1), to_left)
        to_left = jnp.where(lane == 60 + k_, tag, to_left)
    column = lax.rem(dest, NY)
    to_right = jnp.where(column > 0, pltpu.roll(to_right, 1, 0), 0.0)
    to_left = jnp.where(column < NY - 1, pltpu.roll(to_left, DEV - 1, 0), 0.0)
    payload[pl.ds(TAG, DEV, stride=UNITS), :] = tags + to_right + to_left

    parts = [split2(out[i]) for i in range(3)]
    groups, piece = 4, 32
    part = DEV // groups
    for e in range(groups):
        some = jnp.concatenate([x[part * e : part * e + part, :] for x in pickb], axis=0)
        for i in range(3):
            y = pick(some, parts[i])
            for k_ in range(CAP):
                for j in range(4):
                    at = part * UNITS * e + 12 * k_ + 4 * i + j
                    payload[pl.ds(at, part, stride=UNITS), :] = y[part * k_ : part * k_ + part, 128 * j : 128 * j + 128]
        for t in range(part * e, part * e + part, piece):
            s = pl.ds(UNITS * t, UNITS * piece)
            copies.append(pltpu.make_async_copy(payload.at[s, :], sent.at[s, :], sems.at[6 + t // piece]))
            copies[-1].start()
    for copy in copies:
        copy.wait()


def pack(sides, fields, to_right, to_left, from_left, from_right, own, off):
    return pl.pallas_call(
        pack_kernel,
        in_specs=[VMEM] * 8,
        out_specs=[HBM, HBM],
        out_shape=[jax.ShapeDtypeStruct((3, R, C), F32), jax.ShapeDtypeStruct((DEV * UNITS, 128), F32)],
        scratch_shapes=[
            pltpu.VMEM((2, 7, 8, GROUP), F32),
            pltpu.VMEM((3, R, C), F32),
            pltpu.VMEM((DEV * UNITS, 128), F32),
            pltpu.SemaphoreType.DMA((22,)),
        ],
        compiler_params=params(room=10_000_000),
        name="pack",
    )(sides, fields, to_right, to_left, from_left, from_right, own, off)


def prepare_kernel(d, lm, above, below, coef, momentum, first, last):
    step = 64

    def body(t, _):
        r = pl.multiple_of(t * step, step)
        s = pl.ds(r, step)
        to = pl.ds(pl.multiple_of(LTOP + r, 8), step)
        for j in range(4):
            at = slice(128 * j, 128 * j + 128)
            coef[j, to, :] = 2.0 * d[s, at] - 2.0
            for i in range(2):
                momentum[i, j, s, :] = lm[i, s, at]
        return 0

    lax.fori_loop(0, L // step, body, 0)
    for j in range(4):
        coef[j, 0:LTOP, :] = jnp.zeros((LTOP, 128), F32)
        coef[j, LTOP + L :, :] = jnp.zeros((LTOP, 128), F32)
        s = slice(128 * j, 128 * j + 128)
        coef[j, LTOP - 2 : LTOP, :] = 2.0 * above[10:12, s] - 2.0
        coef[j, LTOP + L : LTOP + L + 2, :] = 2.0 * below[10:12, s] - 2.0
    first[...] = momentum[:, :, 0:8, :]
    last[...] = momentum[:, :, L - 8 : L, :]


def prepare(d, lm, above, below):
    return pl.pallas_call(
        prepare_kernel,
        out_shape=[jax.ShapeDtypeStruct(x, F32) for x in ((4, LROWS, 128), (2, 4, L, 128), (2, 4, 8, 128), (2, 4, 8, 128))],
        compiler_params=params(16),
        cost_estimate=pl.CostEstimate(flops=4 * MIB, bytes_accessed=8 * MIB, transcendentals=0),
        name="prepare",
    )(d, lm, above, below)


def lake_turn(from_left, from_right, t):
    gap, s = jnp.zeros((56, 128), F32), slice(128 * t, 128 * t + 128)
    return jnp.concatenate([from_left[:, s], gap, from_right[:, s], gap], axis=0).T


def lake_halo(sides, w, i):
    _, _, on_left, on_right = present(sides)
    at, wide = LAKE_CHANNELS[i]
    lane = lanes(w.shape)
    left = pltpu.roll(w, 128 - wide - at, 1)
    right = pltpu.roll(w, 64 - at, 1)
    return jnp.where(lane >= 128 - wide, on_left * left, jnp.where(lane < wide, on_right * right, 0.0))


def one_hot(hot, tags, first):
    here = (rows((L, DEV)) + 1).astype(F32)
    for group, at in enumerate(first):
        for k in range(CAP):
            col = (group * CAP + k) * DEV
            hot[:, col : col + DEV] = (here == tags[at + k : at + k + 1, :]).astype(BF16)


def gather(recv, term, c):
    for k in range(CAP):
        for j in range(4):
            parts = split2(recv[pl.ds(12 * k + 4 * c + j, DEV, stride=UNITS), :])
            for t in range(2):
                term[t, DEV * k : DEV * k + DEV, 128 * j : 128 * j + 128] = parts[t]


def place_kernel(sides, recv, first_momentum, last_momentum, from_left, from_right, flow, first, last, hot, term):
    marks = recv[pl.ds(TAG, DEV, stride=UNITS), :]
    one_hot(hot, marks.T, (0, 56, 60))
    own = hot[:, 0 : CAP * DEV]
    side = hot[:, CAP * DEV : 3 * CAP * DEV]
    lane = lanes((DEV, 128))
    for c in range(2):
        gather(recv, term, c + 1)
        sums = pick(own, (term[0], term[1]))
        for j in range(4):
            flow[c, j, :, :] = sums[:, 128 * j : 128 * j + 128]
        left, right = [], []
        for k in range(CAP):
            left.append(jnp.where(lane >= 125, pltpu.roll(marks, 117 - 6 * k - 3 * c, 1), 0.0))
            right.append(jnp.where(lane < 3, pltpu.roll(marks, 96 - 6 * k - 3 * c, 1), 0.0))
        flow[c, 4, :, :] = pick(side, split2(jnp.concatenate(left + right, axis=0)))
    first[:, 0:4, :, :] = first_momentum[...] + flow[:, 0:4, 0:8, :]
    last[:, 0:4, :, :] = last_momentum[...] + flow[:, 0:4, L - 8 : L, :]
    top = lake_turn(from_left, from_right, 0)[0:8, :]
    bottom = lake_turn(from_left, from_right, L // 128 - 1)[120:128, :]
    for c in range(2):
        first[c, 4, :, :] = lake_halo(sides, top, c + 1) + flow[c, 4, 0:8, :]
        last[c, 4, :, :] = lake_halo(sides, bottom, c + 1) + flow[c, 4, L - 8 : L, :]


def place(sides, recv, first_momentum, last_momentum, from_left, from_right):
    return pl.pallas_call(
        place_kernel,
        out_shape=[jax.ShapeDtypeStruct((2, 5, n, 128), F32) for n in (L, 8, 8)],
        scratch_shapes=[pltpu.VMEM((L, 3 * CAP * DEV), BF16), pltpu.VMEM((2, CAP * DEV, C), BF16)],
        compiler_params=params(20),
        name="place",
    )(sides, recv, first_momentum, last_momentum, from_left, from_right)


def raise_kernel(recv, height, new_height, hot, term):
    one_hot(hot, recv[pl.ds(TAG, DEV, stride=UNITS), :].T, (0,))
    gather(recv, term, 0)
    new_height[...] = height[...] + pick(hot[...], (term[0], term[1]))


def raise_lake(recv, height):
    return pl.pallas_call(
        raise_kernel,
        in_specs=[VMEM] * 2,
        out_specs=VMEM,
        out_shape=jax.ShapeDtypeStruct((L, C), F32),
        scratch_shapes=[pltpu.VMEM((L, CAP * DEV), BF16), pltpu.VMEM((2, CAP * DEV, C), BF16)],
        compiler_params=params(8),
        cost_estimate=pl.CostEstimate(flops=600 * MIB, bytes_accessed=6 * MIB, transcendentals=0),
        name="raise_lake",
    )(recv, height)


def krylov_kernel(sides, flow, momentum, above, below, coef, from_left, from_right, b, w1, w2, sums, turn, side_coef):
    for x in (b, w1, w2):
        x[:, :, 0 : LTOP - 8, :] = jnp.zeros((2, 5, LTOP - 8, 128), F32)
        x[:, :, LTOP + L + 8 :, :] = jnp.zeros((2, 5, LTOP - 8, 128), F32)
    up, down, left, right = present(sides)
    b[:, :, LTOP - 8 : LTOP, :] = up * above[...]
    b[:, :, LTOP + L : LTOP + L + 8, :] = down * below[...]
    edge = jnp.where(lanes((1, 128)) < 64, right, left)

    def total_side(t, _):
        r = pl.multiple_of(t * 64, 64)
        s, to = pl.ds(r, 64), pl.ds(pl.multiple_of(LTOP + r, 8), 64)
        w = turn[s, :]
        side_coef[to, :] = 2.0 * lake_halo(sides, w, 0) - 2.0
        for i in range(2):
            for j in range(4):
                b[i, j, to, :] = flow[i, j, s, :] + momentum[i, j, s, :]
            b[i, 4, to, :] = flow[i, 4, s, :] + lake_halo(sides, w, i + 1)
        return 0

    for t in range(5):
        turn[128 * t : 128 * t + 128, :] = lake_turn(from_left, from_right, t)
    side_coef[LTOP - 8 : LTOP, :] = 2.0 * lake_halo(sides, turn[L + 120 :, :], 0) - 2.0
    side_coef[LTOP + L : LTOP + L + 8, :] = 2.0 * lake_halo(sides, turn[L : L + 8, :], 0) - 2.0
    lax.fori_loop(0, L // 64, total_side, 0)

    def image(x, i, r, n):
        v = [x[i, j, pl.ds(r, n), :] for j in range(5)]
        west, east = beside(v)
        w = []
        for j in range(5):
            around = (x[i, j, pl.ds(r - 1, n), :] + x[i, j, pl.ds(r + 1, n), :]) + (west[j] + east[j])
            diagonal = coef[j, pl.ds(r, n), :] if j < 4 else side_coef[pl.ds(r, n), :]
            w.append(diagonal * v[j] - around)
        w[4] = w[4] * edge
        return v, w

    def dot(x, y):
        p = (x[0] * y[0] + x[1] * y[1]) + (x[2] * y[2] + x[3] * y[3])
        p = [p[8 * q : 8 * q + 8, :] for q in range(p.shape[0] // 8)]
        while len(p) > 1:
            p = [a + c for a, c in zip(p[::2], p[1::2])]
        return p[0]

    zero = jnp.zeros((8, 128), F32)

    def sweep(src, dst, kinds):
        for i in range(2):
            for r, scale in ((LTOP - 8, up), (LTOP + L, down)):
                _, w = image(src, i, r, 8)
                for j in range(5):
                    dst[i, j, r : r + 8, :] = w[j] * scale

        def body(t, carry):
            r = pl.multiple_of(LTOP + t * LCHUNK, 8)
            carry = list(carry)
            for q0 in range(0, LCHUNK, LSUB):
                rq = pl.multiple_of(r + q0, 8)
                for i in range(2):
                    v, w = image(src, i, rq, LSUB)
                    for j in range(5):
                        dst[i, j, pl.ds(rq, LSUB), :] = w[j]
                    for q, kind in enumerate(kinds):
                        x, y = {"vv": (v, v), "vw": (v, w), "ww": (w, w)}[kind]
                        at = i * len(kinds) + q
                        carry[at] = carry[at] + dot(x, y)
            return tuple(carry)

        total = lax.fori_loop(0, L // LCHUNK, body, (zero,) * (2 * len(kinds)))
        return total[: len(kinds)], total[len(kinds) :]

    def last_sum(x):
        lane = lanes((LSUB, 128))

        def body(t, carry):
            r = pl.multiple_of(LTOP + t * LCHUNK, 8)
            carry = list(carry)
            for q0 in range(0, LCHUNK, LSUB):
                rq = pl.multiple_of(r + q0, 8)
                for i in range(2):
                    v = [x[i, j, pl.ds(rq, LSUB), :] for j in range(5)]
                    turned = [pltpu.roll(y, 127, 1) for y in v]
                    w = []
                    for j in range(4):
                        pair = jnp.where(lane == 127, turned[j + 1], turned[j]) + x[i, j, pl.ds(rq + 1, LSUB), :]
                        w.append(coef[j, pl.ds(rq, LSUB), :] * v[j] - 2.0 * pair)
                    carry[i] = carry[i] + dot(v, w)
            return tuple(carry)

        total = lax.fori_loop(0, L // LCHUNK, body, (zero,) * 2)
        return total[:1], total[1:]

    s1 = sweep(b, w1, ("vv", "vw", "ww"))
    s2 = sweep(w1, w2, ("vw", "ww"))
    s3 = last_sum(w2)
    flat = []
    for i in range(2):
        flat += list(s1[i]) + list(s2[i]) + list(s3[i]) + [zero, zero]
    stack = jnp.concatenate([jnp.sum(x, axis=0, keepdims=True) for x in flat], axis=0)
    total = jnp.sum(stack, axis=1, keepdims=True)
    line = jnp.sum(jnp.where(lanes((16, 128)) == rows((16, 128)), total, 0.0), axis=0, keepdims=True)
    sums[...] = jnp.broadcast_to(line, (DEV, 128))


def krylov(sides, flow, momentum, above, below, coef, from_left, from_right):
    return pl.pallas_call(
        krylov_kernel,
        in_specs=[VMEM] * 8,
        out_specs=[VMEM] * 4,
        out_shape=[jax.ShapeDtypeStruct((2, 5, LROWS, 128), F32)] * 3 + [jax.ShapeDtypeStruct((DEV, 128), F32)],
        scratch_shapes=[pltpu.VMEM((LAKE_WIDTH, 128), F32), pltpu.VMEM((LROWS, 128), F32)],
        compiler_params=params(24),
        name="krylov",
    )(sides, flow, momentum, above, below, coef, from_left, from_right)


def steps(nu):
    def inner(u, v):
        return sum(u[i] * v[j] * nu[i + j] for i in range(len(u)) for j in range(len(v)))

    def times(u):
        lo = [4.0 * x for x in u] + [None]
        hi = [None] + [0.5 * x for x in u]
        return [a if b is None else b if a is None else a + b for a, b in zip(lo, hi)]

    def add(u, v, scale):
        u = list(u) + [None] * (len(v) - len(u))
        return [x + scale * y if x is not None and y is not None else scale * y if x is None else x
                for x, y in zip(u, list(v) + [None] * (len(u) - len(v)))]

    r = p = [jnp.ones_like(nu[0])]
    rr = nu[0]
    x = None
    for it in range(3):
        image = times(p)
        curve = inner(p, image)
        alpha = jnp.where(curve > 0.0, rr / curve, 0.25)
        alpha = jnp.minimum(jnp.maximum(alpha, 1.0 / 7.0), 1.0 / 1.2)
        x = [alpha * q for q in p] if x is None else add(x, p, alpha)
        if it == 2:
            return x
        r = add(r, image, -alpha)
        new = jnp.maximum(inner(r, r), 0.0)
        beta = jnp.minimum(jnp.where(rr > 0.0, new / rr, 0.0), 6.0)
        p = add(r, p, beta)
        rr = new


def finish_kernel(sums, b, w1, w2, x_hbm, coef, x, sems):
    total = jnp.sum(sums[...], axis=0, keepdims=True)
    lane = lanes((1, 128))
    for c in range(2):
        nu = [
            jnp.sum(jnp.where(lane == 8 * c + k, total, 0.0), axis=1, keepdims=True) for k in range(6)
        ]
        e = steps(nu)
        for k in range(3):
            coef[3 * c + k : 3 * c + k + 1, :] = jnp.broadcast_to(e[k], (1, 128))
    step = 64
    copies = []
    for c in range(2):
        e = [jnp.broadcast_to(coef[3 * c + k : 3 * c + k + 1, :], (step, 128)) for k in range(3)]

        def body(t, _):
            s = pl.ds(pl.multiple_of(t * step, step), step)
            at = pl.ds(pl.multiple_of(LTOP + t * step, 8), step)
            for j in range(4):
                x[c, s, 128 * j : 128 * j + 128] = e[0] * b[c, j, at, :] + e[1] * w1[c, j, at, :] + e[2] * w2[c, j, at, :]
            return 0

        for half in range(2):
            lax.fori_loop(half * L // step // 2, (half + 1) * L // step // 2, body, 0)
            s = pl.ds(half * L // 2, L // 2)
            copies.append(pltpu.make_async_copy(x.at[c, s, :], x_hbm.at[c, s, :], sems.at[2 * c + half]))
            copies[-1].start()
    for copy in copies:
        copy.wait()


def finish(sums, b, w1, w2):
    return pl.pallas_call(
        finish_kernel,
        in_specs=[VMEM] * 4,
        out_specs=HBM,
        out_shape=jax.ShapeDtypeStruct((2, L, C), F32),
        scratch_shapes=[pltpu.VMEM((8, 128), F32), pltpu.VMEM((2, L, C), F32), pltpu.SemaphoreType.DMA((4,))],
        compiler_params=params(16),
        name="finish",
    )(sums, b, w1, w2)


def shift(x, axis, by):
    n = {"gx": NX, "gy": NY}[axis]
    return lax.ppermute(x, axis, [(i, (i + by) % n) for i in range(n)])


def exchange(x):
    return lax.all_to_all(x, AXES, split_axis=0, concat_axis=0, tiled=True)


def per_device(h, mom, bed, fric, act, owners, offsets, height, lm, d):
    i, j = lax.axis_index("gx"), lax.axis_index("gy")
    row = rows((8, 128))
    inside = ((row == 0) & (i > 0)) | ((row == 1) & (i < NX - 1)) | ((row == 2) & (j > 0)) | ((row == 3) & (j < NY - 1))
    sides = inside.astype(F32)
    up, dn = edge_rows(h, mom, bed, fric, act, d)
    above, below = shift(dn, "gx", 1), shift(up, "gx", -1)
    columns = edge_columns(h, mom, bed, fric, act)
    to_right, to_left = corners(sides, columns, above, below)
    from_left, from_right = shift(to_right, "gy", 1), shift(to_left, "gy", -1)
    fields = slope(sides, h, mom, bed, fric, act, above, below)
    own, off = owners.reshape(1, R), offsets.reshape(1, R)
    fields, payload = pack(sides, fields, to_right, to_left, from_left, from_right, own, off)
    payload, d, lm = lax.optimization_barrier((payload, d, lm))
    recv = exchange(payload.reshape(DEV, UNITS, 1, 128)).reshape(DEV * UNITS, 128)
    to_right, to_left = lake_columns(sides, d, lm, above, below)
    from_left, from_right = shift(to_right, "gy", 1), shift(to_left, "gy", -1)
    coef, momentum, first, last = prepare(d, lm, above, below)
    flow, first, last = place(sides, recv, first, last, from_left, from_right)
    new_height = raise_lake(recv, height)
    b_above, b_below = shift(last, "gx", 1), shift(first, "gx", -1)
    flow, new_height = lax.optimization_barrier((flow, new_height))
    b, w1, w2, sums = krylov(sides, flow, momentum, b_above, b_below, coef, from_left, from_right)
    sums = exchange(sums.reshape(DEV, 1, 128)).reshape(DEV, 128)
    return fields, new_height, finish(sums, b, w1, w2)


def solution(mesh):
    return jax.shard_map(
        per_device,
        mesh=mesh,
        in_specs=(
            P("gx", "gy"),
            P(None, "gx", "gy"),
            P(None, "gx", "gy"),
            P("gx", "gy"),
            P("gx", "gy"),
            P("gx", "gy", None, None),
            P("gx", "gy", None),
            P("gx", "gy"),
            P(None, "gx", "gy"),
            P("gx", "gy"),
        ),
        out_specs=(P(None, "gx", "gy"), P("gx", "gy"), P(None, "gx", "gy")),
        check_vma=False,
    )
```

```python
import functools

import jax
import jax.numpy as jnp
from jax import lax
from jax.experimental import pallas as pl
from jax.experimental.pallas import tpu as pltpu
from jax.sharding import PartitionSpec as P

F32 = jnp.float32
BF16 = jnp.bfloat16
AXES = ("gx", "gy")
NX, NY = 8, 16
DEV = NX * NY
R, C, L = 256, 512, 512
CAP = 4
UNITS = 12 * CAP + 1
TAG = 12 * CAP
WIDE = C + 128
TOP = 16
SROWS = R + 2 * TOP
CHUNK = 64
LTOP = 16
LROWS = L + 2 * LTOP
LCHUNK = 256
LSUB = 16
MIB = 1 << 20


HBM = pl.BlockSpec(memory_space=pltpu.HBM)
VMEM = pl.BlockSpec(memory_space=pltpu.VMEM)


def params(limit=None, room=0):
    return pltpu.CompilerParams(vmem_limit_bytes=limit * MIB if limit else 60 * 1024 * 1024 - room)


def present(sides):
    return tuple(sides[i : i + 1, :] for i in range(4))


def lanes(shape):
    return lax.broadcasted_iota(jnp.int32, shape, len(shape) - 1)


def rows(shape):
    return lax.broadcasted_iota(jnp.int32, shape, len(shape) - 2)


def edge_rows_kernel(h, m, b, f, a, d, up, dn, hs, ms, bs, fs, as_, ds, sems):
    copies = []
    for q, (src, dst) in enumerate(((h, hs), (f, fs), (a, as_), (d, ds))):
        for side, r in enumerate((0, src.shape[0] - 8)):
            copies.append(pltpu.make_async_copy(src.at[pl.ds(r, 8), :], dst.at[side], sems.at[2 * q + side]))
    for q, (src, dst) in enumerate(((m, ms), (b, bs))):
        for side, r in enumerate((0, R - 8)):
            copies.append(pltpu.make_async_copy(src.at[:, pl.ds(r, 8), :], dst.at[side], sems.at[8 + 2 * q + side]))
    for c in copies:
        c.start()
    for c in copies:
        c.wait()
    for side, out, two, one in ((0, up, slice(0, 2), slice(0, 1)), (1, dn, slice(6, 8), slice(7, 8))):
        out[0:2, :] = hs[side, two, :]
        out[2:4, :] = ms[side, 0, two, :]
        out[4:6, :] = ms[side, 1, two, :]
        out[6:7, :] = bs[side, 0, one, :]
        out[7:8, :] = bs[side, 1, one, :]
        out[8:9, :] = fs[side, one, :]
        out[9:10, :] = as_[side, one, :].astype(F32)
        out[10:12, :] = ds[side, two, :]
        out[12:16, :] = jnp.zeros((4, C), F32)


def edge_rows(h, mom, bed, fric, act, d):
    return pl.pallas_call(
        edge_rows_kernel,
        in_specs=[HBM] * 6,
        out_specs=[VMEM] * 2,
        out_shape=[jax.ShapeDtypeStruct((16, C), F32)] * 2,
        scratch_shapes=[
            pltpu.VMEM((2, 8, C), F32),
            pltpu.VMEM((2, 2, 8, C), F32),
            pltpu.VMEM((2, 2, 8, C), F32),
            pltpu.VMEM((2, 8, C), F32),
            pltpu.VMEM((2, 8, C), jnp.int32),
            pltpu.VMEM((2, 8, C), F32),
            pltpu.SemaphoreType.DMA((12,)),
        ],
        compiler_params=params(room=7_000_000),
        name="edge_rows",
    )(h, mom, bed, fric, act, d)


GROUP = R + 128
WIDTH = 4 * GROUP
LAKE_WIDTH = L + 128
LAKE_CHANNELS = ((0, 2), (2, 3), (5, 3))


def put(acc, lane, first, last, base, wide):
    turned = pltpu.roll(last, (base + wide) % 128, 1)
    acc = jnp.where((lane >= base) & (lane < base + wide), turned, acc)
    turned = pltpu.roll(first, 64 + base, 1)
    return jnp.where((lane >= 64 + base) & (lane < 64 + base + wide), turned, acc)


def edge_columns_kernel(h, m, b, f, a, both, hs, ms, bs, fs, as_, mat, sems):
    copies = []
    pairs = ((h, hs), (m, ms), (b, bs), (f, fs), (a, as_))
    for q, (src, dst) in enumerate(pairs):
        for side, lane in enumerate((0, C - 128)):
            at = (slice(None),) * (len(src.shape) - 1) + (pl.ds(lane, 128),)
            copies.append(pltpu.make_async_copy(src.at[at], dst.at[side], sems.at[2 * q + side]))
    for c in copies:
        c.start()
    slope = (
        lambda e, s: hs[e, s, :],
        lambda e, s: ms[e, 0, s, :],
        lambda e, s: ms[e, 1, s, :],
        lambda e, s: bs[e, 0, s, :],
        lambda e, s: bs[e, 1, s, :],
        lambda e, s: fs[e, s, :],
        lambda e, s: as_[e, s, :].astype(F32),
    )
    step = 64
    mat[R:, :] = jnp.zeros((128, 128), F32)
    for c in copies:
        c.wait()

    def body(t, _):
        s = pl.ds(pl.multiple_of(t * step, step), step)
        lane = lanes((step, 128))
        acc = jnp.zeros((step, 128), F32)
        for i, read in enumerate(slope):
            acc = put(acc, lane, read(0, s), read(1, s), 4 * i, 4)
        mat[s, :] = acc
        return 0

    lax.fori_loop(0, R // step, body, 0)
    for t in range(3):
        turned = mat[128 * t : 128 * t + 128, :].T
        for e, row in ((0, 0), (1, 64)):
            for g in range(4):
                at = GROUP * g + 128 * t
                both[e, :, at : at + 128] = turned[row + 8 * g : row + 8 * g + 8, :]


def edge_columns(h, mom, bed, fric, act):
    return pl.pallas_call(
        edge_columns_kernel,
        in_specs=[HBM] * 5,
        out_specs=VMEM,
        out_shape=jax.ShapeDtypeStruct((2, 8, WIDTH), F32),
        scratch_shapes=[
            pltpu.VMEM((2, R, 128), F32),
            pltpu.VMEM((2, 2, R, 128), F32),
            pltpu.VMEM((2, 2, R, 128), F32),
            pltpu.VMEM((2, R, 128), F32),
            pltpu.VMEM((2, R, 128), jnp.int32),
            pltpu.VMEM((GROUP, 128), F32),
            pltpu.SemaphoreType.DMA((10,)),
        ],
        compiler_params=params(room=7_300_000),
        cost_estimate=pl.CostEstimate(flops=8 * MIB, bytes_accessed=6 * MIB, transcendentals=0),
        name="edge_columns",
    )(h, mom, bed, fric, act)


def corner_block(x, first_row, second_row, a, b):
    row = rows((8, 128))

    def block(where):
        y = jnp.where(row == first_row, jnp.broadcast_to(x[a : a + 1, where], (8, 128)), 0.0)
        return y if b is None else jnp.where(row == second_row, jnp.broadcast_to(x[b : b + 1, where], (8, 128)), y)

    return block(slice(0, 128)), block(slice(C - 128, C))


def corners_kernel(sides, both, above, below, right, left):
    lane = lanes((8, 128))
    low, high = jnp.zeros((8, 128), F32), jnp.zeros((8, 128), F32)
    for i in range(7):
        if i < 3:
            a, b, base, wide = 2 * i, 2 * i + 1, 4 * i, 4
        else:
            a, b, base, wide = 3 + i, None, 4 * i, 4
        low = put(low, lane, *corner_block(below, 0, 1, a, b), base, wide)
        if b is None:
            high = put(high, lane, *corner_block(above, 7, None, a, None), base, wide)
        else:
            high = put(high, lane, *corner_block(above, 6, 7, a, b), base, wide)
    up, down, _, _ = present(sides)
    turned = jnp.concatenate([down * low, jnp.zeros((112, 128), F32), up * high], axis=0).T
    for e, out, at in ((0, right, 0), (1, left, 64)):
        out[...] = both[e]
        for g in range(4):
            s = slice(GROUP * g + R, GROUP * g + R + 128)
            out[:, s] = turned[at + 8 * g : at + 8 * g + 8, :]


def corners(sides, both, above, below):
    return pl.pallas_call(
        corners_kernel,
        in_specs=[VMEM] * 4,
        out_shape=[jax.ShapeDtypeStruct((8, WIDTH), F32)] * 2,
        compiler_params=params(4),
        name="corners",
    )(sides, both, above, below)


def lake_columns_kernel(sides, d, l, above, below, right, left, mat):
    reads = (lambda s, at: d[s, at], lambda s, at: l[0, s, at], lambda s, at: l[1, s, at])
    ends = (slice(0, 128), slice(C - 128, C))
    step = 128

    def body(t, _):
        s = pl.ds(pl.multiple_of(t * step, step), step)
        lane = lanes((step, 128))
        acc = jnp.zeros((step, 128), F32)
        for read, (base, wide) in zip(reads, LAKE_CHANNELS):
            acc = put(acc, lane, read(s, ends[0]), read(s, ends[1]), base, wide)
        mat[s, :] = acc
        return 0

    lax.fori_loop(0, L // step, body, 0)
    up, down, _, _ = present(sides)
    lane, zero = lanes((8, 128)), jnp.zeros((8, 128), F32)
    mat[L:, :] = jnp.zeros((128, 128), F32)
    mat[L : L + 8, :] = down * put(zero, lane, *corner_block(below, 0, 1, 10, 11), *LAKE_CHANNELS[0])
    mat[L + 120 :, :] = up * put(zero, lane, *corner_block(above, 6, 7, 10, 11), *LAKE_CHANNELS[0])
    for t in range(5):
        turned = mat[128 * t : 128 * t + 128, :].T
        right[:, 128 * t : 128 * t + 128] = turned[0:8, :]
        left[:, 128 * t : 128 * t + 128] = turned[64:72, :]


def lake_columns(sides, d, lm, above, below):
    return pl.pallas_call(
        lake_columns_kernel,
        out_shape=[jax.ShapeDtypeStruct((8, LAKE_WIDTH), F32)] * 2,
        scratch_shapes=[pltpu.VMEM((LAKE_WIDTH, 128), F32)],
        compiler_params=params(16),
        cost_estimate=pl.CostEstimate(flops=4 * MIB, bytes_accessed=4 * MIB, transcendentals=0),
        name="lake_columns",
    )(sides, d, lm, above, below)


def split2(x):
    hi = x.astype(BF16)
    return hi, (x - hi.astype(F32)).astype(BF16)


def pick(hot, parts):
    return jnp.dot(hot, parts[0], preferred_element_type=F32) + jnp.dot(hot, parts[1], preferred_element_type=F32)


def beside(xs):
    lane, n = lanes(xs[0].shape), len(xs)
    r = [pltpu.roll(x, 1, 1) for x in xs]
    left = [jnp.where(lane == 0, r[j - 1], r[j]) for j in range(n)]
    r = [pltpu.roll(x, 127, 1) for x in xs]
    right = [jnp.where(lane == 127, r[(j + 1) % n], r[j]) for j in range(n)]
    return left, right


def local_fluxes(h, m, n):
    q = 0.25 / 0.075
    inv = 1.0 / jnp.maximum(h, 0.25)
    p = (0.5 * h) * h
    mi = m * inv
    cross = mi * n
    fm = mi * m + p
    gn = (n * inv) * n + p
    h4, m4, n4 = q * h, q * m, q * n
    along = ((h4 - m, h4 + m), (m4 - fm, m4 + fm), (n4 - cross, n4 + cross))
    across = ((h4 - n, h4 + n), (m4 - cross, m4 + cross), (n4 - gn, n4 + gn))
    return along, across


def forcing(h, m, n, b0, b1, fr):
    return None, 2.0 * (h * b0 - fr * m), 2.0 * (h * b1 - fr * n)


def slope_kernel(sides, h_in, mom, bed, fric, act, above, below, out, ends, pa, qa, acc):
    tile = (
        lambda s, lane: h_in[s, lane],
        lambda s, lane: mom[0, s, lane],
        lambda s, lane: mom[1, s, lane],
        lambda s, lane: bed[0, s, lane],
        lambda s, lane: bed[1, s, lane],
        lambda s, lane: fric[s, lane],
        lambda s, lane: act[s, lane].astype(F32),
    )
    up, down, _, _ = present(sides)
    ends[...] = jnp.zeros(ends.shape, F32)
    for i in range(7):
        for j in range(4):
            s = slice(128 * j, 128 * j + 128)
            if i < 3:
                ends[0, i, j, 6:8, :] = up * above[2 * i : 2 * i + 2, s]
                ends[1, i, j, 0:2, :] = down * below[2 * i : 2 * i + 2, s]
            else:
                ends[0, i, j, 7:8, :] = up * above[3 + i : 4 + i, s]
                ends[1, i, j, 0:1, :] = down * below[3 + i : 4 + i, s]
    k = 0.075

    def fluxes(u, s, get, h, m, n):
        pairs = [[], [], []]
        for j in range(4):
            along, across = local_fluxes(h[j], m[j], n[j])
            force = forcing(h[j], m[j], n[j], get(3, j), get(4, j), get(5, j))
            for i in range(3):
                pa[u, i, j, s, :], qa[u, i, j, s, :] = along[i]
                pairs[i].append(across[i] + (force[i],))
        for i in range(3):
            _, right = beside([x[0] for x in pairs[i]])
            left, _ = beside([x[1] for x in pairs[i]])
            for j in range(4):
                x = left[j] + right[j]
                acc[u, i, j, s, :] = x if i == 0 else x + pairs[i][j][2]

    def combine(u, i, j, r, n, on):
        return (k * on) * (
            acc[u, i, j, pl.ds(r, n), :] + pa[u, i, j, pl.ds(r + 1, n), :] + qa[u, i, j, pl.ds(r - 1, n), :]
        )

    def reader(s):
        def get(i, j):
            return tile[i](s, slice(128 * j, 128 * j + 128))

        return get

    def end_reader(e):
        return lambda i, j: ends[e, i, j, :, :]

    def section(u, to, n, get):
        if u == 0:
            new = [[get(i, j) for j in range(4)] for i in range(3)]
        else:
            new = [[combine(0, i, j, to, n, get(6, j)) for j in range(4)] for i in range(3)]
        fluxes(u, pl.ds(to, n), get, *new)

    def body(u):
        def run(t, _):
            r = pl.multiple_of(t * CHUNK, CHUNK)
            section(u, pl.multiple_of(TOP + r, 8), CHUNK, reader(pl.ds(r, CHUNK)))
            return 0

        return run

    def last(t, _):
        r = pl.multiple_of(t * CHUNK, CHUNK)
        to = pl.ds(r, CHUNK)
        for j in range(4):
            s = slice(128 * j, 128 * j + 128)
            on = tile[6](to, s)
            for i in range(3):
                out[i, to, s] = combine(1, i, j, pl.multiple_of(TOP + r, 8), CHUNK, on)
        return 0

    pa[0, :, :, TOP + R + 8 :, :] = jnp.zeros((3, 4, 8, 128), F32)
    qa[0, :, :, 0:8, :] = jnp.zeros((3, 4, 8, 128), F32)
    for u in range(2):
        section(u, TOP - 8, 8, end_reader(0))
        section(u, TOP + R, 8, end_reader(1))
        lax.fori_loop(0, R // CHUNK, body(u), 0)
    lax.fori_loop(0, R // CHUNK, last, 0)


def slope(sides, h, mom, bed, fric, act, above, below):
    return pl.pallas_call(
        slope_kernel,
        in_specs=[VMEM] * 8,
        out_shape=jax.ShapeDtypeStruct((3, R, C), F32),
        scratch_shapes=[pltpu.VMEM((2, 7, 4, 8, 128), F32)] + [pltpu.VMEM((2, 3, 4, SROWS, 128), F32)] * 3,
        compiler_params=params(24),
        cost_estimate=pl.CostEstimate(flops=32 * MIB, bytes_accessed=6 * MIB, transcendentals=0),
        name="slope",
    )(sides, h, mom, bed, fric, act, above, below)


def pack_kernel(sides, fields, to_right, to_left, from_left, from_right, own, off, fields_out, sent, strip, out, payload, sems):
    shape = (8, GROUP)

    def section(x):
        h, m, n = x[:3]
        along, across = local_fluxes(h, m, n)
        force = forcing(h, m, n, *x[3:6])
        new = []
        for i in range(3):
            y = pltpu.roll(along[i][0], GROUP - 1, 1) + pltpu.roll(along[i][1], 1, 1)
            y = y + pltpu.roll(across[i][0], 7, 0) + pltpu.roll(across[i][1], 1, 0)
            y = y if i == 0 else y + force[i]
            new.append((0.075 * x[6]) * y)
        return new

    ends = []
    _, _, on_left, on_right = present(sides)
    for e, (before, after, a, b) in enumerate(((from_left, to_left, on_left, None), (to_right, from_right, None, on_right))):
        a, b = (1.0 if x is None else jnp.concatenate([x] * (GROUP // 128), axis=1) for x in (a, b))
        for i in range(7):
            r, s = 4 * (i % 2), slice(GROUP * (i // 2), GROUP * (i // 2) + GROUP)
            strip[e, i, 0:4, :] = a * before[r : r + 4, s]
            strip[e, i, 4:8, :] = b * after[r : r + 4, s]
        x = [strip[e, i, :, :] for i in range(7)]
        x = section(x) + x[3:]
        ends.append([pltpu.roll(y, 4, 0) for y in section(x)])
    row, lane = rows(shape), lanes((128, 128))
    copies = []
    for i in range(3):
        first = jnp.where(row < 2, ends[0][i], 0.0)
        last = jnp.where(row >= 6, ends[1][i], 0.0)
        for t in range(R // 128):
            s = slice(128 * t, 128 * t + 128)
            turned = jnp.concatenate([first[:, s], jnp.zeros((112, 128), F32), last[:, s]], axis=0).T
            out[i, s, 0:128] = jnp.where(lane < 2, turned, fields[i, s, 0:128])
            out[i, s, C - 128 : C] = jnp.where(lane >= 126, turned, fields[i, s, C - 128 : C])
        out[i, :, 128 : C - 128] = fields[i, :, 128 : C - 128]
        for t in range(2):
            s = pl.ds(R // 2 * t, R // 2)
            copies.append(pltpu.make_async_copy(out.at[i, s, :], fields_out.at[i, s, :], sems.at[2 * i + t]))
            copies[-1].start()

    owner = jnp.broadcast_to(own[...], (DEV, R))
    mine = rows((DEV, R)) == owner
    before = (rows((R, R)) < lanes((R, R))).astype(BF16)
    rank = jnp.dot(mine.astype(BF16), before, preferred_element_type=F32)
    picks = [mine & (rank == float(k_)) for k_ in range(CAP)]
    pickb = [p.astype(BF16) for p in picks]
    lane, dest = lanes((DEV, 128)), rows((DEV, 128))
    tags = jnp.zeros((DEV, 128), F32)
    tag_value = jnp.broadcast_to((off[...] + 1).astype(F32), (DEV, R))
    edge_lane = lanes((R, 128))
    m_first, n_first = out[1, :, 0:128], out[2, :, 0:128]
    m_last, n_last = out[1, :, C - 128 : C], out[2, :, C - 128 : C]
    edges = jnp.where(edge_lane < 3, m_first, 0.0)
    edges = jnp.where((edge_lane >= 3) & (edge_lane < 6), pltpu.roll(n_first, 3, 1), edges)
    edges = jnp.where((edge_lane >= 8) & (edge_lane < 11), pltpu.roll(m_last, 11, 1), edges)
    edges = jnp.where((edge_lane >= 11) & (edge_lane < 14), pltpu.roll(n_last, 14, 1), edges)
    parts = split2(edges)
    to_right = jnp.zeros((DEV, 128), F32)
    to_left = jnp.zeros((DEV, 128), F32)
    for k_ in range(CAP):
        tag = jnp.sum(jnp.where(picks[k_], tag_value, 0.0), axis=1, keepdims=True)
        tags = jnp.where(lane == k_, tag, tags)
        g = pick(pickb[k_], parts)
        at = 8 + 6 * k_
        to_right = jnp.where((lane >= at) & (lane < at + 6), pltpu.roll(g, at - 8, 1) if k_ else g, to_right)
        to_right = jnp.where(lane == 56 + k_, tag, to_right)
        at = 32 + 6 * k_
        to_left = jnp.where((lane >= at) & (lane < at + 6), pltpu.roll(g, at, 1), to_left)
        to_left = jnp.where(lane == 60 + k_, tag, to_left)
    column = lax.rem(dest, NY)
    to_right = jnp.where(column > 0, pltpu.roll(to_right, 1, 0), 0.0)
    to_left = jnp.where(column < NY - 1, pltpu.roll(to_left, DEV - 1, 0), 0.0)
    payload[pl.ds(TAG, DEV, stride=UNITS), :] = tags + to_right + to_left

    parts = [split2(out[i]) for i in range(3)]
    groups, piece = 4, 32
    part = DEV // groups
    for e in range(groups):
        some = jnp.concatenate([x[part * e : part * e + part, :] for x in pickb], axis=0)
        for i in range(3):
            y = pick(some, parts[i])
            for k_ in range(CAP):
                for j in range(4):
                    at = part * UNITS * e + 12 * k_ + 4 * i + j
                    payload[pl.ds(at, part, stride=UNITS), :] = y[part * k_ : part * k_ + part, 128 * j : 128 * j + 128]
        for t in range(part * e, part * e + part, piece):
            s = pl.ds(UNITS * t, UNITS * piece)
            copies.append(pltpu.make_async_copy(payload.at[s, :], sent.at[s, :], sems.at[6 + t // piece]))
            copies[-1].start()
    for copy in copies:
        copy.wait()


def pack(sides, fields, to_right, to_left, from_left, from_right, own, off):
    return pl.pallas_call(
        pack_kernel,
        in_specs=[VMEM] * 8,
        out_specs=[HBM, HBM],
        out_shape=[jax.ShapeDtypeStruct((3, R, C), F32), jax.ShapeDtypeStruct((DEV * UNITS, 128), F32)],
        scratch_shapes=[
            pltpu.VMEM((2, 7, 8, GROUP), F32),
            pltpu.VMEM((3, R, C), F32),
            pltpu.VMEM((DEV * UNITS, 128), F32),
            pltpu.SemaphoreType.DMA((22,)),
        ],
        compiler_params=params(room=10_000_000),
        name="pack",
    )(sides, fields, to_right, to_left, from_left, from_right, own, off)


def prepare_kernel(d, lm, above, below, coef, momentum, first, last):
    step = 64

    def body(t, _):
        r = pl.multiple_of(t * step, step)
        s = pl.ds(r, step)
        to = pl.ds(pl.multiple_of(LTOP + r, 8), step)
        for j in range(4):
            at = slice(128 * j, 128 * j + 128)
            coef[j, to, :] = 2.0 * d[s, at] - 2.0
            for i in range(2):
                momentum[i, j, s, :] = lm[i, s, at]
        return 0

    lax.fori_loop(0, L // step, body, 0)
    for j in range(4):
        coef[j, 0:LTOP, :] = jnp.zeros((LTOP, 128), F32)
        coef[j, LTOP + L :, :] = jnp.zeros((LTOP, 128), F32)
        s = slice(128 * j, 128 * j + 128)
        coef[j, LTOP - 2 : LTOP, :] = 2.0 * above[10:12, s] - 2.0
        coef[j, LTOP + L : LTOP + L + 2, :] = 2.0 * below[10:12, s] - 2.0
    first[...] = momentum[:, :, 0:8, :]
    last[...] = momentum[:, :, L - 8 : L, :]


def prepare(d, lm, above, below):
    return pl.pallas_call(
        prepare_kernel,
        out_shape=[jax.ShapeDtypeStruct(x, F32) for x in ((4, LROWS, 128), (2, 4, L, 128), (2, 4, 8, 128), (2, 4, 8, 128))],
        compiler_params=params(16),
        cost_estimate=pl.CostEstimate(flops=4 * MIB, bytes_accessed=8 * MIB, transcendentals=0),
        name="prepare",
    )(d, lm, above, below)


def lake_halo(sides, from_left, from_right, t, i):
    _, _, on_left, on_right = present(sides)
    at, wide = LAKE_CHANNELS[i]
    s, row = slice(128 * t, 128 * t + 128), rows((8, 128))
    right = from_right[:, s] if at == 0 else pltpu.roll(from_right[:, s], 8 - at, 0)
    left = from_left[:, s] if at + wide == 8 else pltpu.roll(from_left[:, s], 8 - wide - at, 0)
    right = jnp.where(row < wide, on_right * right, 0.0)
    left = jnp.where(row >= 8 - wide, on_left * left, 0.0)
    return jnp.concatenate([right, jnp.zeros((112, 128), F32), left], axis=0).T


def one_hot(hot, tags, first):
    here = (rows((L, DEV)) + 1).astype(F32)
    for group, at in enumerate(first):
        for k in range(CAP):
            col = (group * CAP + k) * DEV
            hot[:, col : col + DEV] = (here == tags[at + k : at + k + 1, :]).astype(BF16)


def gather(recv, term, c):
    for k in range(CAP):
        for j in range(4):
            parts = split2(recv[pl.ds(12 * k + 4 * c + j, DEV, stride=UNITS), :])
            for t in range(2):
                term[t, DEV * k : DEV * k + DEV, 128 * j : 128 * j + 128] = parts[t]


def place_kernel(sides, recv, first_momentum, last_momentum, from_left, from_right, flow, first, last, hot, term):
    marks = recv[pl.ds(TAG, DEV, stride=UNITS), :]
    one_hot(hot, marks.T, (0, 56, 60))
    own = hot[:, 0 : CAP * DEV]
    side = hot[:, CAP * DEV : 3 * CAP * DEV]
    lane = lanes((DEV, 128))
    for c in range(2):
        gather(recv, term, c + 1)
        sums = pick(own, (term[0], term[1]))
        for j in range(4):
            flow[c, j, :, :] = sums[:, 128 * j : 128 * j + 128]
        left, right = [], []
        for k in range(CAP):
            left.append(jnp.where(lane >= 125, pltpu.roll(marks, 117 - 6 * k - 3 * c, 1), 0.0))
            right.append(jnp.where(lane < 3, pltpu.roll(marks, 96 - 6 * k - 3 * c, 1), 0.0))
        flow[c, 4, :, :] = pick(side, split2(jnp.concatenate(left + right, axis=0)))
    first[:, 0:4, :, :] = first_momentum[...] + flow[:, 0:4, 0:8, :]
    last[:, 0:4, :, :] = last_momentum[...] + flow[:, 0:4, L - 8 : L, :]
    for c in range(2):
        top = lake_halo(sides, from_left, from_right, 0, c + 1)
        first[c, 4, :, :] = top[0:8, :] + flow[c, 4, 0:8, :]
        bottom = lake_halo(sides, from_left, from_right, L // 128 - 1, c + 1)
        last[c, 4, :, :] = bottom[120:128, :] + flow[c, 4, L - 8 : L, :]


def place(sides, recv, first_momentum, last_momentum, from_left, from_right):
    return pl.pallas_call(
        place_kernel,
        out_shape=[jax.ShapeDtypeStruct((2, 5, n, 128), F32) for n in (L, 8, 8)],
        scratch_shapes=[pltpu.VMEM((L, 3 * CAP * DEV), BF16), pltpu.VMEM((2, CAP * DEV, C), BF16)],
        compiler_params=params(20),
        name="place",
    )(sides, recv, first_momentum, last_momentum, from_left, from_right)


def raise_kernel(recv, height, new_height, hot, term):
    one_hot(hot, recv[pl.ds(TAG, DEV, stride=UNITS), :].T, (0,))
    gather(recv, term, 0)
    new_height[...] = height[...] + pick(hot[...], (term[0], term[1]))


def raise_lake(recv, height):
    return pl.pallas_call(
        raise_kernel,
        in_specs=[VMEM] * 2,
        out_specs=VMEM,
        out_shape=jax.ShapeDtypeStruct((L, C), F32),
        scratch_shapes=[pltpu.VMEM((L, CAP * DEV), BF16), pltpu.VMEM((2, CAP * DEV, C), BF16)],
        compiler_params=params(8),
        cost_estimate=pl.CostEstimate(flops=600 * MIB, bytes_accessed=6 * MIB, transcendentals=0),
        name="raise_lake",
    )(recv, height)


def krylov_kernel(sides, flow, momentum, above, below, coef, from_left, from_right, b, w1, w2, sums, side_coef):
    for x in (b, w1, w2):
        x[:, :, 0 : LTOP - 8, :] = jnp.zeros((2, 5, LTOP - 8, 128), F32)
        x[:, :, LTOP + L + 8 :, :] = jnp.zeros((2, 5, LTOP - 8, 128), F32)
    up, down, left, right = present(sides)
    b[:, :, LTOP - 8 : LTOP, :] = up * above[...]
    b[:, :, LTOP + L : LTOP + L + 8, :] = down * below[...]
    edge = jnp.where(lanes((1, 128)) < 64, right, left)

    def total_side(t, _):
        r = pl.multiple_of(t * 64, 64)
        s, to = pl.ds(r, 64), pl.ds(pl.multiple_of(LTOP + r, 8), 64)
        for i in range(2):
            for j in range(4):
                b[i, j, to, :] = flow[i, j, s, :] + momentum[i, j, s, :]
        return 0

    for t in range(4):
        s, to = slice(128 * t, 128 * t + 128), slice(LTOP + 128 * t, LTOP + 128 * t + 128)
        side_coef[to, :] = 2.0 * lake_halo(sides, from_left, from_right, t, 0) - 2.0
        for i in range(2):
            b[i, 4, to, :] = flow[i, 4, s, :] + lake_halo(sides, from_left, from_right, t, i + 1)
    ends = 2.0 * lake_halo(sides, from_left, from_right, 4, 0) - 2.0
    side_coef[LTOP - 8 : LTOP, :] = ends[120:128, :]
    side_coef[LTOP + L : LTOP + L + 8, :] = ends[0:8, :]
    lax.fori_loop(0, L // 64, total_side, 0)

    def image(x, i, r, n):
        v = [x[i, j, pl.ds(r, n), :] for j in range(5)]
        west, east = beside(v)
        w = []
        for j in range(5):
            around = (x[i, j, pl.ds(r - 1, n), :] + x[i, j, pl.ds(r + 1, n), :]) + (west[j] + east[j])
            diagonal = coef[j, pl.ds(r, n), :] if j < 4 else side_coef[pl.ds(r, n), :]
            w.append(diagonal * v[j] - around)
        w[4] = w[4] * edge
        return v, w

    def dot(x, y):
        p = (x[0] * y[0] + x[1] * y[1]) + (x[2] * y[2] + x[3] * y[3])
        p = [p[8 * q : 8 * q + 8, :] for q in range(p.shape[0] // 8)]
        while len(p) > 1:
            p = [a + c for a, c in zip(p[::2], p[1::2])]
        return p[0]

    zero = jnp.zeros((8, 128), F32)

    def sweep(src, dst, kinds):
        for i in range(2):
            for r, scale in ((LTOP - 8, up), (LTOP + L, down)):
                _, w = image(src, i, r, 8)
                for j in range(5):
                    dst[i, j, r : r + 8, :] = w[j] * scale

        def body(t, carry):
            r = pl.multiple_of(LTOP + t * LCHUNK, 8)
            carry = list(carry)
            for q0 in range(0, LCHUNK, LSUB):
                rq = pl.multiple_of(r + q0, 8)
                for i in range(2):
                    v, w = image(src, i, rq, LSUB)
                    for j in range(5):
                        dst[i, j, pl.ds(rq, LSUB), :] = w[j]
                    for q, kind in enumerate(kinds):
                        x, y = {"vv": (v, v), "vw": (v, w), "ww": (w, w)}[kind]
                        at = i * len(kinds) + q
                        carry[at] = carry[at] + dot(x, y)
            return tuple(carry)

        total = lax.fori_loop(0, L // LCHUNK, body, (zero,) * (2 * len(kinds)))
        return total[: len(kinds)], total[len(kinds) :]

    def last_sum(x):
        lane = lanes((LSUB, 128))

        def body(t, carry):
            r = pl.multiple_of(LTOP + t * LCHUNK, 8)
            carry = list(carry)
            for q0 in range(0, LCHUNK, LSUB):
                rq = pl.multiple_of(r + q0, 8)
                for i in range(2):
                    v = [x[i, j, pl.ds(rq, LSUB), :] for j in range(5)]
                    turned = [pltpu.roll(y, 127, 1) for y in v]
                    w = []
                    for j in range(4):
                        pair = jnp.where(lane == 127, turned[j + 1], turned[j]) + x[i, j, pl.ds(rq + 1, LSUB), :]
                        w.append(coef[j, pl.ds(rq, LSUB), :] * v[j] - 2.0 * pair)
                    carry[i] = carry[i] + dot(v, w)
            return tuple(carry)

        total = lax.fori_loop(0, L // LCHUNK, body, (zero,) * 2)
        return total[:1], total[1:]

    s1 = sweep(b, w1, ("vv", "vw", "ww"))
    s2 = sweep(w1, w2, ("vw", "ww"))
    s3 = last_sum(w2)
    flat = []
    for i in range(2):
        flat += list(s1[i]) + list(s2[i]) + list(s3[i]) + [zero, zero]
    stack = jnp.concatenate([jnp.sum(x, axis=0, keepdims=True) for x in flat], axis=0)
    total = jnp.sum(stack, axis=1, keepdims=True)
    line = jnp.sum(jnp.where(lanes((16, 128)) == rows((16, 128)), total, 0.0), axis=0, keepdims=True)
    sums[...] = jnp.broadcast_to(line, (DEV, 128))


def krylov(sides, flow, momentum, above, below, coef, from_left, from_right):
    return pl.pallas_call(
        krylov_kernel,
        in_specs=[VMEM] * 8,
        out_specs=[VMEM] * 4,
        out_shape=[jax.ShapeDtypeStruct((2, 5, LROWS, 128), F32)] * 3 + [jax.ShapeDtypeStruct((DEV, 128), F32)],
        scratch_shapes=[pltpu.VMEM((LROWS, 128), F32)],
        compiler_params=params(24),
        name="krylov",
    )(sides, flow, momentum, above, below, coef, from_left, from_right)


def steps(nu):
    def inner(u, v):
        return sum(u[i] * v[j] * nu[i + j] for i in range(len(u)) for j in range(len(v)))

    def times(u):
        lo = [4.0 * x for x in u] + [None]
        hi = [None] + [0.5 * x for x in u]
        return [a if b is None else b if a is None else a + b for a, b in zip(lo, hi)]

    def add(u, v, scale):
        u = list(u) + [None] * (len(v) - len(u))
        return [x + scale * y if x is not None and y is not None else scale * y if x is None else x
                for x, y in zip(u, list(v) + [None] * (len(u) - len(v)))]

    r = p = [jnp.ones_like(nu[0])]
    rr = nu[0]
    x = None
    for it in range(3):
        image = times(p)
        curve = inner(p, image)
        alpha = jnp.where(curve > 0.0, rr / curve, 0.25)
        alpha = jnp.minimum(jnp.maximum(alpha, 1.0 / 7.0), 1.0 / 1.2)
        x = [alpha * q for q in p] if x is None else add(x, p, alpha)
        if it == 2:
            return x
        r = add(r, image, -alpha)
        new = jnp.maximum(inner(r, r), 0.0)
        beta = jnp.minimum(jnp.where(rr > 0.0, new / rr, 0.0), 6.0)
        p = add(r, p, beta)
        rr = new


def finish_kernel(sums, b, w1, w2, x_hbm, coef, x, sems):
    total = jnp.sum(sums[...], axis=0, keepdims=True)
    lane = lanes((1, 128))
    for c in range(2):
        nu = [
            jnp.sum(jnp.where(lane == 8 * c + k, total, 0.0), axis=1, keepdims=True) for k in range(6)
        ]
        e = steps(nu)
        for k in range(3):
            coef[3 * c + k : 3 * c + k + 1, :] = jnp.broadcast_to(e[k], (1, 128))
    step = 64
    copies = []
    for c in range(2):
        e = [jnp.broadcast_to(coef[3 * c + k : 3 * c + k + 1, :], (step, 128)) for k in range(3)]

        def body(t, _):
            s = pl.ds(pl.multiple_of(t * step, step), step)
            at = pl.ds(pl.multiple_of(LTOP + t * step, 8), step)
            for j in range(4):
                x[c, s, 128 * j : 128 * j + 128] = e[0] * b[c, j, at, :] + e[1] * w1[c, j, at, :] + e[2] * w2[c, j, at, :]
            return 0

        for half in range(2):
            lax.fori_loop(half * L // step // 2, (half + 1) * L // step // 2, body, 0)
            s = pl.ds(half * L // 2, L // 2)
            copies.append(pltpu.make_async_copy(x.at[c, s, :], x_hbm.at[c, s, :], sems.at[2 * c + half]))
            copies[-1].start()
    for copy in copies:
        copy.wait()


def finish(sums, b, w1, w2):
    return pl.pallas_call(
        finish_kernel,
        in_specs=[VMEM] * 4,
        out_specs=HBM,
        out_shape=jax.ShapeDtypeStruct((2, L, C), F32),
        scratch_shapes=[pltpu.VMEM((8, 128), F32), pltpu.VMEM((2, L, C), F32), pltpu.SemaphoreType.DMA((4,))],
        compiler_params=params(16),
        name="finish",
    )(sums, b, w1, w2)


def shift(x, axis, by):
    n = {"gx": NX, "gy": NY}[axis]
    return lax.ppermute(x, axis, [(i, (i + by) % n) for i in range(n)])


def exchange(x):
    return lax.all_to_all(x, AXES, split_axis=0, concat_axis=0, tiled=True)


def per_device(h, mom, bed, fric, act, owners, offsets, height, lm, d):
    i, j = lax.axis_index("gx"), lax.axis_index("gy")
    row = rows((8, 128))
    inside = ((row == 0) & (i > 0)) | ((row == 1) & (i < NX - 1)) | ((row == 2) & (j > 0)) | ((row == 3) & (j < NY - 1))
    sides = inside.astype(F32)
    up, dn = edge_rows(h, mom, bed, fric, act, d)
    above, below = shift(dn, "gx", 1), shift(up, "gx", -1)
    columns = edge_columns(h, mom, bed, fric, act)
    to_right, to_left = corners(sides, columns, above, below)
    from_left, from_right = shift(to_right, "gy", 1), shift(to_left, "gy", -1)
    fields = slope(sides, h, mom, bed, fric, act, above, below)
    own, off = owners.reshape(1, R), offsets.reshape(1, R)
    fields, payload = pack(sides, fields, to_right, to_left, from_left, from_right, own, off)
    payload, d, lm = lax.optimization_barrier((payload, d, lm))
    recv = exchange(payload.reshape(DEV, UNITS, 1, 128)).reshape(DEV * UNITS, 128)
    to_right, to_left = lake_columns(sides, d, lm, above, below)
    from_left, from_right = shift(to_right, "gy", 1), shift(to_left, "gy", -1)
    coef, momentum, first, last = prepare(d, lm, above, below)
    flow, first, last = place(sides, recv, first, last, from_left, from_right)
    new_height = raise_lake(recv, height)
    b_above, b_below = shift(last, "gx", 1), shift(first, "gx", -1)
    flow, new_height = lax.optimization_barrier((flow, new_height))
    b, w1, w2, sums = krylov(sides, flow, momentum, b_above, b_below, coef, from_left, from_right)
    sums = exchange(sums.reshape(DEV, 1, 128)).reshape(DEV, 128)
    return fields, new_height, finish(sums, b, w1, w2)


def solution(mesh):
    return jax.shard_map(
        per_device,
        mesh=mesh,
        in_specs=(
            P("gx", "gy"),
            P(None, "gx", "gy"),
            P(None, "gx", "gy"),
            P("gx", "gy"),
            P("gx", "gy"),
            P("gx", "gy", None, None),
            P("gx", "gy", None),
            P("gx", "gy"),
            P(None, "gx", "gy"),
            P("gx", "gy"),
        ),
        out_specs=(P(None, "gx", "gy"), P("gx", "gy"), P(None, "gx", "gy")),
        check_vma=False,
    )
```
